256 devices in a mesh: ang: 8 (over x, z_hi), rad: 32 (over z_lo, y, core).
Axes of the slice: x: 4, y: 4, z: 8 (z_hi: 2, z_lo: 4; z = z_hi * 4 + z_lo), core: 2. Of those that a mesh axis runs over, the one named last changes fastest.
Arguments:
- psi_bound: bfloat16 [64, 64, 1024], P('rad', None, 'ang'), may hold values from -6 to 6
- psi_cont: bfloat16 [64, 512, 1024], P('rad', None, 'ang'), may hold values from -6 to 6
- ylm: bfloat16 [1024, 1024], P('ang'), may hold values from -0.1875 to 0.1875
- radial_weight: float32 [64], P('rad'), may hold values from 0.0003 to 0.003
- order: int32 [1024], replicated, may hold values from 0 to 1023, each once
Outputs:
- dipole: float32 [64, 512], P('ang', 'rad')
The draws below stay inside these ranges and needn't reach their ends.
Inputs may be any that keep to these rules, and one draw needn't show every extreme that they name: order holds each of the 1024 harmonic indices exactly once.
All inputs are finite; a program needn't handle non-finite values.
Results may differ from the reference program's by a relative error of at most 0.029.
Values may be sent and summed in bfloat16 or wider, within the bound.
A program may use at most 64 MiB of HBM per device.

```python
import math
import jax
import jax.numpy as jnp
from jax import lax

LMAX = 31
NP = 1024
NB = 64
NC = 512
NH = 1024
NR = 64
N_ANG = 8


def with_spikes(entries, own_key, source, target, parts, factor):
    def block_of(position):
        return (jnp.arange(entries.shape[position]) // (entries.shape[position] // parts)).reshape((-1,) + (1,) * (entries.ndim - 1 - position))

    near = jax.random.permutation(own_key, parts)[block_of(target)]
    far = (block_of(target) + parts // 2) % parts
    return jnp.where((block_of(source) == near) | (block_of(source) == far), factor * entries, entries)


def level_of(rng, shape, split, smallest, top_value):
    def one(position, parts):
        draws = jax.random.uniform(jax.random.fold_in(jax.random.fold_in(rng, 6), position), (parts,), jnp.float32, smallest / len(split), top_value / len(split))
        return jnp.repeat(jnp.exp(draws), shape[position] // parts).reshape((-1,) + (1,) * (len(shape) - position - 1))

    loudness = one(*split[0])
    for cut in split[1:]:
        loudness = loudness * one(*cut)
    return loudness


def centred(own_key, extent, scale, limit, shards=(), kind=jnp.bfloat16):
    loudness = level_of(own_key, extent, shards, -0.22, 0.18) if shards else 1.0
    array = jax.random.normal(own_key, extent, jnp.float32) * scale * loudness
    return jnp.minimum(jnp.maximum(array, -limit), limit).astype(kind)


def gaussian_with(key, dims, deviation, limit, shards, heavy, kind=jnp.bfloat16):
    values = deviation * jax.random.normal(key, dims, jnp.float32)
    if shards:
        values = values * level_of(key, dims, shards, -0.22, 0.18)
    return jnp.clip(with_spikes(values, jax.random.fold_in(key, 3), *heavy), -limit, limit).astype(kind)


def setup_inputs(seed: int = 0) -> dict:
    key_list = jax.random.split(jax.random.key(seed), 6)
    return {
        "psi_bound": centred(key_list[0], (NR, NB, NP), 1.0, 6.0, ((0, 32), (2, 8))),
        "psi_cont": gaussian_with(key_list[1], (NR, NC, NP), 1.0, 6.0, ((0, 32), (2, 8)), (0, 1, 32, 2.75)),
        "ylm": centred(key_list[2], (NP, NH), NP ** -0.5, 0.1875, ((0, 8),)),
        "radial_weight": jnp.clip(jnp.exp(math.log(0.003) - 2.3025851 * jax.random.uniform(key_list[3], (NR,), jnp.float32) ** level_of(key_list[3], (NR,), ((0, 32),), -0.2, 0.2)), 0.0003, 0.003),
        "order": jax.random.permutation(key_list[4], NH).astype(jnp.int32),
    }


def harmonic_tables(order, total):
    columns = jnp.arange(total, dtype=jnp.int32)
    squares_list = jnp.arange(1, LMAX + 1, dtype=jnp.int32) ** 2
    degree = lax.optimization_barrier(jnp.sum((order[:, None] >= squares_list[None, :]).astype(jnp.int32), axis=1))
    order_m = order - degree * degree - degree
    inverse = jnp.zeros((total,), jnp.int32).at[order].set(columns)
    degf = degree.astype(jnp.float32)
    mvalue = order_m.astype(jnp.float32)
    upper_l = degree + 1
    upper_ok = upper_l <= LMAX
    upper_idx = jnp.clip(upper_l * upper_l + upper_l + order_m, 0, total - 1).astype(jnp.int32)
    upper_col = inverse[upper_idx]
    upper_num = (degf + 1.0) ** 2 - mvalue ** 2
    upper_den = (2.0 * degf + 1.0) * (2.0 * degf + 3.0)
    upper_coef = jnp.where(upper_ok, jnp.sqrt(jnp.maximum(upper_num, 0.0) / upper_den), 0.0)
    lower_l = degree - 1
    lower_ok = lower_l >= jnp.abs(order_m)
    lower_idx = jnp.clip(lower_l * lower_l + lower_l + order_m, 0, total - 1).astype(jnp.int32)
    lower_col = inverse[lower_idx]
    lower_num = degf ** 2 - mvalue ** 2
    lower_den = jnp.maximum((2.0 * degf - 1.0) * (2.0 * degf + 1.0), 1.0)
    lower_coef = jnp.where(lower_ok, jnp.sqrt(jnp.maximum(lower_num, 0.0) / lower_den), 0.0)
    return (upper_col, upper_coef, lower_col, lower_coef)

def couple(values, tables):
    upper_col, upper_coef, lower_col, lower_coef = tables
    return values[..., upper_col] * upper_coef + values[..., lower_col] * lower_coef

def project(rows, ylm, blocks):
    width = ylm.shape[0] // blocks
    total = jnp.zeros((rows.shape[0], ylm.shape[1]), jnp.float32)
    for block in range(blocks):
        part = jnp.dot(rows[:, block * width:(block + 1) * width], ylm[block * width:(block + 1) * width], preferred_element_type=jnp.float32)
        total = total + part.astype(jnp.bfloat16).astype(jnp.float32)
    return total

def reference(psi_bound, psi_cont, ylm, radial_weight, order):
    tables = harmonic_tables(order, NH)
    shell_block = 16
    count = NR // shell_block
    bound_rows = psi_bound.reshape(count, shell_block, NB, NP)
    cont_rows = psi_cont.reshape(count, shell_block, NC, NP)
    weights = radial_weight.reshape(count, shell_block)

    def one_block(inputs):
        bound_in, cont_in, weight_in = inputs
        bound_coef = project(bound_in.reshape(shell_block * NB, NP), ylm, N_ANG).reshape(shell_block, NB, NH)
        coupled = couple(bound_coef, tables).astype(jnp.bfloat16).astype(jnp.float32)
        cont_coef = project(cont_in.reshape(shell_block * NC, NP), ylm, N_ANG).reshape(shell_block, NC, NH)
        per_shell = jnp.einsum('rbk,rck->rbc', coupled, cont_coef, precision=lax.Precision.HIGHEST)
        return jnp.einsum('r,rbc->bc', weight_in, per_shell, precision=lax.Precision.HIGHEST)
    blocks_out = lax.map(one_block, (bound_rows, cont_rows, weights))
    return lax.optimization_barrier(jnp.sum(blocks_out, axis=0))
```

```python
import functools

import jax
import jax.numpy as jnp
from jax import lax
from jax.experimental import pallas as pl
from jax.experimental.pallas import tpu as pltpu
from jax.sharding import PartitionSpec as P

LMAX = 31
MESH = pl.DeviceIdType.MESH
F32, BF16 = jnp.float32, jnp.bfloat16
NX, NY, NZ, NC, HALF = 4, 4, 8, 2, 4
ANG, RAD = 8, 32
PTS, TOTAL = 128, 1024
PIECE = PTS * ANG // RAD


def ring(d, n):
    return min(d, n - d)


OFFSETS = sorted(
    (
        (dx, dy, dz, dc)
        for dz in range(NZ)
        for dx in range(NX)
        for dy in range(NY)
        for dc in range(NC)
        if (dx, dy, dz, dc) != (0, 0, 0, 0)
    ),
    key=lambda o: -(ring(o[0], NX) + ring(o[1], NY) + ring(o[2], NZ)),
)
PEERS = [(dz, dy) for dz in range(HALF) for dy in range(NY) if (dz, dy) != (0, 0)]


def device(x, y, z, core):
    return (x * 2 + z // HALF, (z % HALF) * (NY * NC) + y * NC + core)


def piece_of(x, half, zl, y, core):
    edge = (zl == 0) | (zl == HALF - 1)
    other = jnp.where(edge, 1 - half, half)
    pair = jnp.where(edge, zl // (HALF - 1), zl - 1)
    return ((x + y) % NX) * 2 + other, pair * 2 + core


def coupling_rows(order):
    degree = jnp.zeros(order.shape, jnp.int32)
    for edge in range(1, LMAX + 1):
        degree = degree + (order >= edge * edge).astype(jnp.int32)
    m = order - degree * degree - degree
    lf, mf = degree.astype(F32), m.astype(F32)
    upper = jnp.where(degree + 1 <= LMAX, order + 2 * degree + 2, -1)
    upper_num = (lf + 1.0) * (lf + 1.0) - mf * mf
    upper_coef = jnp.sqrt(jnp.maximum(upper_num, 0.0) / ((2.0 * lf + 1.0) * (2.0 * lf + 3.0)))
    lower = jnp.where(degree - 1 >= jnp.abs(m), order - 2 * degree, -1)
    lower_num = lf * lf - mf * mf
    lower_den = jnp.maximum((2.0 * lf - 1.0) * (2.0 * lf + 1.0), 1.0)
    lower_coef = jnp.sqrt(jnp.maximum(lower_num, 0.0) / lower_den)
    return upper.astype(F32), upper_coef, lower.astype(F32), lower_coef


def turned(block):
    rows, lanes = block.shape
    row = lax.broadcasted_iota(jnp.int32, block.shape, 0)
    group = lax.broadcasted_iota(jnp.int32, block.shape, 1) // 16
    for s in (1, 2, 4):
        below = pltpu.roll(pltpu.roll(block, rows - s, 0), 16 * s, 1)
        above = pltpu.roll(pltpu.roll(block, s, 0), lanes - 16 * s, 1)
        low_row, low_group = (row & s) == 0, (group & s) == 0
        block = jnp.where(
            low_row == low_group, block, jnp.where(low_row, below, above)
        )
    return block


def kernel(
    bound_hbm, cont_hbm, ylm_hbm, weight_ref, order_ref, out_ref,
    bound, cont, ylm, ys, ncol, z_ref, mine, m_full, cont_t, sendbuf, recvbuf,
    local_sem, out_sem, a_recv, f_recv, m_recv, relay_recv, end_send, end_recv, ready,
):
    ang, rad = lax.axis_index("ang"), lax.axis_index("rad")
    x, half = ang // 2, ang % 2
    zl, y, core = rad // (NY * NC), (rad // NC) % NY, rad % NC
    z = half * HALF + zl
    me = ang * RAD + rad

    x_peers = [device((x + d) % NX, y, z, core) for d in (2, 1, 3)]
    opposite = device(x, y, (z + HALF) % NZ, core)
    twin = device(x, y, z, 1 - core)
    peers = [device(x, (y + dy) % NY, half * HALF + (zl + dz) % HALF, core) for dz, dy in PEERS]
    edge = (zl == 0) | (zl == HALF - 1)
    z_other = jnp.where(edge, NZ - 1 - z, z)
    rows_to = device((x - y + NX) % NX, y, z_other, 1 - core)
    rows_from = device((x + y) % NX, y, z_other, 1 - core)

    barrier = pltpu.get_barrier_semaphore()
    for other in (*peers, opposite, *x_peers, twin, rows_from):
        pl.semaphore_signal(barrier, inc=1, device_id=other, device_id_type=MESH)

    def send(src, dst, send_sem, recv_sem, where):
        return pltpu.make_async_remote_copy(
            src_ref=src, dst_ref=dst, send_sem=send_sem, recv_sem=recv_sem,
            device_id=where, device_id_type=MESH,
        )

    loads = [
        pltpu.make_async_copy(ylm_hbm, ylm, local_sem.at[0]),
        pltpu.make_async_copy(cont_hbm, cont, local_sem.at[1]),
        pltpu.make_async_copy(bound_hbm, bound.at[ang], local_sem.at[2]),
    ]
    for load in loads:
        load.start()
    pl.semaphore_wait(barrier, len(peers) + 6)

    to_zl = z_other % HALF
    _, quarter_to = piece_of((x - y + NX) % NX, z_other // HALF, to_zl, y, 1 - core)
    rows = send(
        ylm_hbm.at[pl.ds(pl.multiple_of(quarter_to * PIECE, PIECE), PIECE)],
        ys, out_sem.at[0], f_recv, rows_to,
    )
    rows.start()
    across = send(bound_hbm, bound.at[ang], out_sem.at[1], a_recv.at[0], opposite)
    across.start()
    along = [
        send(bound_hbm, bound.at[ang], out_sem.at[2 + i], a_recv.at[1 + i], where)
        for i, where in enumerate(x_peers)
    ]
    for copy in along:
        copy.start()
    pl.semaphore_signal(ready.at[0], inc=1, device_id=opposite, device_id_type=MESH)

    order = order_ref[...]
    upper, upper_coef, lower, lower_coef = coupling_rows(order)
    orderf = order.astype(F32)
    for s in range(TOTAL // 128):
        ncol[pl.ds(s * 128, 128)] = jnp.broadcast_to(orderf[s : s + 1], (128, 128)).T
    loads[0].wait()

    def couple(s, carry):
        here = pl.ds(pl.multiple_of(s * 128, 128), 128)
        column = ncol[here]
        blocks = []
        for t in range(TOTAL // 128):
            cut = slice(t, t + 1)
            blocks.append(
                jnp.where(
                    column == upper[cut],
                    upper_coef[cut],
                    jnp.where(column == lower[cut], lower_coef[cut], 0.0),
                ).astype(BF16)
            )
        g = jnp.concatenate(blocks, axis=1)
        z_ref[here] = lax.dot_general(
            g, ylm[...], (((1,), (1,)), ((), ())), preferred_element_type=F32
        ).astype(BF16)
        return carry

    lax.fori_loop(0, TOTAL // 128, couple, 0)
    loads[1].wait()
    shells = weight_ref.shape[0]
    count = cont.shape[0] // shells
    for r in range(shells):
        for c in range(count // 128):
            block = cont[pl.ds(r * count + c * 128, 128)].astype(F32).T
            cont_t[pl.ds(r * 128, 128), pl.ds(c * 128, 128)] = block.astype(BF16)

    rows.wait_recv()
    mine[...] = jnp.dot(ys[...], z_ref[...], preferred_element_type=F32).astype(BF16)
    cls, quarter = piece_of(x, half, zl, y, core)
    block = cls * 4 + quarter
    own = [
        send(mine, m_full.at[block], out_sem.at[8 + i], m_recv.at[i], where)
        for i, where in enumerate(peers)
    ]
    for copy in own:
        copy.start()
    n_peers = len(peers)
    relays = [send(mine, m_full.at[block], out_sem.at[8 + n_peers], relay_recv.at[0], twin)]
    relays[0].start()
    m_full[block] = mine[...]

    pl.semaphore_wait(ready.at[0], 1)
    for where in x_peers:
        pl.semaphore_signal(ready.at[1], inc=1, device_id=where, device_id_type=MESH)

    across_in = send(bound_hbm, bound.at[ang], out_sem.at[1], a_recv.at[0], opposite)
    across_in.wait_recv()
    opposite_cls = opposite[0]
    onward = [
        send(bound.at[opposite_cls], bound.at[opposite_cls], out_sem.at[5 + i], a_recv.at[4 + i], where)
        for i, where in enumerate(x_peers)
    ]
    for copy in onward:
        copy.start()
    pl.semaphore_wait(ready.at[1], NX - 1)
    pl.semaphore_signal(ready.at[2], inc=1, device_id=twin, device_id_type=MESH)

    for i, (dz, dy) in enumerate(PEERS):
        own[i].wait_recv()
        there_cls, there_quarter = piece_of(
            x, half, (zl - dz + HALF) % HALF, (y - dy + NY) % NY, core
        )
        there = there_cls * 4 + there_quarter
        relay = send(
            m_full.at[there], m_full.at[there],
            out_sem.at[9 + n_peers + i], relay_recv.at[1 + i], twin,
        )
        relay.start()
        relays.append(relay)
    loads[2].wait()
    for copy in along:
        copy.wait_recv()
    for copy in onward:
        copy.wait_recv()
    bound_all = jnp.concatenate([bound[i] for i in range(ANG)], axis=1)
    pl.semaphore_wait(ready.at[2], 1)
    for relay in relays:
        relay.wait_recv()

    operator = m_full[...].reshape(PTS * ANG, PTS)
    d = jnp.dot(bound_all, operator, preferred_element_type=F32)
    nb = d.shape[0] // shells
    weighted = [d[r * nb : (r + 1) * nb] * weight_ref[r] for r in range(shells)]
    wide = jnp.concatenate(weighted, axis=1).astype(BF16)
    terms = jnp.dot(wide, cont_t[...], preferred_element_type=F32)
    for q in range(count // 128):
        cut = turned(terms[:, q * 128 : (q + 1) * 128])
        for a in range(ANG):
            sendbuf[pl.ds(a * RAD + q * 8, 8)] = cut[a * 8 : a * 8 + 8]

    for dx, dy, dz, dc in OFFSETS:
        where = device((x + dx) % NX, (y + dy) % NY, (z + dz) % NZ, (core + dc) % NC)
        send(
            sendbuf.at[pl.ds(where[0] * RAD + where[1], 1)],
            recvbuf.at[pl.ds(me, 1)],
            end_send, end_recv, where,
        ).start()
    pltpu.make_async_copy(
        sendbuf.at[pl.ds(me, 1)], recvbuf.at[pl.ds(me, 1)], end_recv
    ).start()
    for copy in (rows, across, *along, *onward, *own, *relays):
        copy.wait_send()
    pltpu.make_async_copy(sendbuf, recvbuf, end_recv).wait()
    row = jnp.sum(recvbuf[...], axis=0, keepdims=True)
    wide_row = jnp.broadcast_to(row, (8, 128))
    at = lax.broadcasted_iota(jnp.int32, (8, 128), 0)
    spread = wide_row
    for j in range(1, 8):
        spread = jnp.where(at == j, pltpu.roll(wide_row, 128 - 16 * j, 1), spread)
    out_ref[...] = spread[:, : out_ref.shape[1]]
    pltpu.make_async_copy(
        sendbuf.at[pl.ds(0, ANG * RAD - 1)], recvbuf.at[pl.ds(0, ANG * RAD - 1)], end_send
    ).wait()


def shards(psi_bound, psi_cont, ylm, radial_weight, order):
    shells, nb, points = psi_bound.shape
    count = psi_cont.shape[1]
    any_space = pl.BlockSpec(memory_space=pl.ANY)
    dma = pltpu.SemaphoreType.DMA
    n_peers = len(PEERS)
    return pl.pallas_call(
        kernel,
        out_shape=jax.ShapeDtypeStruct((nb // ANG, count // RAD), F32),
        in_specs=[
            any_space,
            any_space,
            any_space,
            pl.BlockSpec(memory_space=pltpu.SMEM),
            pl.BlockSpec(memory_space=pltpu.VMEM),
        ],
        out_specs=pl.BlockSpec(memory_space=pltpu.VMEM),
        scratch_shapes=[
            pltpu.VMEM((ANG, shells * nb, points), BF16),
            pltpu.VMEM((shells * count, points), BF16),
            pltpu.VMEM((points, TOTAL), BF16),
            pltpu.VMEM((PIECE, TOTAL), BF16),
            pltpu.VMEM((TOTAL, 128), F32),
            pltpu.VMEM((TOTAL, points), BF16),
            pltpu.VMEM((PIECE, points), BF16),
            pltpu.VMEM((RAD, PIECE, points), BF16),
            pltpu.VMEM((shells * points, count), BF16),
            pltpu.VMEM((ANG * RAD, 128), F32),
            pltpu.VMEM((ANG * RAD, 128), F32),
            dma((3,)),
            dma((9 + 2 * n_peers,)),
            dma((7,)),
            dma,
            dma((n_peers,)),
            dma((n_peers + 1,)),
            dma,
            dma,
            pltpu.SemaphoreType.REGULAR((3,)),
        ],
        compiler_params=pltpu.CompilerParams(collective_id=0, has_side_effects=True),
        name="dipole",
    )(
        psi_bound.reshape(shells * nb, points),
        psi_cont.reshape(shells * count, points),
        ylm,
        radial_weight,
        order.reshape(8, TOTAL // 8),
    )


def solution(mesh):
    return jax.shard_map(
        shards,
        mesh=mesh,
        in_specs=(P("rad", None, "ang"), P("rad", None, "ang"), P("ang", None), P("rad"), P()),
        out_specs=P("ang", "rad"),
        check_vma=False,
    )
```

```python
import functools

import jax
import jax.numpy as jnp
from jax import lax
from jax.experimental import pallas as pl
from jax.experimental.pallas import tpu as pltpu
from jax.sharding import PartitionSpec as P

LMAX = 31
F32, BF16 = jnp.float32, jnp.bfloat16
NX, NY, NZ, NC, HALF = 4, 4, 8, 2, 4
ANG, RAD = 8, 32
PTS, TOTAL = 128, 1024
PIECE = PTS * ANG // RAD


def ring(d, n):
    return min(d, n - d)


PLANE = sorted(
    ((dx, dy, dc) for dx in range(NX) for dy in range(NY) for dc in range(NC) if (dx, dy, dc) != (0, 0, 0)),
    key=lambda o: -(ring(o[0], NX) + ring(o[1], NY)),
)
PEERS = [(dz, dy) for dz in range(HALF) for dy in range(NY) if (dz, dy) != (0, 0)]
BY_ID = pl.DeviceIdType.LOGICAL


def device(place):
    x, y, z, core = place
    return x * (ANG * RAD // NX) + z * (NY * NC) + y * NC + core


def turn_of(place):
    x, y, z, core = place
    return z * 32 + y * 8 + x * 2 + (1 - core)


def piece_of(x, half, zl, y, core):
    edge = (zl == 0) | (zl == HALF - 1)
    other = jnp.where(edge, 1 - half, half)
    pair = jnp.where(edge, zl // (HALF - 1), zl - 1)
    return ((x - y + 2 + NX) % NX) * 2 + other, pair * 2 + core


def coupling_rows(order):
    degree = jnp.zeros(order.shape, jnp.int32)
    for edge in range(1, LMAX + 1):
        degree = degree + (order >= edge * edge).astype(jnp.int32)
    m = order - degree * degree - degree
    lf, mf = degree.astype(F32), m.astype(F32)
    upper = jnp.where(degree + 1 <= LMAX, order + 2 * degree + 2, -1)
    upper_num = (lf + 1.0) * (lf + 1.0) - mf * mf
    upper_coef = jnp.sqrt(jnp.maximum(upper_num, 0.0) / ((2.0 * lf + 1.0) * (2.0 * lf + 3.0)))
    lower = jnp.where(degree - 1 >= jnp.abs(m), order - 2 * degree, -1)
    lower_num = lf * lf - mf * mf
    lower_den = jnp.maximum((2.0 * lf - 1.0) * (2.0 * lf + 1.0), 1.0)
    lower_coef = jnp.sqrt(jnp.maximum(lower_num, 0.0) / lower_den)
    return upper.astype(F32), upper_coef, lower.astype(F32), lower_coef


def turned(block):
    rows, lanes = block.shape
    row = lax.broadcasted_iota(jnp.int32, block.shape, 0)
    group = lax.broadcasted_iota(jnp.int32, block.shape, 1) // 16
    for s in (1, 2, 4):
        below = pltpu.roll(pltpu.roll(block, rows - s, 0), 16 * s, 1)
        above = pltpu.roll(pltpu.roll(block, s, 0), lanes - 16 * s, 1)
        low_row, low_group = (row & s) == 0, (group & s) == 0
        block = jnp.where(
            low_row == low_group, block, jnp.where(low_row, below, above)
        )
    return block


def kernel(
    bound_hbm, cont_hbm, ylm_hbm, weight_hbm, order_hbm, out_ref,
    bound, cont, ylm, order_ref, weight_ref, ys, ncol, z_ref, mine, m_full, cont_t, sendbuf, recvbuf,
    local_sem, out_sem, a_recv, f_recv, m_recv, relay_recv, end_send, end_recv, here, all_here,
):
    ang, rad = lax.axis_index("ang"), lax.axis_index("rad")
    x, half = ang // 2, ang % 2
    zl, y, core = rad // (NY * NC), (rad // NC) % NY, rad % NC
    z = half * HALF + zl
    me = ang * RAD + rad

    x_peers = [((x + d) % NX, y, z, core) for d in (2, 1, 3)]
    opposite = (x, y, (z + HALF) % NZ, core)
    twin = (x, y, z, 1 - core)
    peers = [(x, (y + dy) % NY, half * HALF + (zl + dz) % HALF, core) for dz, dy in PEERS]
    edge = (zl == 0) | (zl == HALF - 1)
    z_other = jnp.where(edge, NZ - 1 - z, z)
    rows_to = ((x + y + 2) % NX, y, z_other, 1 - core)
    rows_from = ((x - y + 2 + NX) % NX, y, z_other, 1 - core)

    turn = turn_of((x, y, z, core))
    links = [(rows_from, 2), (opposite, 1), *((p, 0) for p in x_peers), *((p, 3) for p in peers), (twin, 3), (rows_to, None)]
    firsts = [turn < turn_of(place) for place, _ in links]
    barrier = pltpu.get_barrier_semaphore()
    before = 0
    for (place, _), first in zip(links, firsts):
        before = before + jnp.where(first, 0, 1)

        @pl.when(first)
        def _():
            pl.semaphore_signal(barrier, inc=1, device_id=device(place), device_id_type=BY_ID)

    def send(src, dst, send_sem, recv_sem, where):
        return pltpu.make_async_remote_copy(
            src_ref=src, dst_ref=dst, send_sem=send_sem, recv_sem=recv_sem,
            device_id=device(where), device_id_type=BY_ID,
        )

    loads = [
        pltpu.make_async_copy(order_hbm, order_ref, local_sem.at[3]),
        pltpu.make_async_copy(ylm_hbm, ylm, local_sem.at[0]),
        pltpu.make_async_copy(cont_hbm, cont, local_sem.at[1]),
        pltpu.make_async_copy(bound_hbm, bound.at[ang], local_sem.at[2]),
        pltpu.make_async_copy(weight_hbm, weight_ref, local_sem.at[4]),
    ]
    load_order, load_ylm, load_cont, load_bound, load_weight = loads
    for load in loads:
        load.start()

    @pl.when(before > 0)
    def _():
        pl.semaphore_wait(barrier, before)

    for (place, kind), first in zip(links, firsts):
        if kind is not None:

            @pl.when(jnp.logical_not(first))
            def _():
                pl.semaphore_signal(here.at[kind], inc=1, device_id=device(place), device_id_type=BY_ID)

    _, quarter_to = piece_of(rows_to[0], z_other // HALF, z_other % HALF, y, 1 - core)
    rows = send(
        ylm_hbm.at[pl.ds(pl.multiple_of(quarter_to * PIECE, PIECE), PIECE)],
        ys, out_sem.at[0], f_recv, rows_to,
    )
    across = send(bound_hbm, bound.at[ang], out_sem.at[1], a_recv.at[0], opposite)
    along = [
        send(bound_hbm, bound.at[ang], out_sem.at[2 + i], a_recv.at[1 + i], where)
        for i, where in enumerate(x_peers)
    ]

    def wait_for(kind, *which):
        count = sum(jnp.where(firsts[i], 1, 0) for i in which)

        @pl.when(count > 0)
        def _():
            pl.semaphore_wait(here.at[kind], count)

    wait_for(2, len(links) - 1)
    rows.start()
    wait_for(0, 2, 3, 4)
    for copy in along:
        copy.start()


    @pl.when(jnp.logical_not(firsts[1]))
    def _():
        across.start()

    load_order.wait()
    order = order_ref[...]
    upper, upper_coef, lower, lower_coef = coupling_rows(order)
    orderf = order.astype(F32)
    for s in range(TOTAL // 128):
        ncol[pl.ds(s * 128, 128)] = jnp.broadcast_to(orderf[s : s + 1], (128, 128)).T
    load_ylm.wait()

    def couple(s, carry):
        here = pl.ds(pl.multiple_of(s * 128, 128), 128)
        column = ncol[here]
        blocks = []
        for t in range(TOTAL // 128):
            cut = slice(t, t + 1)
            blocks.append(
                jnp.where(
                    column == upper[cut],
                    upper_coef[cut],
                    jnp.where(column == lower[cut], lower_coef[cut], 0.0),
                ).astype(BF16)
            )
        g = jnp.concatenate(blocks, axis=1)
        z_ref[here] = lax.dot_general(
            g, ylm[...], (((1,), (1,)), ((), ())), preferred_element_type=F32
        ).astype(BF16)
        return carry

    lax.fori_loop(0, TOTAL // 128, couple, 0)

    @pl.when(firsts[1])
    def _():
        pl.semaphore_wait(here.at[1], 1)
        across.start()

    load_cont.wait()
    shells = weight_ref.shape[0]
    count = cont.shape[0] // shells
    for r in range(shells):
        for c in range(count // 128):
            block = cont[pl.ds(r * count + c * 128, 128)].astype(F32).T
            cont_t[pl.ds(r * 128, 128), pl.ds(c * 128, 128)] = block.astype(BF16)

    rows.wait_recv()
    mine[...] = jnp.dot(ys[...], z_ref[...], preferred_element_type=F32).astype(BF16)
    cls, quarter = piece_of(x, half, zl, y, core)
    block = cls * 4 + quarter
    wait_for(3, *range(5, 6 + len(peers)))
    own = [
        send(mine, m_full.at[block], out_sem.at[8 + i], m_recv.at[i], where)
        for i, where in enumerate(peers)
    ]
    for copy in own:
        copy.start()
    n_peers = len(peers)
    relays = [send(mine, m_full.at[block], out_sem.at[8 + n_peers], relay_recv.at[0], twin)]
    relays[0].start()
    m_full[block] = mine[...]

    pl.semaphore_signal(all_here.at[0], inc=1, device_id=device(opposite), device_id_type=BY_ID)
    across.wait_recv()
    opposite_cls = x * 2 + 1 - half
    onward = [
        send(bound.at[opposite_cls], bound.at[opposite_cls], out_sem.at[5 + i], a_recv.at[4 + i], where)
        for i, where in enumerate(x_peers)
    ]
    for copy in onward:
        copy.start()
    pl.semaphore_wait(all_here.at[0], 1)
    for where in x_peers:
        pl.semaphore_signal(all_here.at[1], inc=1, device_id=device(where), device_id_type=BY_ID)

    for i, (dz, dy) in enumerate(PEERS):
        own[i].wait_recv()
        there_cls, there_quarter = piece_of(
            x, half, (zl - dz + HALF) % HALF, (y - dy + NY) % NY, core
        )
        there = there_cls * 4 + there_quarter
        relay = send(
            m_full.at[there], m_full.at[there],
            out_sem.at[9 + n_peers + i], relay_recv.at[1 + i], twin,
        )
        relay.start()
        relays.append(relay)
    load_bound.wait()
    load_weight.wait()
    for copy in (*along, *onward):
        copy.wait_recv()
    pl.semaphore_wait(all_here.at[1], NX - 1)
    pl.semaphore_signal(all_here.at[2], inc=1, device_id=device(twin), device_id_type=BY_ID)
    bound_all = jnp.concatenate([bound[i] for i in range(ANG)], axis=1)
    for relay in relays:
        relay.wait_recv()
    pl.semaphore_wait(all_here.at[2], 1)

    operator = m_full[...].reshape(PTS * ANG, PTS)
    d = jnp.dot(bound_all, operator, preferred_element_type=F32)
    nb = d.shape[0] // shells
    weighted = [d[r * nb : (r + 1) * nb] * weight_ref[r] for r in range(shells)]
    wide = jnp.concatenate(weighted, axis=1).astype(BF16)
    terms = jnp.dot(wide, cont_t[...], preferred_element_type=F32)
    for q in range(count // 128):
        cut = turned(terms[:, q * 128 : (q + 1) * 128])
        for a in range(ANG):
            sendbuf[pl.ds(a * RAD + q * 8, 8)] = cut[a * 8 : a * 8 + 8]

    def give(number):
        pltpu.make_async_remote_copy(
            src_ref=sendbuf.at[pl.ds(number, 1)], dst_ref=recvbuf.at[pl.ds(me, 1)],
            send_sem=end_send, recv_sem=end_recv, device_id=number, device_id_type=BY_ID,
        ).start()

    columns = [
        device(((x + dx) % NX, (y + dy) % NY, 0, (core + dc) % NC)) for dx, dy, dc in PLANE
    ]
    for zs in (range(HALF), range(HALF, NZ)):
        for column in columns:
            for there in zs:
                give(column + there * (NY * NC))
    for dz in (4, 3, 5, 2, 6, 1, 7):
        give(device((x, y, (z + dz) % NZ, core)))
    pltpu.make_async_copy(
        sendbuf.at[pl.ds(me, 1)], recvbuf.at[pl.ds(me, 1)], end_recv
    ).start()
    for copy in (rows, across, *along, *onward, *own, *relays):
        copy.wait_send()
    pltpu.make_async_copy(sendbuf, recvbuf, end_recv).wait()
    row = jnp.sum(recvbuf[...], axis=0, keepdims=True)
    wide_row = jnp.broadcast_to(row, (8, 128))
    at = lax.broadcasted_iota(jnp.int32, (8, 128), 0)
    spread = wide_row
    for j in range(1, 8):
        spread = jnp.where(at == j, pltpu.roll(wide_row, 128 - 16 * j, 1), spread)
    out_ref[...] = spread[:, : out_ref.shape[1]]
    pltpu.make_async_copy(
        sendbuf.at[pl.ds(0, ANG * RAD - 1)], recvbuf.at[pl.ds(0, ANG * RAD - 1)], end_send
    ).wait()


def shards(psi_bound, psi_cont, ylm, radial_weight, order):
    shells, nb, points = psi_bound.shape
    count = psi_cont.shape[1]
    any_space = pl.BlockSpec(memory_space=pl.ANY)
    dma = pltpu.SemaphoreType.DMA
    n_peers = len(PEERS)
    return pl.pallas_call(
        kernel,
        out_shape=jax.ShapeDtypeStruct((nb // ANG, count // RAD), F32),
        in_specs=[
            any_space,
            any_space,
            any_space,
            any_space,
            any_space,
        ],
        out_specs=pl.BlockSpec(memory_space=pltpu.VMEM),
        scratch_shapes=[
            pltpu.VMEM((ANG, shells * nb, points), BF16),
            pltpu.VMEM((shells * count, points), BF16),
            pltpu.VMEM((points, TOTAL), BF16),
            pltpu.VMEM((8, TOTAL // 8), jnp.int32),
            pltpu.SMEM((shells,), F32),
            pltpu.VMEM((PIECE, TOTAL), BF16),
            pltpu.VMEM((TOTAL, 128), F32),
            pltpu.VMEM((TOTAL, points), BF16),
            pltpu.VMEM((PIECE, points), BF16),
            pltpu.VMEM((RAD, PIECE, points), BF16),
            pltpu.VMEM((shells * points, count), BF16),
            pltpu.VMEM((ANG * RAD, 128), F32),
            pltpu.VMEM((ANG * RAD, 128), F32),
            dma((5,)),
            dma((9 + 2 * n_peers,)),
            dma((7,)),
            dma,
            dma((n_peers,)),
            dma((n_peers + 1,)),
            dma,
            dma,
            pltpu.SemaphoreType.REGULAR((4,)),
            pltpu.SemaphoreType.REGULAR((3,)),
        ],
        compiler_params=pltpu.CompilerParams(collective_id=0, has_side_effects=True),
        name="dipole",
    )(
        psi_bound.reshape(shells * nb, points),
        psi_cont.reshape(shells * count, points),
        ylm,
        radial_weight,
        order.reshape(8, TOTAL // 8),
    )


def solution(mesh):
    return jax.shard_map(
        shards,
        mesh=mesh,
        in_specs=(P("rad", None, "ang"), P("rad", None, "ang"), P("ang", None), P("rad"), P()),
        out_specs=P("ang", "rad"),
        check_vma=False,
    )
```

```python
import functools

import jax
import jax.numpy as jnp
from jax import lax
from jax.experimental import pallas as pl
from jax.experimental.pallas import tpu as pltpu
from jax.sharding import PartitionSpec as P

LMAX = 31
F32, BF16 = jnp.float32, jnp.bfloat16
NX, NY, NZ, NC, HALF = 4, 4, 8, 2, 4
ANG, RAD = 8, 32
PTS, TOTAL = 128, 1024
PIECE = PTS * ANG // RAD


def ring(d, n):
    return min(d, n - d)


PLANE = sorted(
    ((dx, dy, dc) for dx in range(NX) for dy in range(NY) for dc in range(NC) if (dx, dy, dc) != (0, 0, 0)),
    key=lambda o: -(ring(o[0], NX) + ring(o[1], NY)),
)
BY_ID = pl.DeviceIdType.LOGICAL


def device(place):
    x, y, z, core = place
    return x * (ANG * RAD // NX) + z * (NY * NC) + y * NC + core


def turn_of(place):
    x, y, z, core = place
    return z * 32 + y * 8 + x * 2 + (1 - core)


def piece_of(x, half, zl, y, core):
    edge = (zl == 0) | (zl == HALF - 1)
    other = jnp.where(edge, 1 - half, half)
    pair = jnp.where(edge, lax.div(zl, HALF - 1), zl - 1)
    return lax.rem(x - y + 2 + NX, NX) * 2 + other, pair * 2 + core


def coupling_rows(order):
    degree = jnp.zeros(order.shape, jnp.int32)
    for edge in range(1, LMAX + 1):
        degree = degree + (order >= edge * edge).astype(jnp.int32)
    m = order - degree * degree - degree
    lf, mf = degree.astype(F32), m.astype(F32)
    upper = jnp.where(degree + 1 <= LMAX, order + 2 * degree + 2, -1)
    upper_num = (lf + 1.0) * (lf + 1.0) - mf * mf
    upper_coef = jnp.sqrt(jnp.maximum(upper_num, 0.0) / ((2.0 * lf + 1.0) * (2.0 * lf + 3.0)))
    lower = jnp.where(degree - 1 >= jnp.abs(m), order - 2 * degree, -1)
    lower_num = lf * lf - mf * mf
    lower_den = jnp.maximum((2.0 * lf - 1.0) * (2.0 * lf + 1.0), 1.0)
    lower_coef = jnp.sqrt(jnp.maximum(lower_num, 0.0) / lower_den)
    return upper.astype(F32), upper_coef, lower.astype(F32), lower_coef


def turned(block):
    rows, lanes = block.shape
    row = lax.broadcasted_iota(jnp.int32, block.shape, 0)
    group = lax.broadcasted_iota(jnp.int32, block.shape, 1) // 16
    for s in (1, 2, 4):
        below = pltpu.roll(pltpu.roll(block, rows - s, 0), 16 * s, 1)
        above = pltpu.roll(pltpu.roll(block, s, 0), lanes - 16 * s, 1)
        low_row, low_group = (row & s) == 0, (group & s) == 0
        block = jnp.where(
            low_row == low_group, block, jnp.where(low_row, below, above)
        )
    return block


def kernel(
    bound_hbm, cont_hbm, ylm_hbm, weight_hbm, order_hbm, out_ref,
    bound, cont, ylm, order_ref, weight_ref, ys, ncol, z_ref, mine, m_full, cont_t, sendbuf, recvbuf,
    local_sem, out_sem, a_recv, f_recv, m_recv, relay_recv, end_send, end_recv, here, all_here,
):
    ang, rad = lax.axis_index("ang"), lax.axis_index("rad")
    x, half, core, spot = lax.div(ang, 2), lax.rem(ang, 2), lax.rem(rad, NC), lax.div(rad, NC)
    zl, y = lax.div(spot, NY), lax.rem(spot, NY)
    z = half * HALF + zl
    me = ang * RAD + rad
    x_step = ANG * RAD // NX
    x_peers = [me + (lax.rem(x + d, NX) - x) * x_step for d in (2, 1, 3)]
    opposite = me + RAD - 2 * RAD * half
    twin = me + 1 - 2 * core
    first_spot = me - NC * spot
    edge = (zl == 0) | (zl == HALF - 1)
    z_other = jnp.where(edge, NZ - 1 - z, z)
    turn = turn_of((x, y, z, core))
    to_x, from_x = lax.rem(x + y + 2, NX), lax.rem(x - y + 2 + NX, NX)
    rows_to, rows_from = (device((i, y, z_other, 1 - core)) for i in (to_x, from_x))
    ahead_to, ahead_from = (turn < turn_of((i, y, z_other, 1 - core)) for i in (to_x, from_x))
    count = lambda flag: jnp.where(flag, 1, 0)

    def signal(semaphore, where):
        pl.semaphore_signal(semaphore, inc=1, device_id=where, device_id_type=BY_ID)

    def each(start, end, act):
        def body(i, carry):
            act(i)
            return carry

        lax.fori_loop(start, end, body, 0)

    def send(src, dst, send_sem, recv_sem, where):
        return pltpu.make_async_remote_copy(
            src_ref=src, dst_ref=dst, send_sem=send_sem, recv_sem=recv_sem,
            device_id=where, device_id_type=BY_ID,
        )

    loads = [
        pltpu.make_async_copy(ylm_hbm, ylm, local_sem.at[0]),
        pltpu.make_async_copy(order_hbm, order_ref, local_sem.at[3]),
        pltpu.make_async_copy(cont_hbm, cont, local_sem.at[1]),
        pltpu.make_async_copy(bound_hbm, bound.at[ang], local_sem.at[2]),
        pltpu.make_async_copy(weight_hbm, weight_ref, local_sem.at[4]),
    ]
    load_ylm, load_order, load_cont, load_bound, load_weight = loads
    for load in loads:
        load.start()

    barrier = pltpu.get_barrier_semaphore()

    @pl.when(ahead_from)
    def _():
        signal(barrier, rows_from)

    @pl.when(ahead_to)
    def _():
        signal(barrier, rows_to)

    @pl.when(half == 0)
    def _():
        signal(barrier, opposite)

    each(x + 1, NX, lambda i: signal(barrier, me + (i - x) * x_step))

    @pl.when(core == 1)
    def _():
        signal(barrier, twin)

    each(spot + 1, RAD // NC, lambda i: signal(barrier, first_spot + NC * i))
    before = 2 - count(ahead_from) - count(ahead_to) + half + x + (1 - core) + spot

    @pl.when(before > 0)
    def _():
        pl.semaphore_wait(barrier, before)

    @pl.when(jnp.logical_not(ahead_from))
    def _():
        signal(here.at[2], rows_from)

    quarter_to = piece_of(to_x, lax.div(z_other, HALF), lax.rem(z_other, HALF), y, 1 - core)[1]
    rows = send(
        ylm_hbm.at[pl.ds(pl.multiple_of(quarter_to * PIECE, PIECE), PIECE)],
        ys, out_sem.at[0], f_recv, rows_to,
    )
    across = send(bound_hbm, bound.at[ang], out_sem.at[1], a_recv.at[0], opposite)

    @pl.when(jnp.logical_not(ahead_to))
    def _():
        rows.start()

    each(0, x, lambda i: signal(here.at[0], me + (i - x) * x_step))

    @pl.when(half == 1)
    def _():
        signal(here.at[1], opposite)
        across.start()

    @pl.when(core == 0)
    def _():
        signal(here.at[3], twin)

    each(0, spot, lambda i: signal(here.at[3], first_spot + NC * i))

    @pl.when(ahead_to)
    def _():
        pl.semaphore_wait(here.at[2], 1)
        rows.start()

    @pl.when(x < NX - 1)
    def _():
        pl.semaphore_wait(here.at[0], NX - 1 - x)

    along = [
        send(bound_hbm, bound.at[ang], out_sem.at[2], a_recv.at[1], where) for where in x_peers
    ]
    for copy in along:
        copy.start()

    load_order.wait()
    order = order_ref[...]
    upper, upper_coef, lower, lower_coef = coupling_rows(order)
    orderf = order.astype(F32)
    for s in range(TOTAL // 128):
        ncol[pl.ds(s * 128, 128)] = jnp.broadcast_to(orderf[s : s + 1], (128, 128)).T
    load_ylm.wait()

    def couple(s, carry):
        here = pl.ds(pl.multiple_of(s * 128, 128), 128)
        column = ncol[here]
        blocks = []
        for t in range(TOTAL // 128):
            cut = slice(t, t + 1)
            blocks.append(
                jnp.where(
                    column == upper[cut],
                    upper_coef[cut],
                    jnp.where(column == lower[cut], lower_coef[cut], 0.0),
                ).astype(BF16)
            )
        g = jnp.concatenate(blocks, axis=1)
        z_ref[here] = lax.dot_general(
            g, ylm[...], (((1,), (1,)), ((), ())), preferred_element_type=F32
        ).astype(BF16)
        return carry

    lax.fori_loop(0, TOTAL // 128, couple, 0)

    @pl.when(half == 0)
    def _():
        pl.semaphore_wait(here.at[1], 1)
        across.start()

    def block_of(i):
        cls, quarter = piece_of(x, half, lax.div(i, NY), lax.rem(i, NY), core)
        return cls * (RAD // ANG) + quarter

    block = block_of(spot)
    rows.wait_recv()
    mine[...] = jnp.dot(ys[...], z_ref[...], preferred_element_type=F32).astype(BF16)
    spots = RAD // NC
    later_ones = spots - 1 - spot + core

    @pl.when(later_ones > 0)
    def _():
        pl.semaphore_wait(here.at[3], later_ones)

    def give_piece(i):
        send(mine, m_full.at[block], out_sem.at[3], m_recv.at[spot], first_spot + NC * i).start()

    each(spot + 1, spots, give_piece)
    each(0, spot, give_piece)
    send(mine, m_full.at[block], out_sem.at[4], relay_recv, twin).start()
    m_full[block] = mine[...]

    signal(all_here.at[0], opposite)
    across.wait_recv()
    other_cls = bound.at[ang + 1 - 2 * half]
    onward = [send(other_cls, other_cls, out_sem.at[5], a_recv.at[2], where) for where in x_peers]
    for copy in onward:
        copy.start()
    pl.semaphore_wait(all_here.at[0], 1)
    for where in x_peers:
        signal(all_here.at[1], where)

    load_cont.wait()
    shells = weight_ref.shape[0]
    count_c = cont.shape[0] // shells
    for r in range(shells):
        for c in range(count_c // 128):
            part = cont[pl.ds(r * count_c + c * 128, 128)].astype(F32).T
            cont_t[pl.ds(r * 128, 128), pl.ds(c * 128, 128)] = part.astype(BF16)

    def pass_on(i):
        there = m_full.at[block_of(i)]
        send(there, there, out_sem.at[4], m_recv.at[i], twin).wait_recv()
        send(there, there, out_sem.at[4], relay_recv, twin).start()

    each(0, spot, pass_on)
    each(spot + 1, spots, pass_on)
    load_bound.wait()
    load_weight.wait()
    three = bound.at[pl.ds(0, NX - 1)]
    for i in (1, 2):
        send(three, three, out_sem.at[2], a_recv.at[i], twin).wait_recv()
    pl.semaphore_wait(all_here.at[1], NX - 1)
    signal(all_here.at[2], twin)
    bound_all = jnp.concatenate([bound[i] for i in range(ANG)], axis=1)
    half_m = m_full.at[pl.ds(0, spots)]
    send(half_m, half_m, out_sem.at[4], relay_recv, twin).wait_recv()
    pl.semaphore_wait(all_here.at[2], 1)

    operator = m_full[...].reshape(PTS * ANG, PTS)
    d = jnp.dot(bound_all, operator, preferred_element_type=F32)
    nb = d.shape[0] // shells
    weighted = [d[r * nb : (r + 1) * nb] * weight_ref[r] for r in range(shells)]
    wide = jnp.concatenate(weighted, axis=1).astype(BF16)
    terms = jnp.dot(wide, cont_t[...], preferred_element_type=F32)
    for q in range(count_c // 128):
        cut = turned(terms[:, q * 128 : (q + 1) * 128])
        for a in range(ANG):
            sendbuf[pl.ds(a * RAD + q * 8, 8)] = cut[a * 8 : a * 8 + 8]

    def give(number):
        pltpu.make_async_remote_copy(
            src_ref=sendbuf.at[pl.ds(number, 1)], dst_ref=recvbuf.at[pl.ds(me, 1)],
            send_sem=end_send, recv_sem=end_recv, device_id=number, device_id_type=BY_ID,
        ).start()

    columns = [
        device((lax.rem(x + dx, NX), lax.rem(y + dy, NY), 0, lax.rem(core + dc, NC)))
        for dx, dy, dc in PLANE
    ]
    for zs in (range(HALF), range(HALF, NZ)):
        for column in columns:
            for there in zs:
                give(column + there * (NY * NC))
    own_column = device((x, y, 0, core))
    for dz in (4, 3, 5, 2, 6, 1, 7):
        give(own_column + lax.rem(z + dz, NZ) * (NY * NC))
    pltpu.make_async_copy(
        sendbuf.at[pl.ds(me, 1)], recvbuf.at[pl.ds(me, 1)], end_recv
    ).start()
    rows.wait_send()
    across.wait_send()
    for i in (2, 5):
        send(three, three, out_sem.at[i], a_recv.at[1], twin).wait_send()
    own_m = m_full.at[pl.ds(0, spots - 1)]
    send(own_m, own_m, out_sem.at[3], relay_recv, twin).wait_send()
    send(half_m, half_m, out_sem.at[4], relay_recv, twin).wait_send()
    pltpu.make_async_copy(sendbuf, recvbuf, end_recv).wait()
    row = jnp.sum(recvbuf[...], axis=0, keepdims=True)
    wide_row = jnp.broadcast_to(row, (8, 128))
    at = lax.broadcasted_iota(jnp.int32, (8, 128), 0)
    spread = wide_row
    for j in range(1, 8):
        spread = jnp.where(at == j, pltpu.roll(wide_row, 128 - 16 * j, 1), spread)
    out_ref[...] = spread[:, : out_ref.shape[1]]
    pltpu.make_async_copy(
        sendbuf.at[pl.ds(0, ANG * RAD - 1)], recvbuf.at[pl.ds(0, ANG * RAD - 1)], end_send
    ).wait()


def shards(psi_bound, psi_cont, ylm, radial_weight, order):
    shells, nb, points = psi_bound.shape
    count = psi_cont.shape[1]
    any_space = pl.BlockSpec(memory_space=pl.ANY)
    dma = pltpu.SemaphoreType.DMA
    return pl.pallas_call(
        kernel,
        out_shape=jax.ShapeDtypeStruct((nb // ANG, count // RAD), F32),
        in_specs=[
            any_space,
            any_space,
            any_space,
            any_space,
            any_space,
        ],
        out_specs=pl.BlockSpec(memory_space=pltpu.VMEM),
        scratch_shapes=[
            pltpu.VMEM((ANG, shells * nb, points), BF16),
            pltpu.VMEM((shells * count, points), BF16),
            pltpu.VMEM((points, TOTAL), BF16),
            pltpu.VMEM((8, TOTAL // 8), jnp.int32),
            pltpu.SMEM((shells,), F32),
            pltpu.VMEM((PIECE, TOTAL), BF16),
            pltpu.VMEM((TOTAL, 128), F32),
            pltpu.VMEM((TOTAL, points), BF16),
            pltpu.VMEM((PIECE, points), BF16),
            pltpu.VMEM((RAD, PIECE, points), BF16),
            pltpu.VMEM((shells * points, count), BF16),
            pltpu.VMEM((ANG * RAD, 128), F32),
            pltpu.VMEM((ANG * RAD, 128), F32),
            dma((5,)),
            dma((6,)),
            dma((3,)),
            dma,
            dma((RAD // NC,)),
            dma,
            dma,
            dma,
            pltpu.SemaphoreType.REGULAR((4,)),
            pltpu.SemaphoreType.REGULAR((3,)),
        ],
        compiler_params=pltpu.CompilerParams(collective_id=0, has_side_effects=True),
        name="dipole",
    )(
        psi_bound.reshape(shells * nb, points),
        psi_cont.reshape(shells * count, points),
        ylm,
        radial_weight,
        order.reshape(8, TOTAL // 8),
    )


def solution(mesh):
    return jax.shard_map(
        shards,
        mesh=mesh,
        in_specs=(P("rad", None, "ang"), P("rad", None, "ang"), P("ang", None), P("rad"), P()),
        out_specs=P("ang", "rad"),
        check_vma=False,
    )
```

```python
import functools

import jax
import jax.numpy as jnp
from jax import lax
from jax.experimental import pallas as pl
from jax.experimental.pallas import tpu as pltpu
from jax.sharding import PartitionSpec as P

LMAX = 31
F32, BF16 = jnp.float32, jnp.bfloat16
NX, NY, NZ, NC, HALF = 4, 4, 8, 2, 4
ANG, RAD = 8, 32
PTS, TOTAL = 128, 1024
PIECE = PTS * ANG // RAD


def ring(d, n):
    return min(d, n - d)


PLANE = sorted(
    ((dx, dy, dc) for dx in range(NX) for dy in range(NY) for dc in range(NC) if (dx, dy, dc) != (0, 0, 0)),
    key=lambda o: -(ring(o[0], NX) + ring(o[1], NY)),
)
BY_ID = pl.DeviceIdType.LOGICAL


def device(place):
    x, y, z, core = place
    return x * (ANG * RAD // NX) + z * (NY * NC) + y * NC + core


def piece_of(x, half, zl, y, core):
    edge = (zl == 0) | (zl == HALF - 1)
    other = jnp.where(edge, 1 - half, half)
    pair = jnp.where(edge, lax.div(zl, HALF - 1), zl - 1)
    return lax.rem(x - y + 2 + NX, NX) * 2 + other, pair * 2 + core


def coupling_rows(order):
    degree = jnp.zeros(order.shape, jnp.int32)
    for edge in range(1, LMAX + 1):
        degree = degree + (order >= edge * edge).astype(jnp.int32)
    m = order - degree * degree - degree
    lf, mf = degree.astype(F32), m.astype(F32)
    upper = jnp.where(degree + 1 <= LMAX, order + 2 * degree + 2, -1)
    upper_num = (lf + 1.0) * (lf + 1.0) - mf * mf
    upper_coef = jnp.sqrt(jnp.maximum(upper_num, 0.0) / ((2.0 * lf + 1.0) * (2.0 * lf + 3.0)))
    lower = jnp.where(degree - 1 >= jnp.abs(m), order - 2 * degree, -1)
    lower_num = lf * lf - mf * mf
    lower_den = jnp.maximum((2.0 * lf - 1.0) * (2.0 * lf + 1.0), 1.0)
    lower_coef = jnp.sqrt(jnp.maximum(lower_num, 0.0) / lower_den)
    return upper.astype(F32), upper_coef, lower.astype(F32), lower_coef


def turned(block):
    rows, lanes = block.shape
    row = lax.broadcasted_iota(jnp.int32, block.shape, 0)
    group = lax.broadcasted_iota(jnp.int32, block.shape, 1) // 16
    for s in (1, 2, 4):
        below = pltpu.roll(pltpu.roll(block, rows - s, 0), 16 * s, 1)
        above = pltpu.roll(pltpu.roll(block, s, 0), lanes - 16 * s, 1)
        low_row, low_group = (row & s) == 0, (group & s) == 0
        block = jnp.where(
            low_row == low_group, block, jnp.where(low_row, below, above)
        )
    return block


def kernel(
    bound_hbm, cont_hbm, ylm_hbm, weight_hbm, order_hbm, out_ref,
    bound, cont, ylm, order_ref, weight_ref, ys, ncol, z_ref, mine, m_full, cont_t, sendbuf, recvbuf,
    local_sem, out_sem, a_recv, f_recv, m_recv, relay_recv, end_send, end_recv, here, all_here,
):
    ang, rad = lax.axis_index("ang"), lax.axis_index("rad")
    x, half, core, spot = lax.div(ang, 2), lax.rem(ang, 2), lax.rem(rad, NC), lax.div(rad, NC)
    zl, y = lax.div(spot, NY), lax.rem(spot, NY)
    z = half * HALF + zl
    me = ang * RAD + rad
    x_step = ANG * RAD // NX
    x_peers = [me + (lax.rem(x + d, NX) - x) * x_step for d in (2, 1, 3)]
    opposite = me + RAD - 2 * RAD * half
    twin = me + 1 - 2 * core
    first_spot = me - NC * spot
    edge = (zl == 0) | (zl == HALF - 1)
    z_other = jnp.where(edge, NZ - 1 - z, z)
    to_x, from_x = lax.rem(x + y + 2, NX), lax.rem(x - y + 2 + NX, NX)
    rows_to, rows_from = (device((i, y, z_other, 1 - core)) for i in (to_x, from_x))
    y_peers = [me + (lax.rem(y + d, NY) - y) * NC for d in (2, 1, 3)]
    zl_peers = [me + (lax.rem(zl + d, HALF) - zl) * NY * NC for d in (2, 1, 3)]

    def signal(semaphore, where):
        pl.semaphore_signal(semaphore, inc=1, device_id=where, device_id_type=BY_ID)

    def each(start, end, act):
        def body(i, carry):
            act(i)
            return carry

        lax.fori_loop(start, end, body, 0)

    def send(src, dst, send_sem, recv_sem, where):
        return pltpu.make_async_remote_copy(
            src_ref=src, dst_ref=dst, send_sem=send_sem, recv_sem=recv_sem,
            device_id=where, device_id_type=BY_ID,
        )

    barrier = pltpu.get_barrier_semaphore()
    lines = (opposite, rows_from, rows_to, *zl_peers, *x_peers, *y_peers, twin)
    for where in lines:
        signal(barrier, where)
    loads = [
        pltpu.make_async_copy(ylm_hbm, ylm, local_sem.at[0]),
        pltpu.make_async_copy(order_hbm, order_ref, local_sem.at[3]),
        pltpu.make_async_copy(cont_hbm, cont, local_sem.at[1]),
        pltpu.make_async_copy(bound_hbm, bound.at[ang], local_sem.at[2]),
        pltpu.make_async_copy(weight_hbm, weight_ref, local_sem.at[4]),
    ]
    load_ylm, load_order, load_cont, load_bound, load_weight = loads
    for load in loads:
        load.start()
    pl.semaphore_wait(barrier, len(lines))

    quarter_to = piece_of(to_x, lax.div(z_other, HALF), lax.rem(z_other, HALF), y, 1 - core)[1]
    rows = send(
        ylm_hbm.at[pl.ds(pl.multiple_of(quarter_to * PIECE, PIECE), PIECE)],
        ys, out_sem.at[0], f_recv, rows_to,
    )
    across = send(bound_hbm, bound.at[ang], out_sem.at[1], a_recv.at[0], opposite)

    rows.start()
    across.start()
    along = [
        send(bound_hbm, bound.at[ang], out_sem.at[2], a_recv.at[1], where) for where in x_peers
    ]
    for copy in along:
        copy.start()
    for where in y_peers:
        signal(here, where)

    load_order.wait()
    order = order_ref[...]
    upper, upper_coef, lower, lower_coef = coupling_rows(order)
    orderf = order.astype(F32)
    for s in range(TOTAL // 128):
        ncol[pl.ds(s * 128, 128)] = jnp.broadcast_to(orderf[s : s + 1], (128, 128)).T
    load_ylm.wait()

    def couple(s, carry):
        here = pl.ds(pl.multiple_of(s * 128, 128), 128)
        column = ncol[here]
        blocks = []
        for t in range(TOTAL // 128):
            cut = slice(t, t + 1)
            blocks.append(
                jnp.where(
                    column == upper[cut],
                    upper_coef[cut],
                    jnp.where(column == lower[cut], lower_coef[cut], 0.0),
                ).astype(BF16)
            )
        g = jnp.concatenate(blocks, axis=1)
        z_ref[here] = lax.dot_general(
            g, ylm[...], (((1,), (1,)), ((), ())), preferred_element_type=F32
        ).astype(BF16)
        return carry

    lax.fori_loop(0, TOTAL // 128, couple, 0)

    def block_of(i):
        cls, quarter = piece_of(x, half, lax.div(i, NY), lax.rem(i, NY), core)
        return cls * (RAD // ANG) + quarter

    block = block_of(spot)
    rows.wait_recv()
    mine[...] = jnp.dot(ys[...], z_ref[...], preferred_element_type=F32).astype(BF16)
    spots = RAD // NC
    pl.semaphore_wait(here, NY - 1)

    def give_piece(i):
        send(mine, m_full.at[block], out_sem.at[3], m_recv.at[spot], first_spot + NC * i).start()

    each(spot + 1, spots, give_piece)
    each(0, spot, give_piece)
    send(mine, m_full.at[block], out_sem.at[4], relay_recv, twin).start()
    m_full[block] = mine[...]

    signal(all_here.at[0], opposite)
    across.wait_recv()
    other_cls = bound.at[ang + 1 - 2 * half]
    onward = [send(other_cls, other_cls, out_sem.at[5], a_recv.at[2], where) for where in x_peers]
    for copy in onward:
        copy.start()
    pl.semaphore_wait(all_here.at[0], 1)
    for where in x_peers:
        signal(all_here.at[1], where)

    load_cont.wait()
    shells = weight_ref.shape[0]
    count_c = cont.shape[0] // shells
    for r in range(shells):
        for c in range(count_c // 128):
            part = cont[pl.ds(r * count_c + c * 128, 128)].astype(F32).T
            cont_t[pl.ds(r * 128, 128), pl.ds(c * 128, 128)] = part.astype(BF16)

    def pass_on(i):
        there = m_full.at[block_of(i)]
        send(there, there, out_sem.at[4], m_recv.at[i], twin).wait_recv()
        send(there, there, out_sem.at[4], relay_recv, twin).start()

    each(0, spot, pass_on)
    each(spot + 1, spots, pass_on)
    load_bound.wait()
    load_weight.wait()
    three = bound.at[pl.ds(0, NX - 1)]
    for i in (1, 2):
        send(three, three, out_sem.at[2], a_recv.at[i], twin).wait_recv()
    pl.semaphore_wait(all_here.at[1], NX - 1)
    signal(all_here.at[2], twin)
    bound_all = jnp.concatenate([bound[i] for i in range(ANG)], axis=1)
    half_m = m_full.at[pl.ds(0, spots)]
    send(half_m, half_m, out_sem.at[4], relay_recv, twin).wait_recv()
    pl.semaphore_wait(all_here.at[2], 1)

    operator = m_full[...].reshape(PTS * ANG, PTS)
    d = jnp.dot(bound_all, operator, preferred_element_type=F32)
    nb = d.shape[0] // shells
    weighted = [d[r * nb : (r + 1) * nb] * weight_ref[r] for r in range(shells)]
    wide = jnp.concatenate(weighted, axis=1).astype(BF16)
    terms = jnp.dot(wide, cont_t[...], preferred_element_type=F32)
    for q in range(count_c // 128):
        cut = turned(terms[:, q * 128 : (q + 1) * 128])
        for a in range(ANG):
            sendbuf[pl.ds(a * RAD + q * 8, 8)] = cut[a * 8 : a * 8 + 8]

    def give(number):
        pltpu.make_async_remote_copy(
            src_ref=sendbuf.at[pl.ds(number, 1)], dst_ref=recvbuf.at[pl.ds(me, 1)],
            send_sem=end_send, recv_sem=end_recv, device_id=number, device_id_type=BY_ID,
        ).start()

    columns = [
        device((lax.rem(x + dx, NX), lax.rem(y + dy, NY), 0, lax.rem(core + dc, NC)))
        for dx, dy, dc in PLANE
    ]
    for zs in (range(HALF), range(HALF, NZ)):
        for column in columns:
            for there in zs:
                give(column + there * (NY * NC))
    own_column = device((x, y, 0, core))
    for dz in (4, 3, 5, 2, 6, 1, 7):
        give(own_column + lax.rem(z + dz, NZ) * (NY * NC))
    pltpu.make_async_copy(
        sendbuf.at[pl.ds(me, 1)], recvbuf.at[pl.ds(me, 1)], end_recv
    ).start()
    rows.wait_send()
    across.wait_send()
    for i in (2, 5):
        send(three, three, out_sem.at[i], a_recv.at[1], twin).wait_send()
    own_m = m_full.at[pl.ds(0, spots - 1)]
    send(own_m, own_m, out_sem.at[3], relay_recv, twin).wait_send()
    send(half_m, half_m, out_sem.at[4], relay_recv, twin).wait_send()
    pltpu.make_async_copy(sendbuf, recvbuf, end_recv).wait()
    row = jnp.sum(recvbuf[...], axis=0, keepdims=True)
    wide_row = jnp.broadcast_to(row, (8, 128))
    at = lax.broadcasted_iota(jnp.int32, (8, 128), 0)
    spread = wide_row
    for j in range(1, 8):
        spread = jnp.where(at == j, pltpu.roll(wide_row, 128 - 16 * j, 1), spread)
    out_ref[...] = spread[:, : out_ref.shape[1]]
    pltpu.make_async_copy(
        sendbuf.at[pl.ds(0, ANG * RAD - 1)], recvbuf.at[pl.ds(0, ANG * RAD - 1)], end_send
    ).wait()


def shards(psi_bound, psi_cont, ylm, radial_weight, order):
    shells, nb, points = psi_bound.shape
    count = psi_cont.shape[1]
    any_space = pl.BlockSpec(memory_space=pl.ANY)
    dma = pltpu.SemaphoreType.DMA
    return pl.pallas_call(
        kernel,
        out_shape=jax.ShapeDtypeStruct((nb // ANG, count // RAD), F32),
        in_specs=[
            any_space,
            any_space,
            any_space,
            any_space,
            any_space,
        ],
        out_specs=pl.BlockSpec(memory_space=pltpu.VMEM),
        scratch_shapes=[
            pltpu.VMEM((ANG, shells * nb, points), BF16),
            pltpu.VMEM((shells * count, points), BF16),
            pltpu.VMEM((points, TOTAL), BF16),
            pltpu.VMEM((8, TOTAL // 8), jnp.int32),
            pltpu.SMEM((shells,), F32),
            pltpu.VMEM((PIECE, TOTAL), BF16),
            pltpu.VMEM((TOTAL, 128), F32),
            pltpu.VMEM((TOTAL, points), BF16),
            pltpu.VMEM((PIECE, points), BF16),
            pltpu.VMEM((RAD, PIECE, points), BF16),
            pltpu.VMEM((shells * points, count), BF16),
            pltpu.VMEM((ANG * RAD, 128), F32),
            pltpu.VMEM((ANG * RAD, 128), F32),
            dma((5,)),
            dma((6,)),
            dma((3,)),
            dma,
            dma((RAD // NC,)),
            dma,
            dma,
            dma,
            pltpu.SemaphoreType.REGULAR,
            pltpu.SemaphoreType.REGULAR((3,)),
        ],
        compiler_params=pltpu.CompilerParams(collective_id=0, has_side_effects=True),
        name="dipole",
    )(
        psi_bound.reshape(shells * nb, points),
        psi_cont.reshape(shells * count, points),
        ylm,
        radial_weight,
        order.reshape(8, TOTAL // 8),
    )


def solution(mesh):
    return jax.shard_map(
        shards,
        mesh=mesh,
        in_specs=(P("rad", None, "ang"), P("rad", None, "ang"), P("ang", None), P("rad"), P()),
        out_specs=P("ang", "rad"),
        check_vma=False,
    )
```

```python
import functools

import jax
import jax.numpy as jnp
from jax import lax
from jax.experimental import pallas as pl
from jax.experimental.pallas import tpu as pltpu
from jax.sharding import PartitionSpec as P

LMAX = 31
F32, BF16 = jnp.float32, jnp.bfloat16
NX, NY, NZ, NC, HALF = 4, 4, 8, 2, 4
ANG, RAD = 8, 32
PTS, TOTAL = 128, 1024
PIECE = PTS * ANG // RAD


def ring(d, n):
    return min(d, n - d)


PLANE = sorted(
    ((dx, dy, dc) for dx in range(NX) for dy in range(NY) for dc in range(NC) if (dx, dy, dc) != (0, 0, 0)),
    key=lambda o: -(ring(o[0], NX) + ring(o[1], NY)),
)
BY_ID = pl.DeviceIdType.LOGICAL


def device(place):
    x, y, z, core = place
    return x * (ANG * RAD // NX) + z * (NY * NC) + y * NC + core


def piece_of(x, half, zl, y, core):
    edge = (zl == 0) | (zl == HALF - 1)
    other = jnp.where(edge, 1 - half, half)
    pair = jnp.where(edge, lax.div(zl, HALF - 1), zl - 1)
    return lax.rem(x - y + 2 + NX, NX) * 2 + other, pair * 2 + core


def coupling_rows(order):
    degree = jnp.zeros(order.shape, jnp.int32)
    for edge in range(1, LMAX + 1):
        degree = degree + (order >= edge * edge).astype(jnp.int32)
    m = order - degree * degree - degree
    lf, mf = degree.astype(F32), m.astype(F32)
    upper = jnp.where(degree + 1 <= LMAX, order + 2 * degree + 2, -1)
    upper_num = (lf + 1.0) * (lf + 1.0) - mf * mf
    upper_coef = jnp.sqrt(jnp.maximum(upper_num, 0.0) / ((2.0 * lf + 1.0) * (2.0 * lf + 3.0)))
    lower = jnp.where(degree - 1 >= jnp.abs(m), order - 2 * degree, -1)
    lower_num = lf * lf - mf * mf
    lower_den = jnp.maximum((2.0 * lf - 1.0) * (2.0 * lf + 1.0), 1.0)
    lower_coef = jnp.sqrt(jnp.maximum(lower_num, 0.0) / lower_den)
    return upper.astype(F32), upper_coef, lower.astype(F32), lower_coef


def turned(block):
    rows, lanes = block.shape
    row = lax.broadcasted_iota(jnp.int32, block.shape, 0)
    group = lax.broadcasted_iota(jnp.int32, block.shape, 1) // 16
    for s in (1, 2, 4):
        below = pltpu.roll(pltpu.roll(block, rows - s, 0), 16 * s, 1)
        above = pltpu.roll(pltpu.roll(block, s, 0), lanes - 16 * s, 1)
        low_row, low_group = (row & s) == 0, (group & s) == 0
        block = jnp.where(
            low_row == low_group, block, jnp.where(low_row, below, above)
        )
    return block


def kernel(
    bound_hbm, cont_hbm, ylm_hbm, weight_hbm, order_hbm, out_ref,
    bound, cont, ylm, order_ref, weight_ref, ys, ncol, z_ref, mine, m_full, cont_t, *rest
):
    sendbufs, (recvbuf, *semaphores) = rest[:HALF], rest[HALF:]
    local_sem, out_sem, a_recv, f_recv, m_recv, relay_recv, end_send, end_recv, *signals = semaphores
    here, answer, all_here = signals
    ang, rad = lax.axis_index("ang"), lax.axis_index("rad")
    x, half, core, spot = lax.div(ang, 2), lax.rem(ang, 2), lax.rem(rad, NC), lax.div(rad, NC)
    zl, y = lax.div(spot, NY), lax.rem(spot, NY)
    z = half * HALF + zl
    me = ang * RAD + rad
    x_step = ANG * RAD // NX
    x_peers = [me + (lax.rem(x + d, NX) - x) * x_step for d in (2, 1, 3)]
    opposite = me + RAD - 2 * RAD * half
    twin = me + 1 - 2 * core
    first_spot = me - NC * spot
    edge = (zl == 0) | (zl == HALF - 1)
    z_other = jnp.where(edge, NZ - 1 - z, z)
    to_x, from_x = lax.rem(x + y + 2, NX), lax.rem(x - y + 2 + NX, NX)
    rows_to, rows_from = (device((i, y, z_other, 1 - core)) for i in (to_x, from_x))
    y_peers = [me + (lax.rem(y + d, NY) - y) * NC for d in (2, 1, 3)]
    zl_peers = [me + (lax.rem(zl + d, HALF) - zl) * NY * NC for d in (2, 1, 3)]

    def signal(semaphore, where):
        pl.semaphore_signal(semaphore, inc=1, device_id=where, device_id_type=BY_ID)

    def each(start, end, act):
        def body(i, carry):
            act(i)
            return carry

        lax.fori_loop(start, end, body, 0)

    def send(src, dst, send_sem, recv_sem, where):
        return pltpu.make_async_remote_copy(
            src_ref=src, dst_ref=dst, send_sem=send_sem, recv_sem=recv_sem,
            device_id=where, device_id_type=BY_ID,
        )

    barrier = pltpu.get_barrier_semaphore()
    lines = (rows_from, rows_to, *zl_peers, *x_peers, *y_peers, twin)
    for where in lines:
        signal(barrier, where)

    @pl.when(half == 0)
    def _():
        signal(barrier, opposite)

    loads = [
        pltpu.make_async_copy(ylm_hbm, ylm, local_sem.at[0]),
        pltpu.make_async_copy(order_hbm, order_ref, local_sem.at[3]),
        pltpu.make_async_copy(cont_hbm, cont, local_sem.at[1]),
        pltpu.make_async_copy(bound_hbm, bound.at[ang], local_sem.at[2]),
        pltpu.make_async_copy(weight_hbm, weight_ref, local_sem.at[4]),
    ]
    load_ylm, load_order, load_cont, load_bound, load_weight = loads
    for load in loads:
        load.start()
    pl.semaphore_wait(barrier, len(lines) + half)

    quarter_to = piece_of(to_x, lax.div(z_other, HALF), lax.rem(z_other, HALF), y, 1 - core)[1]
    rows = send(
        ylm_hbm.at[pl.ds(pl.multiple_of(quarter_to * PIECE, PIECE), PIECE)],
        ys, out_sem.at[0], f_recv, rows_to,
    )
    rows.start()
    mine_across = send(bound_hbm, bound.at[ang], out_sem.at[1], a_recv.at[0], opposite)

    @pl.when(half == 1)
    def _():
        signal(answer, opposite)
        mine_across.start()

    along = [
        send(bound_hbm, bound.at[ang], out_sem.at[2], a_recv.at[1], where) for where in x_peers
    ]
    for copy in along:
        copy.start()
    for where in y_peers:
        signal(here, where)

    load_order.wait()
    order = order_ref[...]
    upper, upper_coef, lower, lower_coef = coupling_rows(order)
    orderf = order.astype(F32)
    for s in range(TOTAL // 128):
        ncol[pl.ds(s * 128, 128)] = jnp.broadcast_to(orderf[s : s + 1], (128, 128)).T
    load_ylm.wait()

    def couple(s, carry):
        here = pl.ds(pl.multiple_of(s * 128, 128), 128)
        column = ncol[here]
        blocks = []
        for t in range(TOTAL // 128):
            cut = slice(t, t + 1)
            blocks.append(
                jnp.where(
                    column == upper[cut],
                    upper_coef[cut],
                    jnp.where(column == lower[cut], lower_coef[cut], 0.0),
                ).astype(BF16)
            )
        g = jnp.concatenate(blocks, axis=1)
        z_ref[here] = lax.dot_general(
            g, ylm[...], (((1,), (1,)), ((), ())), preferred_element_type=F32
        ).astype(BF16)
        return carry

    lax.fori_loop(0, TOTAL // 128, couple, 0)
    three = bound.at[pl.ds(0, NX - 1)]
    send(three, three, out_sem.at[2], a_recv.at[1], twin).wait_recv()

    @pl.when(half == 0)
    def _():
        pl.semaphore_wait(answer, 1)
        mine_across.start()
        for d in range(1, NX):
            there = bound.at[2 * lax.rem(x + d, NX)]
            send(there, there, out_sem.at[1], a_recv.at[0], opposite).start()


    def block_of(i):
        cls, quarter = piece_of(x, half, lax.div(i, NY), lax.rem(i, NY), core)
        return cls * (RAD // ANG) + quarter

    block = block_of(spot)
    rows.wait_recv()
    mine[...] = jnp.dot(ys[...], z_ref[...], preferred_element_type=F32).astype(BF16)
    spots = RAD // NC
    pl.semaphore_wait(here, NY - 1)

    far, step = jnp.where(zl < HALF // 2, HALF - 1, 0), jnp.where(zl < HALF // 2, -1, 1)
    there = [
        ang * RAD + (far + step * k) * NY * NC + lax.rem(y + d, NY) * NC + core
        for k in range(HALF)
        for d in (2, 1, 3)
    ]
    for where in (*there[:6], *zl_peers, *there[6:]):
        send(mine, m_full.at[block], out_sem.at[3], m_recv.at[spot], where).start()
    send(mine, m_full.at[block], out_sem.at[4], relay_recv, twin).start()
    m_full[block] = mine[...]

    signal(all_here.at[0], opposite)

    @pl.when(half == 0)
    def _():
        mine_across.wait_recv()
        other = bound.at[ang + 1]
        for where in x_peers:
            send(other, other, out_sem.at[5], a_recv.at[2], where).start()

    pl.semaphore_wait(all_here.at[0], 1)
    for where in x_peers:
        signal(all_here.at[1], where)

    load_cont.wait()
    shells = weight_ref.shape[0]
    count_c = cont.shape[0] // shells
    for r in range(shells):
        for c in range(count_c // 128):
            part = cont[pl.ds(r * count_c + c * 128, 128)].astype(F32).T
            cont_t[pl.ds(r * 128, 128), pl.ds(c * 128, 128)] = part.astype(BF16)

    def pass_on(i):
        there = m_full.at[block_of(i)]
        send(there, there, out_sem.at[4], m_recv.at[i], twin).wait_recv()
        send(there, there, out_sem.at[4], relay_recv, twin).start()

    each(0, spot, pass_on)
    each(spot + 1, spots, pass_on)
    load_bound.wait()
    load_weight.wait()

    @pl.when(half == 0)
    def _():
        send(three, three, out_sem.at[5], a_recv.at[2], twin).wait()

    four = bound.at[pl.ds(0, NX)]

    @pl.when(half == 1)
    def _():
        send(four, four, out_sem.at[1], a_recv.at[0], twin).wait_recv()

    pl.semaphore_wait(all_here.at[1], NX - 1)
    signal(all_here.at[2], twin)
    bound_all = jnp.concatenate([bound[i] for i in range(ANG)], axis=1)
    half_m = m_full.at[pl.ds(0, spots)]
    send(half_m, half_m, out_sem.at[4], relay_recv, twin).wait_recv()
    pl.semaphore_wait(all_here.at[2], 1)

    operator = m_full[...].reshape(PTS * ANG, PTS)
    d = jnp.dot(bound_all, operator, preferred_element_type=F32)
    nb = d.shape[0] // shells
    weighted = [d[r * nb : (r + 1) * nb] * weight_ref[r] for r in range(shells)]
    wide = jnp.concatenate(weighted, axis=1).astype(BF16)

    def give(q, row, number):
        pltpu.make_async_remote_copy(
            src_ref=sendbufs[q].at[pl.ds(row, 1)], dst_ref=recvbuf.at[pl.ds(me, 1)],
            send_sem=end_send, recv_sem=end_recv, device_id=number, device_id_type=BY_ID,
        ).start()

    columns = []
    for dx, dy, dc in PLANE:
        there_x = lax.rem(x + dx, NX)
        there_yc = lax.rem(y + dy, NY) * NC + lax.rem(core + dc, NC)
        columns.append((there_x * 16 + there_yc, there_x * x_step + there_yc))
    for q in range(HALF):
        terms = jnp.dot(
            wide, cont_t[:, pl.ds(q * 128, 128)], preferred_element_type=F32
        )
        sendbufs[q][...] = turned(terms)
        for row, number in columns:
            give(q, row, number + q * NY * NC)
    for q in range(HALF):
        for row, number in columns:
            give(q, row + 8, number + (q + HALF) * NY * NC)
    own_yc = y * NC + core
    for there in range(NZ):
        q, row = there % HALF, x * 16 + there // HALF * 8 + own_yc

        @pl.when(z != there)
        def _():
            give(q, row, x * x_step + there * NY * NC + own_yc)

        @pl.when(z == there)
        def _():
            pltpu.make_async_copy(
                sendbufs[q].at[pl.ds(row, 1)], recvbuf.at[pl.ds(me, 1)], end_recv
            ).start()

    rows.wait_send()

    @pl.when(half == 0)
    def _():
        send(four, four, out_sem.at[1], a_recv.at[0], twin).wait_send()

    @pl.when(half == 1)
    def _():
        mine_across.wait_send()

    send(three, three, out_sem.at[2], a_recv.at[1], twin).wait_send()
    own_m = m_full.at[pl.ds(0, spots - 1)]
    send(own_m, own_m, out_sem.at[3], relay_recv, twin).wait_send()
    send(half_m, half_m, out_sem.at[4], relay_recv, twin).wait_send()
    pltpu.make_async_copy(recvbuf, recvbuf, end_recv).wait()
    row = jnp.sum(recvbuf[...], axis=0, keepdims=True)
    wide_row = jnp.broadcast_to(row, (8, 128))
    at = lax.broadcasted_iota(jnp.int32, (8, 128), 0)
    spread = wide_row
    for j in range(1, 8):
        spread = jnp.where(at == j, pltpu.roll(wide_row, 128 - 16 * j, 1), spread)
    out_ref[...] = spread[:, : out_ref.shape[1]]
    sent = recvbuf.at[pl.ds(0, ANG * RAD - 1)]
    pltpu.make_async_copy(sent, sent, end_send).wait()


def shards(psi_bound, psi_cont, ylm, radial_weight, order):
    shells, nb, points = psi_bound.shape
    count = psi_cont.shape[1]
    any_space = pl.BlockSpec(memory_space=pl.ANY)
    dma = pltpu.SemaphoreType.DMA
    return pl.pallas_call(
        kernel,
        out_shape=jax.ShapeDtypeStruct((nb // ANG, count // RAD), F32),
        in_specs=[
            any_space,
            any_space,
            any_space,
            any_space,
            any_space,
        ],
        out_specs=pl.BlockSpec(memory_space=pltpu.VMEM),
        scratch_shapes=[
            pltpu.VMEM((ANG, shells * nb, points), BF16),
            pltpu.VMEM((shells * count, points), BF16),
            pltpu.VMEM((points, TOTAL), BF16),
            pltpu.VMEM((8, TOTAL // 8), jnp.int32),
            pltpu.SMEM((shells,), F32),
            pltpu.VMEM((PIECE, TOTAL), BF16),
            pltpu.VMEM((TOTAL, 128), F32),
            pltpu.VMEM((TOTAL, points), BF16),
            pltpu.VMEM((PIECE, points), BF16),
            pltpu.VMEM((RAD, PIECE, points), BF16),
            pltpu.VMEM((shells * points, count), BF16),
            *[pltpu.VMEM((64, 128), F32)] * HALF,
            pltpu.VMEM((ANG * RAD, 128), F32),
            dma((5,)),
            dma((6,)),
            dma((3,)),
            dma,
            dma((RAD // NC,)),
            dma,
            dma,
            dma,
            pltpu.SemaphoreType.REGULAR,
            pltpu.SemaphoreType.REGULAR,
            pltpu.SemaphoreType.REGULAR((3,)),
        ],
        compiler_params=pltpu.CompilerParams(collective_id=0, has_side_effects=True),
        name="dipole",
    )(
        psi_bound.reshape(shells * nb, points),
        psi_cont.reshape(shells * count, points),
        ylm,
        radial_weight,
        order.reshape(8, TOTAL // 8),
    )


def solution(mesh):
    return jax.shard_map(
        shards,
        mesh=mesh,
        in_specs=(P("rad", None, "ang"), P("rad", None, "ang"), P("ang", None), P("rad"), P()),
        out_specs=P("ang", "rad"),
        check_vma=False,
    )
```

```python
import functools

import jax
import jax.numpy as jnp
from jax import lax
from jax.experimental import pallas as pl
from jax.experimental.pallas import tpu as pltpu
from jax.sharding import PartitionSpec as P

LMAX = 31
F32, BF16 = jnp.float32, jnp.bfloat16
NX, NY, NZ, NC, HALF = 4, 4, 8, 2, 4
ANG, RAD = 8, 32
PTS, TOTAL = 128, 1024
PIECE = PTS * ANG // RAD


def ring(d, n):
    return min(d, n - d)


PLANE = sorted(
    ((dx, dy, dc) for dx in range(NX) for dy in range(NY) for dc in range(NC) if (dx, dy, dc) != (0, 0, 0)),
    key=lambda o: -(ring(o[0], NX) + ring(o[1], NY)),
)
FAR = 4
BY_ID = pl.DeviceIdType.LOGICAL


def device(place):
    x, y, z, core = place
    return x * (ANG * RAD // NX) + z * (NY * NC) + y * NC + core


def piece_of(x, half, zl, y, core):
    edge = (zl == 0) | (zl == HALF - 1)
    other = jnp.where(edge, 1 - half, half)
    pair = jnp.where(edge, lax.div(zl, HALF - 1), zl - 1)
    return lax.rem(x - y + 2 + NX, NX) * 2 + other, pair * 2 + core


def coupling_rows(order):
    degree = jnp.zeros(order.shape, jnp.int32)
    for edge in range(1, LMAX + 1):
        degree = degree + (order >= edge * edge).astype(jnp.int32)
    m = order - degree * degree - degree
    lf, mf = degree.astype(F32), m.astype(F32)
    upper = jnp.where(degree + 1 <= LMAX, order + 2 * degree + 2, -1)
    upper_num = (lf + 1.0) * (lf + 1.0) - mf * mf
    upper_coef = jnp.sqrt(jnp.maximum(upper_num, 0.0) / ((2.0 * lf + 1.0) * (2.0 * lf + 3.0)))
    lower = jnp.where(degree - 1 >= jnp.abs(m), order - 2 * degree, -1)
    lower_num = lf * lf - mf * mf
    lower_den = jnp.maximum((2.0 * lf - 1.0) * (2.0 * lf + 1.0), 1.0)
    lower_coef = jnp.sqrt(jnp.maximum(lower_num, 0.0) / lower_den)
    return upper.astype(F32), upper_coef, lower.astype(F32), lower_coef


def turned(block):
    rows, lanes = block.shape
    row = lax.broadcasted_iota(jnp.int32, block.shape, 0)
    group = lax.broadcasted_iota(jnp.int32, block.shape, 1) // 16
    for s in (1, 2, 4):
        below = pltpu.roll(pltpu.roll(block, rows - s, 0), 16 * s, 1)
        above = pltpu.roll(pltpu.roll(block, s, 0), lanes - 16 * s, 1)
        low_row, low_group = (row & s) == 0, (group & s) == 0
        block = jnp.where(
            low_row == low_group, block, jnp.where(low_row, below, above)
        )
    return block


def kernel(
    bound_hbm, cont_hbm, ylm_hbm, weight_hbm, order_hbm, out_ref,
    bound, cont, ylm, order_ref, weight_ref, ys, ncol, z_ref, mine, m_full, cont_t, *rest
):
    sendbufs, (recvbuf, *semaphores) = rest[:HALF], rest[HALF:]
    local_sem, out_sem, a_recv, f_recv, m_recv, relay_recv, end_send, end_recv, *signals = semaphores
    here, both, answer, all_here = signals
    ang, rad = lax.axis_index("ang"), lax.axis_index("rad")
    x, half, core, spot = lax.div(ang, 2), lax.rem(ang, 2), lax.rem(rad, NC), lax.div(rad, NC)
    zl, y = lax.div(spot, NY), lax.rem(spot, NY)
    z = half * HALF + zl
    me = ang * RAD + rad
    x_step = ANG * RAD // NX
    x_peers = [me + (lax.rem(x + d, NX) - x) * x_step for d in (2, 1, 3)]
    opposite = me + RAD - 2 * RAD * half
    twin = me + 1 - 2 * core
    first_spot = me - NC * spot
    edge = (zl == 0) | (zl == HALF - 1)
    z_other = jnp.where(edge, NZ - 1 - z, z)
    to_x, from_x = lax.rem(x + y + 2, NX), lax.rem(x - y + 2 + NX, NX)
    rows_to, rows_from = (device((i, y, z_other, 1 - core)) for i in (to_x, from_x))
    y_peers = [me + (lax.rem(y + d, NY) - y) * NC for d in (2, 1, 3)]
    zl_peers = [me + (lax.rem(zl + d, HALF) - zl) * NY * NC for d in (2, 1, 3)]

    def signal(semaphore, where):
        pl.semaphore_signal(semaphore, inc=1, device_id=where, device_id_type=BY_ID)

    def each(start, end, act):
        def body(i, carry):
            act(i)
            return carry

        lax.fori_loop(start, end, body, 0)

    def send(src, dst, send_sem, recv_sem, where):
        return pltpu.make_async_remote_copy(
            src_ref=src, dst_ref=dst, send_sem=send_sem, recv_sem=recv_sem,
            device_id=where, device_id_type=BY_ID,
        )

    barrier = pltpu.get_barrier_semaphore()
    lines = (rows_from, rows_to, *zl_peers, *x_peers, *y_peers, twin)
    for where in lines:
        signal(barrier, where)

    @pl.when(half == 0)
    def _():
        signal(barrier, opposite)

    loads = [
        pltpu.make_async_copy(ylm_hbm, ylm, local_sem.at[0]),
        pltpu.make_async_copy(order_hbm, order_ref, local_sem.at[3]),
        pltpu.make_async_copy(cont_hbm, cont, local_sem.at[1]),
        pltpu.make_async_copy(bound_hbm, bound.at[ang], local_sem.at[2]),
        pltpu.make_async_copy(weight_hbm, weight_ref, local_sem.at[4]),
    ]
    load_ylm, load_order, load_cont, load_bound, load_weight = loads
    for load in loads:
        load.start()
    pl.semaphore_wait(barrier, len(lines) + half)

    quarter_to = piece_of(to_x, lax.div(z_other, HALF), lax.rem(z_other, HALF), y, 1 - core)[1]
    rows = send(
        ylm_hbm.at[pl.ds(pl.multiple_of(quarter_to * PIECE, PIECE), PIECE)],
        ys, out_sem.at[0], f_recv, rows_to,
    )
    rows.start()

    @pl.when(half == 1)
    def _():
        signal(answer, opposite)

    for where in y_peers:
        signal(here, where)

    load_order.wait()
    order = order_ref[...]
    upper, upper_coef, lower, lower_coef = coupling_rows(order)
    orderf = order.astype(F32)
    for s in range(TOTAL // 128):
        ncol[pl.ds(s * 128, 128)] = jnp.broadcast_to(orderf[s : s + 1], (128, 128)).T
    load_ylm.wait()

    def couple(s, carry):
        here = pl.ds(pl.multiple_of(s * 128, 128), 128)
        column = ncol[here]
        blocks = []
        for t in range(TOTAL // 128):
            cut = slice(t, t + 1)
            blocks.append(
                jnp.where(
                    column == upper[cut],
                    upper_coef[cut],
                    jnp.where(column == lower[cut], lower_coef[cut], 0.0),
                ).astype(BF16)
            )
        g = jnp.concatenate(blocks, axis=1)
        z_ref[here] = lax.dot_general(
            g, ylm[...], (((1,), (1,)), ((), ())), preferred_element_type=F32
        ).astype(BF16)
        return carry

    lax.fori_loop(0, TOTAL // 128, couple, 0)
    for where in x_peers:
        send(bound_hbm, bound.at[ang], out_sem.at[2], a_recv.at[1], where).start()
    across = send(bound_hbm, bound.at[ang], out_sem.at[1], a_recv.at[0], opposite)

    @pl.when(half == 0)
    def _():
        pl.semaphore_wait(answer, 1)

    across.start()
    pl.semaphore_wait(here, NY - 1)
    signal(both, twin)

    def block_of(i):
        cls, quarter = piece_of(x, half, lax.div(i, NY), lax.rem(i, NY), core)
        return cls * (RAD // ANG) + quarter

    block = block_of(spot)
    rows.wait_recv()
    mine[...] = jnp.dot(ys[...], z_ref[...], preferred_element_type=F32).astype(BF16)
    spots = RAD // NC
    pl.semaphore_wait(both, 1)

    far, step = jnp.where(zl < HALF // 2, HALF - 1, 0), jnp.where(zl < HALF // 2, -1, 1)
    flip = 1 - 2 * core
    there = [(far + step * k, d) for k in range(HALF) for d in (2, 1, 3)]

    def give_piece(where):
        send(mine, m_full.at[block], out_sem.at[3], m_recv.at[spot], where).start()

    def give_far_piece(zl_there, d):
        where = ang * RAD + zl_there * NY * NC + lax.rem(y + d, NY) * NC + core
        give_piece(where)

        @pl.when(jnp.abs(zl_there - zl) + ring(d, NY) >= FAR)
        def _():
            send(mine, m_full.at[block], out_sem.at[4], relay_recv, where + flip).start()

    for zl_there, d in there[:6]:
        give_far_piece(zl_there, d)
    for where in zl_peers:
        give_piece(where)
    for zl_there, d in there[6:]:
        give_far_piece(zl_there, d)
    send(mine, m_full.at[block], out_sem.at[4], relay_recv, twin).start()
    m_full[block] = mine[...]

    signal(all_here.at[0], opposite)
    across.wait_recv()
    other = bound.at[ang + 1 - 2 * half]
    for where in x_peers:
        send(other, other, out_sem.at[5], a_recv.at[2], where).start()
    pl.semaphore_wait(all_here.at[0], 1)
    for where in x_peers:
        signal(all_here.at[1], where)

    load_cont.wait()
    shells = weight_ref.shape[0]
    count_c = cont.shape[0] // shells
    for r in range(shells):
        for c in range(count_c // 128):
            part = cont[pl.ds(r * count_c + c * 128, 128)].astype(F32).T
            cont_t[pl.ds(r * 128, 128), pl.ds(c * 128, 128)] = part.astype(BF16)

    def pass_on(i):
        there = m_full.at[block_of(i)]
        send(there, there, out_sem.at[4], m_recv.at[i], twin).wait_recv()
        dy = jnp.abs(lax.rem(i, NY) - y)

        @pl.when(jnp.abs(lax.div(i, NY) - zl) + jnp.minimum(dy, NY - dy) < FAR)
        def _():
            send(there, there, out_sem.at[4], relay_recv, twin).start()

    each(0, spot, pass_on)
    each(spot + 1, spots, pass_on)
    load_bound.wait()
    load_weight.wait()
    three = bound.at[pl.ds(0, NX - 1)]
    for i in (1, 2):
        send(three, three, out_sem.at[2], a_recv.at[i], twin).wait_recv()
    pl.semaphore_wait(all_here.at[1], NX - 1)
    signal(all_here.at[2], twin)
    bound_all = jnp.concatenate([bound[i] for i in range(ANG)], axis=1)
    half_m = m_full.at[pl.ds(0, spots)]
    send(half_m, half_m, out_sem.at[4], relay_recv, twin).wait_recv()
    pl.semaphore_wait(all_here.at[2], 1)

    operator = m_full[...].reshape(PTS * ANG, PTS)
    d = jnp.dot(bound_all, operator, preferred_element_type=F32)
    nb = d.shape[0] // shells
    weighted = [d[r * nb : (r + 1) * nb] * weight_ref[r] for r in range(shells)]
    wide = jnp.concatenate(weighted, axis=1).astype(BF16)

    def give(q, row, number):
        pltpu.make_async_remote_copy(
            src_ref=sendbufs[q].at[pl.ds(row, 1)], dst_ref=recvbuf.at[pl.ds(me, 1)],
            send_sem=end_send, recv_sem=end_recv, device_id=number, device_id_type=BY_ID,
        ).start()

    columns = []
    for dx, dy, dc in PLANE:
        there_x = lax.rem(x + dx, NX)
        there_yc = lax.rem(y + dy, NY) * NC + lax.rem(core + dc, NC)
        columns.append((there_x * 16 + there_yc, there_x * x_step + there_yc))
    for q in range(HALF):
        terms = jnp.dot(
            wide, cont_t[:, pl.ds(q * 128, 128)], preferred_element_type=F32
        )
        sendbufs[q][...] = turned(terms)
        for row, number in columns:
            give(q, row, number + q * NY * NC)
    for q in range(HALF):
        for row, number in columns:
            give(q, row + 8, number + (q + HALF) * NY * NC)
    own_yc = y * NC + core
    for there in range(NZ):
        q, row = there % HALF, x * 16 + there // HALF * 8 + own_yc

        @pl.when(z != there)
        def _():
            give(q, row, x * x_step + there * NY * NC + own_yc)

        @pl.when(z == there)
        def _():
            pltpu.make_async_copy(
                sendbufs[q].at[pl.ds(row, 1)], recvbuf.at[pl.ds(me, 1)], end_recv
            ).start()

    rows.wait_send()
    across.wait_send()
    for i in (2, 5):
        send(three, three, out_sem.at[i], a_recv.at[1], twin).wait_send()
    own_m = m_full.at[pl.ds(0, spots - 1)]
    send(own_m, own_m, out_sem.at[3], relay_recv, twin).wait_send()
    send(half_m, half_m, out_sem.at[4], relay_recv, twin).wait_send()
    pltpu.make_async_copy(recvbuf, recvbuf, end_recv).wait()
    row = jnp.sum(recvbuf[...], axis=0, keepdims=True)
    wide_row = jnp.broadcast_to(row, (8, 128))
    at = lax.broadcasted_iota(jnp.int32, (8, 128), 0)
    spread = wide_row
    for j in range(1, 8):
        spread = jnp.where(at == j, pltpu.roll(wide_row, 128 - 16 * j, 1), spread)
    out_ref[...] = spread[:, : out_ref.shape[1]]
    sent = recvbuf.at[pl.ds(0, ANG * RAD - 1)]
    pltpu.make_async_copy(sent, sent, end_send).wait()


def shards(psi_bound, psi_cont, ylm, radial_weight, order):
    shells, nb, points = psi_bound.shape
    count = psi_cont.shape[1]
    any_space = pl.BlockSpec(memory_space=pl.ANY)
    dma = pltpu.SemaphoreType.DMA
    return pl.pallas_call(
        kernel,
        out_shape=jax.ShapeDtypeStruct((nb // ANG, count // RAD), F32),
        in_specs=[
            any_space,
            any_space,
            any_space,
            any_space,
            any_space,
        ],
        out_specs=pl.BlockSpec(memory_space=pltpu.VMEM),
        scratch_shapes=[
            pltpu.VMEM((ANG, shells * nb, points), BF16),
            pltpu.VMEM((shells * count, points), BF16),
            pltpu.VMEM((points, TOTAL), BF16),
            pltpu.VMEM((8, TOTAL // 8), jnp.int32),
            pltpu.SMEM((shells,), F32),
            pltpu.VMEM((PIECE, TOTAL), BF16),
            pltpu.VMEM((TOTAL, 128), F32),
            pltpu.VMEM((TOTAL, points), BF16),
            pltpu.VMEM((PIECE, points), BF16),
            pltpu.VMEM((RAD, PIECE, points), BF16),
            pltpu.VMEM((shells * points, count), BF16),
            *[pltpu.VMEM((64, 128), F32)] * HALF,
            pltpu.VMEM((ANG * RAD, 128), F32),
            dma((5,)),
            dma((6,)),
            dma((3,)),
            dma,
            dma((RAD // NC,)),
            dma,
            dma,
            dma,
            *[pltpu.SemaphoreType.REGULAR] * 3,
            pltpu.SemaphoreType.REGULAR((3,)),
        ],
        compiler_params=pltpu.CompilerParams(collective_id=0, has_side_effects=True),
        name="dipole",
    )(
        psi_bound.reshape(shells * nb, points),
        psi_cont.reshape(shells * count, points),
        ylm,
        radial_weight,
        order.reshape(8, TOTAL // 8),
    )


def solution(mesh):
    return jax.shard_map(
        shards,
        mesh=mesh,
        in_specs=(P("rad", None, "ang"), P("rad", None, "ang"), P("ang", None), P("rad"), P()),
        out_specs=P("ang", "rad"),
        check_vma=False,
    )
```

```python
import functools

import jax
import jax.numpy as jnp
from jax import lax
from jax.experimental import pallas as pl
from jax.experimental.pallas import tpu as pltpu
from jax.sharding import PartitionSpec as P

LMAX = 31
F32, BF16 = jnp.float32, jnp.bfloat16
NX, NY, NZ, NC, HALF = 4, 4, 8, 2, 4
ANG, RAD = 8, 32
PTS, TOTAL = 128, 1024
PIECE = PTS * ANG // RAD


def ring(d, n):
    return min(d, n - d)


PLANE = sorted(
    ((dx, dy, dc) for dx in range(NX) for dy in range(NY) for dc in range(NC) if (dx, dy, dc) != (0, 0, 0)),
    key=lambda o: -(ring(o[0], NX) + ring(o[1], NY)),
)
NEXT = 2
BY_ID = pl.DeviceIdType.LOGICAL


def device(place):
    x, y, z, core = place
    return x * (ANG * RAD // NX) + z * (NY * NC) + y * NC + core


def piece_of(x, half, zl, y, core):
    edge = (zl == 0) | (zl == HALF - 1)
    other = jnp.where(edge, 1 - half, half)
    pair = jnp.where(edge, lax.div(zl, HALF - 1), zl - 1)
    return lax.rem(x - y + 2 + NX, NX) * 2 + other, pair * 2 + core


def coupling_rows(order):
    degree = jnp.zeros(order.shape, jnp.int32)
    for edge in range(1, LMAX + 1):
        degree = degree + (order >= edge * edge).astype(jnp.int32)
    m = order - degree * degree - degree
    lf, mf = degree.astype(F32), m.astype(F32)
    upper = jnp.where(degree + 1 <= LMAX, order + 2 * degree + 2, -1)
    upper_num = (lf + 1.0) * (lf + 1.0) - mf * mf
    upper_coef = jnp.sqrt(jnp.maximum(upper_num, 0.0) / ((2.0 * lf + 1.0) * (2.0 * lf + 3.0)))
    lower = jnp.where(degree - 1 >= jnp.abs(m), order - 2 * degree, -1)
    lower_num = lf * lf - mf * mf
    lower_den = jnp.maximum((2.0 * lf - 1.0) * (2.0 * lf + 1.0), 1.0)
    lower_coef = jnp.sqrt(jnp.maximum(lower_num, 0.0) / lower_den)
    return upper.astype(F32), upper_coef, lower.astype(F32), lower_coef


def turned(block):
    rows, lanes = block.shape
    row = lax.broadcasted_iota(jnp.int32, block.shape, 0)
    group = lax.broadcasted_iota(jnp.int32, block.shape, 1) // 16
    for s in (1, 2, 4):
        below = pltpu.roll(pltpu.roll(block, rows - s, 0), 16 * s, 1)
        above = pltpu.roll(pltpu.roll(block, s, 0), lanes - 16 * s, 1)
        low_row, low_group = (row & s) == 0, (group & s) == 0
        block = jnp.where(
            low_row == low_group, block, jnp.where(low_row, below, above)
        )
    return block


def kernel(
    bound_hbm, cont_hbm, ylm_hbm, weight_hbm, order_hbm, out_ref,
    bound, cont, ylm, order_ref, weight_ref, ys, ncol, z_ref, mine, m_full, cont_t, *rest
):
    sendbufs, (recvbuf, *semaphores) = rest[:HALF], rest[HALF:]
    local_sem, out_sem, a_recv, f_recv, m_recv, relay_recv, end_send, end_recv, *signals = semaphores
    here, both, answer, all_here = signals
    ang, rad = lax.axis_index("ang"), lax.axis_index("rad")
    x, half, core, spot = lax.div(ang, 2), lax.rem(ang, 2), lax.rem(rad, NC), lax.div(rad, NC)
    zl, y = lax.div(spot, NY), lax.rem(spot, NY)
    z = half * HALF + zl
    me = ang * RAD + rad
    x_step = ANG * RAD // NX
    x_peers = [me + (lax.rem(x + d, NX) - x) * x_step for d in (2, 1, 3)]
    opposite = me + RAD - 2 * RAD * half
    twin = me + 1 - 2 * core
    first_spot = me - NC * spot
    edge = (zl == 0) | (zl == HALF - 1)
    z_other = jnp.where(edge, NZ - 1 - z, z)
    to_x, from_x = lax.rem(x + y + 2, NX), lax.rem(x - y + 2 + NX, NX)
    rows_to, rows_from = (device((i, y, z_other, 1 - core)) for i in (to_x, from_x))
    y_peers = [me + (lax.rem(y + d, NY) - y) * NC for d in (2, 1, 3)]
    zl_peers = [me + (lax.rem(zl + d, HALF) - zl) * NY * NC for d in (2, 1, 3)]

    def signal(semaphore, where):
        pl.semaphore_signal(semaphore, inc=1, device_id=where, device_id_type=BY_ID)

    def each(start, end, act):
        def body(i, carry):
            act(i)
            return carry

        lax.fori_loop(start, end, body, 0)

    def send(src, dst, send_sem, recv_sem, where):
        return pltpu.make_async_remote_copy(
            src_ref=src, dst_ref=dst, send_sem=send_sem, recv_sem=recv_sem,
            device_id=where, device_id_type=BY_ID,
        )

    barrier = pltpu.get_barrier_semaphore()
    lines = (rows_from, rows_to, *zl_peers, *x_peers, *y_peers, twin)
    for where in lines:
        signal(barrier, where)

    @pl.when(half == 0)
    def _():
        signal(barrier, opposite)

    loads = [
        pltpu.make_async_copy(ylm_hbm, ylm, local_sem.at[0]),
        pltpu.make_async_copy(order_hbm, order_ref, local_sem.at[3]),
        pltpu.make_async_copy(cont_hbm, cont, local_sem.at[1]),
        pltpu.make_async_copy(bound_hbm, bound.at[ang], local_sem.at[2]),
        pltpu.make_async_copy(weight_hbm, weight_ref, local_sem.at[4]),
    ]
    load_ylm, load_order, load_cont, load_bound, load_weight = loads
    for load in loads:
        load.start()
    pl.semaphore_wait(barrier, len(lines) + half)

    quarter_to = piece_of(to_x, lax.div(z_other, HALF), lax.rem(z_other, HALF), y, 1 - core)[1]
    rows = send(
        ylm.at[pl.ds(pl.multiple_of(quarter_to * PIECE, PIECE), PIECE)],
        ys, out_sem.at[0], f_recv, rows_to,
    )
    load_ylm.wait()
    rows.start()

    @pl.when(half == 1)
    def _():
        signal(answer, opposite)

    for where in y_peers:
        signal(here, where)

    load_order.wait()
    order = order_ref[...]
    upper, upper_coef, lower, lower_coef = coupling_rows(order)
    orderf = order.astype(F32)
    for s in range(TOTAL // 128):
        ncol[pl.ds(s * 128, 128)] = jnp.broadcast_to(orderf[s : s + 1], (128, 128)).T

    def couple(s, carry):
        here = pl.ds(pl.multiple_of(s * 128, 128), 128)
        column = ncol[here]
        blocks = []
        for t in range(TOTAL // 128):
            cut = slice(t, t + 1)
            blocks.append(
                jnp.where(
                    column == upper[cut],
                    upper_coef[cut],
                    jnp.where(column == lower[cut], lower_coef[cut], 0.0),
                ).astype(BF16)
            )
        g = jnp.concatenate(blocks, axis=1)
        z_ref[here] = lax.dot_general(
            g, ylm[...], (((1,), (1,)), ((), ())), preferred_element_type=F32
        ).astype(BF16)
        return carry

    lax.fori_loop(0, TOTAL // 128, couple, 0)
    for where in x_peers:
        send(bound_hbm, bound.at[ang], out_sem.at[2], a_recv.at[1], where).start()
    across = send(bound_hbm, bound.at[ang], out_sem.at[1], a_recv.at[0], opposite)

    @pl.when(half == 0)
    def _():
        pl.semaphore_wait(answer, 1)

    across.start()
    load_cont.wait()
    shells = weight_ref.shape[0]
    count_c = cont.shape[0] // shells
    for r in range(shells):
        for c in range(count_c // 128):
            part = cont[pl.ds(r * count_c + c * 128, 128)].astype(F32).T
            cont_t[pl.ds(r * 128, 128), pl.ds(c * 128, 128)] = part.astype(BF16)

    pl.semaphore_wait(here, NY - 1)
    signal(both, twin)

    def block_of(i):
        cls, quarter = piece_of(x, half, lax.div(i, NY), lax.rem(i, NY), core)
        return cls * (RAD // ANG) + quarter

    block = block_of(spot)
    rows.wait_recv()
    mine[...] = jnp.dot(ys[...], z_ref[...], preferred_element_type=F32).astype(BF16)
    spots = RAD // NC
    pl.semaphore_wait(both, 1)

    far, step = jnp.where(zl < HALF // 2, HALF - 1, 0), jnp.where(zl < HALF // 2, -1, 1)

    def give_pieces(own_k, both_from):
        for k in range(HALF):
            for d in (2, 1, 3, 0):
                if (k, d) == (own_k, 0):
                    continue
                where = ang * RAD + (far + step * k) * NY * NC + lax.rem(y + d, NY) * NC + core
                send(mine, m_full.at[block], out_sem.at[3], m_recv.at[spot], where).start()
                if both_from and own_k - k + ring(d, NY) >= both_from:
                    where = where + 1 - 2 * core
                    send(mine, m_full.at[block], out_sem.at[6], relay_recv, where).start()

    @pl.when(edge)
    def _():
        give_pieces(HALF - 1, NEXT)

    @pl.when(jnp.logical_not(edge))
    def _():
        give_pieces(HALF // 2, 0)

    send(mine, m_full.at[block], out_sem.at[4], relay_recv, twin).start()
    m_full[block] = mine[...]

    signal(all_here.at[0], opposite)
    across.wait_recv()
    other = bound.at[ang + 1 - 2 * half]
    for where in x_peers:
        send(other, other, out_sem.at[5], a_recv.at[2], where).start()
    pl.semaphore_wait(all_here.at[0], 1)
    for where in x_peers:
        signal(all_here.at[1], where)

    def pass_on(start, end, limit):
        def act(i):
            @pl.when(i != spot)
            def _():
                there = m_full.at[block_of(i)]
                send(there, there, out_sem.at[4], m_recv.at[i], twin).wait_recv()
                dy = jnp.abs(lax.rem(i, NY) - y)

                @pl.when(jnp.abs(lax.div(i, NY) - zl) + jnp.minimum(dy, NY - dy) < limit)
                def _():
                    send(there, there, out_sem.at[4], relay_recv, twin).start()

        each(start, end, act)

    pass_on(NY, spots - NY, spots)
    pass_on(0, NY, NEXT)
    pass_on(spots - NY, spots, NEXT)
    load_bound.wait()
    load_weight.wait()
    three = bound.at[pl.ds(0, NX - 1)]
    for i in (1, 2):
        send(three, three, out_sem.at[2], a_recv.at[i], twin).wait_recv()
    pl.semaphore_wait(all_here.at[1], NX - 1)
    signal(all_here.at[2], twin)
    bound_all = jnp.concatenate([bound[i] for i in range(ANG)], axis=1)
    half_m = m_full.at[pl.ds(0, spots)]
    send(half_m, half_m, out_sem.at[4], relay_recv, twin).wait_recv()
    pl.semaphore_wait(all_here.at[2], 1)

    operator = m_full[...].reshape(PTS * ANG, PTS)
    d = jnp.dot(bound_all, operator, preferred_element_type=F32)
    nb = d.shape[0] // shells
    weighted = [d[r * nb : (r + 1) * nb] * weight_ref[r] for r in range(shells)]
    wide = jnp.concatenate(weighted, axis=1).astype(BF16)

    def give(q, row, number):
        pltpu.make_async_remote_copy(
            src_ref=sendbufs[q].at[pl.ds(row, 1)], dst_ref=recvbuf.at[pl.ds(me, 1)],
            send_sem=end_send, recv_sem=end_recv, device_id=number, device_id_type=BY_ID,
        ).start()

    columns = []
    for dx, dy, dc in PLANE:
        there_x = lax.rem(x + dx, NX)
        there_yc = lax.rem(y + dy, NY) * NC + lax.rem(core + dc, NC)
        columns.append((there_x * 16 + there_yc, there_x * x_step + there_yc))
    for q in range(HALF):
        terms = jnp.dot(
            wide, cont_t[:, pl.ds(q * 128, 128)], preferred_element_type=F32
        )
        sendbufs[q][...] = turned(terms)
        for row, number in columns:
            give(q, row, number + q * NY * NC)
    for q in range(HALF):
        for row, number in columns:
            give(q, row + 8, number + (q + HALF) * NY * NC)
    own_yc = y * NC + core
    for there in range(NZ):
        q, row = there % HALF, x * 16 + there // HALF * 8 + own_yc

        @pl.when(z != there)
        def _():
            give(q, row, x * x_step + there * NY * NC + own_yc)

        @pl.when(z == there)
        def _():
            pltpu.make_async_copy(
                sendbufs[q].at[pl.ds(row, 1)], recvbuf.at[pl.ds(me, 1)], end_recv
            ).start()

    rows.wait_send()
    across.wait_send()
    for i in (2, 5):
        send(three, three, out_sem.at[i], a_recv.at[1], twin).wait_send()
    own_m = m_full.at[pl.ds(0, spots - 1)]
    send(own_m, own_m, out_sem.at[3], relay_recv, twin).wait_send()

    def sent_pieces(i, n):
        part = m_full.at[pl.ds(0, n)]
        send(part, part, out_sem.at[i], relay_recv, twin).wait_send()

    @pl.when(edge)
    def _():
        sent_pieces(4, 11)
        sent_pieces(6, 12)

    @pl.when(jnp.logical_not(edge))
    def _():
        sent_pieces(4, 9)

    pltpu.make_async_copy(recvbuf, recvbuf, end_recv).wait()
    row = jnp.sum(recvbuf[...], axis=0, keepdims=True)
    wide_row = jnp.broadcast_to(row, (8, 128))
    at = lax.broadcasted_iota(jnp.int32, (8, 128), 0)
    spread = wide_row
    for j in range(1, 8):
        spread = jnp.where(at == j, pltpu.roll(wide_row, 128 - 16 * j, 1), spread)
    out_ref[...] = spread[:, : out_ref.shape[1]]
    sent = recvbuf.at[pl.ds(0, ANG * RAD - 1)]
    pltpu.make_async_copy(sent, sent, end_send).wait()


def shards(psi_bound, psi_cont, ylm, radial_weight, order):
    shells, nb, points = psi_bound.shape
    count = psi_cont.shape[1]
    any_space = pl.BlockSpec(memory_space=pl.ANY)
    dma = pltpu.SemaphoreType.DMA
    return pl.pallas_call(
        kernel,
        out_shape=jax.ShapeDtypeStruct((nb // ANG, count // RAD), F32),
        in_specs=[
            any_space,
            any_space,
            any_space,
            any_space,
            any_space,
        ],
        out_specs=pl.BlockSpec(memory_space=pltpu.VMEM),
        scratch_shapes=[
            pltpu.VMEM((ANG, shells * nb, points), BF16),
            pltpu.VMEM((shells * count, points), BF16),
            pltpu.VMEM((points, TOTAL), BF16),
            pltpu.VMEM((8, TOTAL // 8), jnp.int32),
            pltpu.SMEM((shells,), F32),
            pltpu.VMEM((PIECE, TOTAL), BF16),
            pltpu.VMEM((TOTAL, 128), F32),
            pltpu.VMEM((TOTAL, points), BF16),
            pltpu.VMEM((PIECE, points), BF16),
            pltpu.VMEM((RAD, PIECE, points), BF16),
            pltpu.VMEM((shells * points, count), BF16),
            *[pltpu.VMEM((64, 128), F32)] * HALF,
            pltpu.VMEM((ANG * RAD, 128), F32),
            dma((5,)),
            dma((7,)),
            dma((3,)),
            dma,
            dma((RAD // NC,)),
            dma,
            dma,
            dma,
            *[pltpu.SemaphoreType.REGULAR] * 3,
            pltpu.SemaphoreType.REGULAR((3,)),
        ],
        compiler_params=pltpu.CompilerParams(collective_id=0, has_side_effects=True),
        name="dipole",
    )(
        psi_bound.reshape(shells * nb, points),
        psi_cont.reshape(shells * count, points),
        ylm,
        radial_weight,
        order.reshape(8, TOTAL // 8),
    )


def solution(mesh):
    return jax.shard_map(
        shards,
        mesh=mesh,
        in_specs=(P("rad", None, "ang"), P("rad", None, "ang"), P("ang", None), P("rad"), P()),
        out_specs=P("ang", "rad"),
        check_vma=False,
    )
```

```python
import functools

import jax
import jax.numpy as jnp
from jax import lax
from jax.experimental import pallas as pl
from jax.experimental.pallas import tpu as pltpu
from jax.sharding import PartitionSpec as P

LMAX = 31
F32, BF16 = jnp.float32, jnp.bfloat16
NX, NY, NZ, NC, HALF = 4, 4, 8, 2, 4
ANG, RAD = 8, 32
PTS, TOTAL = 128, 1024
PIECE = PTS * ANG // RAD


def ring(d, n):
    return min(d, n - d)


PLANE = sorted(
    ((dx, dy, dc) for dx in range(NX) for dy in range(NY) for dc in range(NC) if (dx, dy, dc) != (0, 0, 0)),
    key=lambda o: -(ring(o[0], NX) + ring(o[1], NY)),
)
NEXT = 2
BY_ID = pl.DeviceIdType.LOGICAL


def device(place):
    x, y, z, core = place
    return x * (ANG * RAD // NX) + z * (NY * NC) + y * NC + core


def piece_of(x, half, zl, y, core):
    edge = (zl == 0) | (zl == HALF - 1)
    other = jnp.where(edge, 1 - half, half)
    pair = jnp.where(edge, lax.div(zl, HALF - 1), zl - 1)
    return lax.rem(x - y + 2 + NX, NX) * 2 + other, pair * 2 + core


def coupling_rows(order):
    degree = jnp.zeros(order.shape, jnp.int32)
    for edge in range(1, LMAX + 1):
        degree = degree + (order >= edge * edge).astype(jnp.int32)
    m = order - degree * degree - degree
    lf, mf = degree.astype(F32), m.astype(F32)
    upper = jnp.where(degree + 1 <= LMAX, order + 2 * degree + 2, -1)
    upper_num = (lf + 1.0) * (lf + 1.0) - mf * mf
    upper_coef = jnp.sqrt(jnp.maximum(upper_num, 0.0) / ((2.0 * lf + 1.0) * (2.0 * lf + 3.0)))
    lower = jnp.where(degree - 1 >= jnp.abs(m), order - 2 * degree, -1)
    lower_num = lf * lf - mf * mf
    lower_den = jnp.maximum((2.0 * lf - 1.0) * (2.0 * lf + 1.0), 1.0)
    lower_coef = jnp.sqrt(jnp.maximum(lower_num, 0.0) / lower_den)
    return upper.astype(F32), upper_coef, lower.astype(F32), lower_coef


def turned(block):
    rows, lanes = block.shape
    row = lax.broadcasted_iota(jnp.int32, block.shape, 0)
    group = lax.broadcasted_iota(jnp.int32, block.shape, 1) // 16
    for s in (1, 2, 4):
        below = pltpu.roll(pltpu.roll(block, rows - s, 0), 16 * s, 1)
        above = pltpu.roll(pltpu.roll(block, s, 0), lanes - 16 * s, 1)
        low_row, low_group = (row & s) == 0, (group & s) == 0
        block = jnp.where(
            low_row == low_group, block, jnp.where(low_row, below, above)
        )
    return block


def kernel(
    bound_hbm, cont_hbm, ylm_hbm, weight_hbm, order_hbm, out_ref,
    bound, cont, ylm, order_ref, weight_ref, ys, ncol, z_ref, mine, m_full, cont_t, *rest
):
    sendbufs, (recvbuf, *semaphores) = rest[:HALF], rest[HALF:]
    local_sem, out_sem, a_recv, f_recv, m_recv, relay_recv, end_send, end_recv, *signals = semaphores
    here, both, all_here = signals
    ang, rad = lax.axis_index("ang"), lax.axis_index("rad")
    x, half, core, spot = lax.div(ang, 2), lax.rem(ang, 2), lax.rem(rad, NC), lax.div(rad, NC)
    zl, y = lax.div(spot, NY), lax.rem(spot, NY)
    z = half * HALF + zl
    me = ang * RAD + rad
    x_step = ANG * RAD // NX
    x_peers = [me + (lax.rem(x + d, NX) - x) * x_step for d in (2, 1, 3)]
    opposite = me + RAD - 2 * RAD * half
    twin = me + 1 - 2 * core
    first_spot = me - NC * spot
    edge = (zl == 0) | (zl == HALF - 1)
    z_other = jnp.where(edge, NZ - 1 - z, z)
    to_x, from_x = lax.rem(x + y + 2, NX), lax.rem(x - y + 2 + NX, NX)
    rows_to, rows_from = (device((i, y, z_other, 1 - core)) for i in (to_x, from_x))
    y_peers = [me + (lax.rem(y + d, NY) - y) * NC for d in (2, 1, 3)]
    zl_peers = [me + (lax.rem(zl + d, HALF) - zl) * NY * NC for d in (2, 1, 3)]

    def signal(semaphore, where):
        pl.semaphore_signal(semaphore, inc=1, device_id=where, device_id_type=BY_ID)

    def each(start, end, act):
        def body(i, carry):
            act(i)
            return carry

        lax.fori_loop(start, end, body, 0)

    def send(src, dst, send_sem, recv_sem, where):
        return pltpu.make_async_remote_copy(
            src_ref=src, dst_ref=dst, send_sem=send_sem, recv_sem=recv_sem,
            device_id=where, device_id_type=BY_ID,
        )

    barrier = pltpu.get_barrier_semaphore()
    lines = (rows_from, opposite, rows_to, *zl_peers, *x_peers, *y_peers, twin)
    for where in lines:
        signal(barrier, where)
    loads = [
        pltpu.make_async_copy(ylm_hbm, ylm, local_sem.at[0]),
        pltpu.make_async_copy(order_hbm, order_ref, local_sem.at[3]),
        pltpu.make_async_copy(cont_hbm, cont, local_sem.at[1]),
        pltpu.make_async_copy(bound_hbm, bound.at[ang], local_sem.at[2]),
        pltpu.make_async_copy(weight_hbm, weight_ref, local_sem.at[4]),
    ]
    load_ylm, load_order, load_cont, load_bound, load_weight = loads
    for load in loads:
        load.start()
    pl.semaphore_wait(barrier, len(lines))

    quarter_to = piece_of(to_x, lax.div(z_other, HALF), lax.rem(z_other, HALF), y, 1 - core)[1]
    rows = send(
        ylm.at[pl.ds(pl.multiple_of(quarter_to * PIECE, PIECE), PIECE)],
        ys, out_sem.at[0], f_recv, rows_to,
    )
    load_ylm.wait()
    rows.start()

    across = send(bound_hbm, bound.at[ang], out_sem.at[1], a_recv.at[0], opposite)

    @pl.when(half == 0)
    def _():
        across.start()

    for where in y_peers:
        signal(here, where)

    load_order.wait()
    order = order_ref[...]
    upper, upper_coef, lower, lower_coef = coupling_rows(order)
    orderf = order.astype(F32)
    for s in range(TOTAL // 128):
        ncol[pl.ds(s * 128, 128)] = jnp.broadcast_to(orderf[s : s + 1], (128, 128)).T

    def couple(s, carry):
        here = pl.ds(pl.multiple_of(s * 128, 128), 128)
        column = ncol[here]
        blocks = []
        for t in range(TOTAL // 128):
            cut = slice(t, t + 1)
            blocks.append(
                jnp.where(
                    column == upper[cut],
                    upper_coef[cut],
                    jnp.where(column == lower[cut], lower_coef[cut], 0.0),
                ).astype(BF16)
            )
        g = jnp.concatenate(blocks, axis=1)
        z_ref[here] = lax.dot_general(
            g, ylm[...], (((1,), (1,)), ((), ())), preferred_element_type=F32
        ).astype(BF16)
        return carry

    lax.fori_loop(0, TOTAL // 128, couple, 0)
    for where in x_peers:
        send(bound_hbm, bound.at[ang], out_sem.at[2], a_recv.at[1], where).start()

    @pl.when(half == 1)
    def _():
        across.start()

    load_cont.wait()
    shells = weight_ref.shape[0]
    count_c = cont.shape[0] // shells
    for r in range(shells):
        for c in range(count_c // 128):
            part = cont[pl.ds(r * count_c + c * 128, 128)].astype(F32).T
            cont_t[pl.ds(r * 128, 128), pl.ds(c * 128, 128)] = part.astype(BF16)

    pl.semaphore_wait(here, NY - 1)
    signal(both, twin)

    def block_of(i):
        cls, quarter = piece_of(x, half, lax.div(i, NY), lax.rem(i, NY), core)
        return cls * (RAD // ANG) + quarter

    block = block_of(spot)
    rows.wait_recv()
    mine[...] = jnp.dot(ys[...], z_ref[...], preferred_element_type=F32).astype(BF16)
    spots = RAD // NC
    pl.semaphore_wait(both, 1)

    far, step = jnp.where(zl < HALF // 2, HALF - 1, 0), jnp.where(zl < HALF // 2, -1, 1)

    def give_pieces(own_k, both_from):
        for k in range(HALF):
            for d in (2, 1, 3, 0):
                if (k, d) == (own_k, 0):
                    continue
                where = ang * RAD + (far + step * k) * NY * NC + lax.rem(y + d, NY) * NC + core
                send(mine, m_full.at[block], out_sem.at[3], m_recv.at[spot], where).start()
                if both_from and own_k - k >= both_from:
                    where = where + 1 - 2 * core
                    send(mine, m_full.at[block], out_sem.at[6], relay_recv, where).start()

    @pl.when(edge)
    def _():
        give_pieces(HALF - 1, NEXT)

    @pl.when(jnp.logical_not(edge))
    def _():
        give_pieces(HALF // 2, 0)

    send(mine, m_full.at[block], out_sem.at[4], relay_recv, twin).start()
    m_full[block] = mine[...]

    signal(all_here.at[0], opposite)
    across.wait_recv()
    other = bound.at[ang + 1 - 2 * half]
    for where in x_peers:
        send(other, other, out_sem.at[5], a_recv.at[2], where).start()
    pl.semaphore_wait(all_here.at[0], 1)
    for where in x_peers:
        signal(all_here.at[1], where)

    def pass_on(start, end, limit):
        def act(i):
            @pl.when(i != spot)
            def _():
                there = m_full.at[block_of(i)]
                send(there, there, out_sem.at[4], m_recv.at[i], twin).wait_recv()

                @pl.when(jnp.abs(lax.div(i, NY) - zl) < limit)
                def _():
                    send(there, there, out_sem.at[4], relay_recv, twin).start()

        each(start, end, act)

    pass_on(NY, spots - NY, spots)
    pass_on(0, NY, NEXT)
    pass_on(spots - NY, spots, NEXT)
    load_bound.wait()
    load_weight.wait()
    three = bound.at[pl.ds(0, NX - 1)]
    for i in (1, 2):
        send(three, three, out_sem.at[2], a_recv.at[i], twin).wait_recv()
    pl.semaphore_wait(all_here.at[1], NX - 1)
    signal(all_here.at[2], twin)
    bound_all = jnp.concatenate([bound[i] for i in range(ANG)], axis=1)
    half_m = m_full.at[pl.ds(0, spots)]
    send(half_m, half_m, out_sem.at[4], relay_recv, twin).wait_recv()
    pl.semaphore_wait(all_here.at[2], 1)

    operator = m_full[...].reshape(PTS * ANG, PTS)
    d = jnp.dot(bound_all, operator, preferred_element_type=F32)
    nb = d.shape[0] // shells
    weighted = [d[r * nb : (r + 1) * nb] * weight_ref[r] for r in range(shells)]
    wide = jnp.concatenate(weighted, axis=1).astype(BF16)

    def give(q, row, number):
        pltpu.make_async_remote_copy(
            src_ref=sendbufs[q].at[pl.ds(row, 1)], dst_ref=recvbuf.at[pl.ds(me, 1)],
            send_sem=end_send, recv_sem=end_recv, device_id=number, device_id_type=BY_ID,
        ).start()

    columns = []
    for dx, dy, dc in PLANE:
        there_x = lax.rem(x + dx, NX)
        there_yc = lax.rem(y + dy, NY) * NC + lax.rem(core + dc, NC)
        columns.append((there_x * 16 + there_yc, there_x * x_step + there_yc))
    for q in range(HALF):
        terms = jnp.dot(
            wide, cont_t[:, pl.ds(q * 128, 128)], preferred_element_type=F32
        )
        sendbufs[q][...] = turned(terms)
        for row, number in columns:
            give(q, row, number + q * NY * NC)
    for q in range(HALF):
        for row, number in columns:
            give(q, row + 8, number + (q + HALF) * NY * NC)
    own_yc = y * NC + core
    for there in range(NZ):
        q, row = there % HALF, x * 16 + there // HALF * 8 + own_yc

        @pl.when(z != there)
        def _():
            give(q, row, x * x_step + there * NY * NC + own_yc)

        @pl.when(z == there)
        def _():
            pltpu.make_async_copy(
                sendbufs[q].at[pl.ds(row, 1)], recvbuf.at[pl.ds(me, 1)], end_recv
            ).start()

    rows.wait_send()
    across.wait_send()
    for i in (2, 5):
        send(three, three, out_sem.at[i], a_recv.at[1], twin).wait_send()
    own_m = m_full.at[pl.ds(0, spots - 1)]
    send(own_m, own_m, out_sem.at[3], relay_recv, twin).wait_send()

    def sent_pieces(i, n):
        part = m_full.at[pl.ds(0, n)]
        send(part, part, out_sem.at[i], relay_recv, twin).wait_send()

    sent_pieces(4, spots - NY)

    @pl.when(edge)
    def _():
        sent_pieces(6, 2 * NY)

    pltpu.make_async_copy(recvbuf, recvbuf, end_recv).wait()
    row = jnp.sum(recvbuf[...], axis=0, keepdims=True)
    wide_row = jnp.broadcast_to(row, (8, 128))
    at = lax.broadcasted_iota(jnp.int32, (8, 128), 0)
    spread = wide_row
    for j in range(1, 8):
        spread = jnp.where(at == j, pltpu.roll(wide_row, 128 - 16 * j, 1), spread)
    out_ref[...] = spread[:, : out_ref.shape[1]]
    sent = recvbuf.at[pl.ds(0, ANG * RAD - 1)]
    pltpu.make_async_copy(sent, sent, end_send).wait()


def shards(psi_bound, psi_cont, ylm, radial_weight, order):
    shells, nb, points = psi_bound.shape
    count = psi_cont.shape[1]
    any_space = pl.BlockSpec(memory_space=pl.ANY)
    dma = pltpu.SemaphoreType.DMA
    return pl.pallas_call(
        kernel,
        out_shape=jax.ShapeDtypeStruct((nb // ANG, count // RAD), F32),
        in_specs=[
            any_space,
            any_space,
            any_space,
            any_space,
            any_space,
        ],
        out_specs=pl.BlockSpec(memory_space=pltpu.VMEM),
        scratch_shapes=[
            pltpu.VMEM((ANG, shells * nb, points), BF16),
            pltpu.VMEM((shells * count, points), BF16),
            pltpu.VMEM((points, TOTAL), BF16),
            pltpu.VMEM((8, TOTAL // 8), jnp.int32),
            pltpu.SMEM((shells,), F32),
            pltpu.VMEM((PIECE, TOTAL), BF16),
            pltpu.VMEM((TOTAL, 128), F32),
            pltpu.VMEM((TOTAL, points), BF16),
            pltpu.VMEM((PIECE, points), BF16),
            pltpu.VMEM((RAD, PIECE, points), BF16),
            pltpu.VMEM((shells * points, count), BF16),
            *[pltpu.VMEM((64, 128), F32)] * HALF,
            pltpu.VMEM((ANG * RAD, 128), F32),
            dma((5,)),
            dma((7,)),
            dma((3,)),
            dma,
            dma((RAD // NC,)),
            dma,
            dma,
            dma,
            *[pltpu.SemaphoreType.REGULAR] * 2,
            pltpu.SemaphoreType.REGULAR((3,)),
        ],
        compiler_params=pltpu.CompilerParams(collective_id=0, has_side_effects=True),
        name="dipole",
    )(
        psi_bound.reshape(shells * nb, points),
        psi_cont.reshape(shells * count, points),
        ylm,
        radial_weight,
        order.reshape(8, TOTAL // 8),
    )


def solution(mesh):
    return jax.shard_map(
        shards,
        mesh=mesh,
        in_specs=(P("rad", None, "ang"), P("rad", None, "ang"), P("ang", None), P("rad"), P()),
        out_specs=P("ang", "rad"),
        check_vma=False,
    )
```

```python
import functools

import jax
import jax.numpy as jnp
from jax import lax
from jax.experimental import pallas as pl
from jax.experimental.pallas import tpu as pltpu
from jax.sharding import PartitionSpec as P

LMAX = 31
F32, BF16 = jnp.float32, jnp.bfloat16
NX, NY, NZ, NC, HALF = 4, 4, 8, 2, 4
ANG, RAD = 8, 32
PTS, TOTAL = 128, 1024
PIECE = PTS * ANG // RAD


def ring(d, n):
    return min(d, n - d)


PLANE = sorted(
    ((dx, dy, dc) for dx in range(NX) for dy in range(NY) for dc in range(NC) if (dx, dy, dc) != (0, 0, 0)),
    key=lambda o: -(ring(o[0], NX) + ring(o[1], NY)),
)
NEXT = 3
BY_ID = pl.DeviceIdType.LOGICAL


def device(place):
    x, y, z, core = place
    return x * (ANG * RAD // NX) + z * (NY * NC) + y * NC + core


def piece_of(x, half, zl, y, core):
    edge = (zl == 0) | (zl == HALF - 1)
    other = jnp.where(edge, 1 - half, half)
    pair = jnp.where(edge, lax.div(zl, HALF - 1), zl - 1)
    return lax.rem(x - y + 2 + NX, NX) * 2 + other, pair * 2 + core


def coupling_rows(order):
    degree = jnp.zeros(order.shape, jnp.int32)
    for edge in range(1, LMAX + 1):
        degree = degree + (order >= edge * edge).astype(jnp.int32)
    m = order - degree * degree - degree
    lf, mf = degree.astype(F32), m.astype(F32)
    upper = jnp.where(degree + 1 <= LMAX, order + 2 * degree + 2, -1)
    upper_num = (lf + 1.0) * (lf + 1.0) - mf * mf
    upper_coef = jnp.sqrt(jnp.maximum(upper_num, 0.0) / ((2.0 * lf + 1.0) * (2.0 * lf + 3.0)))
    lower = jnp.where(degree - 1 >= jnp.abs(m), order - 2 * degree, -1)
    lower_num = lf * lf - mf * mf
    lower_den = jnp.maximum((2.0 * lf - 1.0) * (2.0 * lf + 1.0), 1.0)
    lower_coef = jnp.sqrt(jnp.maximum(lower_num, 0.0) / lower_den)
    return upper.astype(F32), upper_coef, lower.astype(F32), lower_coef


def turned(block):
    rows, lanes = block.shape
    row = lax.broadcasted_iota(jnp.int32, block.shape, 0)
    group = lax.broadcasted_iota(jnp.int32, block.shape, 1) // 16
    for s in (1, 2, 4):
        below = pltpu.roll(pltpu.roll(block, rows - s, 0), 16 * s, 1)
        above = pltpu.roll(pltpu.roll(block, s, 0), lanes - 16 * s, 1)
        low_row, low_group = (row & s) == 0, (group & s) == 0
        block = jnp.where(
            low_row == low_group, block, jnp.where(low_row, below, above)
        )
    return block


def kernel(
    bound_hbm, cont_hbm, ylm_hbm, weight_hbm, order_hbm, out_ref,
    bound, cont, ylm, order_ref, weight_ref, ys, ncol, z_ref, mine, m_full, cont_t, *rest
):
    sendbufs, (recvbuf, *semaphores) = rest[:HALF], rest[HALF:]
    local_sem, out_sem, a_recv, f_recv, m_recv, relay_recv, end_send, end_recv, *signals = semaphores
    here, both, all_here = signals
    ang, rad = lax.axis_index("ang"), lax.axis_index("rad")
    x, half, core, spot = lax.div(ang, 2), lax.rem(ang, 2), lax.rem(rad, NC), lax.div(rad, NC)
    zl, y = lax.div(spot, NY), lax.rem(spot, NY)
    z = half * HALF + zl
    me = ang * RAD + rad
    x_step = ANG * RAD // NX
    x_peers = [me + (lax.rem(x + d, NX) - x) * x_step for d in (2, 1, 3)]
    opposite = me + RAD - 2 * RAD * half
    twin = me + 1 - 2 * core
    first_spot = me - NC * spot
    edge = (zl == 0) | (zl == HALF - 1)
    z_other = jnp.where(edge, NZ - 1 - z, z)
    to_x, from_x = lax.rem(x + y + 2, NX), lax.rem(x - y + 2 + NX, NX)
    rows_to, rows_from = (device((i, y, z_other, 1 - core)) for i in (to_x, from_x))
    y_peers = [me + (lax.rem(y + d, NY) - y) * NC for d in (2, 1, 3)]
    zl_peers = [me + (lax.rem(zl + d, HALF) - zl) * NY * NC for d in (2, 1, 3)]

    def signal(semaphore, where):
        pl.semaphore_signal(semaphore, inc=1, device_id=where, device_id_type=BY_ID)

    def each(start, end, act):
        def body(i, carry):
            act(i)
            return carry

        lax.fori_loop(start, end, body, 0)

    def send(src, dst, send_sem, recv_sem, where):
        return pltpu.make_async_remote_copy(
            src_ref=src, dst_ref=dst, send_sem=send_sem, recv_sem=recv_sem,
            device_id=where, device_id_type=BY_ID,
        )

    barrier = pltpu.get_barrier_semaphore()
    lines = (rows_from, opposite, rows_to, *zl_peers, *x_peers, *y_peers, twin)
    for where in lines:
        signal(barrier, where)
    loads = [
        pltpu.make_async_copy(ylm_hbm, ylm, local_sem.at[0]),
        pltpu.make_async_copy(order_hbm, order_ref, local_sem.at[3]),
        pltpu.make_async_copy(cont_hbm, cont, local_sem.at[1]),
        pltpu.make_async_copy(bound_hbm, bound.at[ang], local_sem.at[2]),
        pltpu.make_async_copy(weight_hbm, weight_ref, local_sem.at[4]),
    ]
    load_ylm, load_order, load_cont, load_bound, load_weight = loads
    for load in loads:
        load.start()
    pl.semaphore_wait(barrier, len(lines))

    quarter_to = piece_of(to_x, lax.div(z_other, HALF), lax.rem(z_other, HALF), y, 1 - core)[1]
    rows = send(
        ylm.at[pl.ds(pl.multiple_of(quarter_to * PIECE, PIECE), PIECE)],
        ys, out_sem.at[0], f_recv, rows_to,
    )
    load_ylm.wait()
    rows.start()

    across = send(bound_hbm, bound.at[ang], out_sem.at[1], a_recv.at[0], opposite)

    @pl.when(half == 0)
    def _():
        across.start()

    for where in y_peers:
        signal(here, where)

    load_order.wait()
    order = order_ref[...]
    upper, upper_coef, lower, lower_coef = coupling_rows(order)
    orderf = order.astype(F32)
    for s in range(TOTAL // 128):
        ncol[pl.ds(s * 128, 128)] = jnp.broadcast_to(orderf[s : s + 1], (128, 128)).T

    def couple(s, carry):
        here = pl.ds(pl.multiple_of(s * 128, 128), 128)
        column = ncol[here]
        blocks = []
        for t in range(TOTAL // 128):
            cut = slice(t, t + 1)
            blocks.append(
                jnp.where(
                    column == upper[cut],
                    upper_coef[cut],
                    jnp.where(column == lower[cut], lower_coef[cut], 0.0),
                ).astype(BF16)
            )
        g = jnp.concatenate(blocks, axis=1)
        z_ref[here] = lax.dot_general(
            g, ylm[...], (((1,), (1,)), ((), ())), preferred_element_type=F32
        ).astype(BF16)
        return carry

    lax.fori_loop(0, TOTAL // 128, couple, 0)
    for where in x_peers:
        send(bound_hbm, bound.at[ang], out_sem.at[2], a_recv.at[1], where).start()

    @pl.when(half == 1)
    def _():
        across.start()

    load_cont.wait()
    shells = weight_ref.shape[0]
    count_c = cont.shape[0] // shells
    for r in range(shells):
        for c in range(count_c // 128):
            part = cont[pl.ds(r * count_c + c * 128, 128)].astype(F32).T
            cont_t[pl.ds(r * 128, 128), pl.ds(c * 128, 128)] = part.astype(BF16)

    pl.semaphore_wait(here, NY - 1)
    signal(both, twin)

    def block_of(i):
        cls, quarter = piece_of(x, half, lax.div(i, NY), lax.rem(i, NY), core)
        return cls * (RAD // ANG) + quarter

    block = block_of(spot)
    rows.wait_recv()
    mine[...] = jnp.dot(ys[...], z_ref[...], preferred_element_type=F32).astype(BF16)
    spots = RAD // NC
    pl.semaphore_wait(both, 1)

    far, step = jnp.where(zl < HALF // 2, HALF - 1, 0), jnp.where(zl < HALF // 2, -1, 1)

    def give_pieces(own_k, steps, both_from):
        for k in steps:
            for d in (2, 1, 3, 0):
                if (k, d) == (own_k, 0):
                    continue
                where = ang * RAD + (far + step * k) * NY * NC + lax.rem(y + d, NY) * NC + core
                send(mine, m_full.at[block], out_sem.at[3], m_recv.at[spot], where).start()
                if both_from and own_k - k >= both_from:
                    where = where + 1 - 2 * core
                    send(mine, m_full.at[block], out_sem.at[6], relay_recv, where).start()

    @pl.when(edge)
    def _():
        give_pieces(HALF - 1, (1, 0, 2, 3), NEXT)

    @pl.when(jnp.logical_not(edge))
    def _():
        give_pieces(HALF // 2, range(HALF), 0)

    send(mine, m_full.at[block], out_sem.at[4], relay_recv, twin).start()
    m_full[block] = mine[...]

    signal(all_here.at[0], opposite)
    across.wait_recv()
    other = bound.at[ang + 1 - 2 * half]
    for where in x_peers:
        send(other, other, out_sem.at[5], a_recv.at[2], where).start()
    pl.semaphore_wait(all_here.at[0], 1)
    for where in x_peers:
        signal(all_here.at[1], where)

    def pass_on(start, end, limit):
        def act(i):
            @pl.when(i != spot)
            def _():
                there = m_full.at[block_of(i)]
                send(there, there, out_sem.at[4], m_recv.at[i], twin).wait_recv()

                @pl.when(jnp.abs(lax.div(i, NY) - zl) < limit)
                def _():
                    send(there, there, out_sem.at[4], relay_recv, twin).start()

        each(start, end, act)

    pass_on(NY, spots - NY, spots)
    pass_on(0, NY, NEXT)
    pass_on(spots - NY, spots, NEXT)
    load_bound.wait()
    load_weight.wait()
    three = bound.at[pl.ds(0, NX - 1)]
    for i in (1, 2):
        send(three, three, out_sem.at[2], a_recv.at[i], twin).wait_recv()
    pl.semaphore_wait(all_here.at[1], NX - 1)
    signal(all_here.at[2], twin)
    bound_all = jnp.concatenate([bound[i] for i in range(ANG)], axis=1)
    half_m = m_full.at[pl.ds(0, spots)]
    send(half_m, half_m, out_sem.at[4], relay_recv, twin).wait_recv()
    pl.semaphore_wait(all_here.at[2], 1)

    operator = m_full[...].reshape(PTS * ANG, PTS)
    d = jnp.dot(bound_all, operator, preferred_element_type=F32)
    nb = d.shape[0] // shells
    weighted = [d[r * nb : (r + 1) * nb] * weight_ref[r] for r in range(shells)]
    wide = jnp.concatenate(weighted, axis=1).astype(BF16)

    def give(q, row, number):
        pltpu.make_async_remote_copy(
            src_ref=sendbufs[q].at[pl.ds(row, 1)], dst_ref=recvbuf.at[pl.ds(me, 1)],
            send_sem=end_send, recv_sem=end_recv, device_id=number, device_id_type=BY_ID,
        ).start()

    columns = []
    for dx, dy, dc in PLANE:
        there_x = lax.rem(x + dx, NX)
        there_yc = lax.rem(y + dy, NY) * NC + lax.rem(core + dc, NC)
        columns.append((there_x * 16 + there_yc, there_x * x_step + there_yc))
    for q in range(HALF):
        terms = jnp.dot(
            wide, cont_t[:, pl.ds(q * 128, 128)], preferred_element_type=F32
        )
        sendbufs[q][...] = turned(terms)
        for row, number in columns:
            give(q, row, number + q * NY * NC)
    for q in range(HALF):
        for row, number in columns:
            give(q, row + 8, number + (q + HALF) * NY * NC)
    own_yc = y * NC + core
    for there in range(NZ):
        q, row = there % HALF, x * 16 + there // HALF * 8 + own_yc

        @pl.when(z != there)
        def _():
            give(q, row, x * x_step + there * NY * NC + own_yc)

        @pl.when(z == there)
        def _():
            pltpu.make_async_copy(
                sendbufs[q].at[pl.ds(row, 1)], recvbuf.at[pl.ds(me, 1)], end_recv
            ).start()

    rows.wait_send()
    across.wait_send()
    for i in (2, 5):
        send(three, three, out_sem.at[i], a_recv.at[1], twin).wait_send()
    own_m = m_full.at[pl.ds(0, spots - 1)]
    send(own_m, own_m, out_sem.at[3], relay_recv, twin).wait_send()

    def sent_pieces(i, n):
        part = m_full.at[pl.ds(0, n)]
        send(part, part, out_sem.at[i], relay_recv, twin).wait_send()

    sent_pieces(4, spots - NY)

    @pl.when(edge)
    def _():
        sent_pieces(6, NY)

    @pl.when(jnp.logical_not(edge))
    def _():
        sent_pieces(4, NY)

    pltpu.make_async_copy(recvbuf, recvbuf, end_recv).wait()
    row = jnp.sum(recvbuf[...], axis=0, keepdims=True)
    wide_row = jnp.broadcast_to(row, (8, 128))
    at = lax.broadcasted_iota(jnp.int32, (8, 128), 0)
    spread = wide_row
    for j in range(1, 8):
        spread = jnp.where(at == j, pltpu.roll(wide_row, 128 - 16 * j, 1), spread)
    out_ref[...] = spread[:, : out_ref.shape[1]]
    sent = recvbuf.at[pl.ds(0, ANG * RAD - 1)]
    pltpu.make_async_copy(sent, sent, end_send).wait()


def shards(psi_bound, psi_cont, ylm, radial_weight, order):
    shells, nb, points = psi_bound.shape
    count = psi_cont.shape[1]
    any_space = pl.BlockSpec(memory_space=pl.ANY)
    dma = pltpu.SemaphoreType.DMA
    return pl.pallas_call(
        kernel,
        out_shape=jax.ShapeDtypeStruct((nb // ANG, count // RAD), F32),
        in_specs=[
            any_space,
            any_space,
            any_space,
            any_space,
            any_space,
        ],
        out_specs=pl.BlockSpec(memory_space=pltpu.VMEM),
        scratch_shapes=[
            pltpu.VMEM((ANG, shells * nb, points), BF16),
            pltpu.VMEM((shells * count, points), BF16),
            pltpu.VMEM((points, TOTAL), BF16),
            pltpu.VMEM((8, TOTAL // 8), jnp.int32),
            pltpu.SMEM((shells,), F32),
            pltpu.VMEM((PIECE, TOTAL), BF16),
            pltpu.VMEM((TOTAL, 128), F32),
            pltpu.VMEM((TOTAL, points), BF16),
            pltpu.VMEM((PIECE, points), BF16),
            pltpu.VMEM((RAD, PIECE, points), BF16),
            pltpu.VMEM((shells * points, count), BF16),
            *[pltpu.VMEM((64, 128), F32)] * HALF,
            pltpu.VMEM((ANG * RAD, 128), F32),
            dma((5,)),
            dma((7,)),
            dma((3,)),
            dma,
            dma((RAD // NC,)),
            dma,
            dma,
            dma,
            *[pltpu.SemaphoreType.REGULAR] * 2,
            pltpu.SemaphoreType.REGULAR((3,)),
        ],
        compiler_params=pltpu.CompilerParams(collective_id=0, has_side_effects=True),
        name="dipole",
    )(
        psi_bound.reshape(shells * nb, points),
        psi_cont.reshape(shells * count, points),
        ylm,
        radial_weight,
        order.reshape(8, TOTAL // 8),
    )


def solution(mesh):
    return jax.shard_map(
        shards,
        mesh=mesh,
        in_specs=(P("rad", None, "ang"), P("rad", None, "ang"), P("ang", None), P("rad"), P()),
        out_specs=P("ang", "rad"),
        check_vma=False,
    )
```

```python
import functools

import jax
import jax.numpy as jnp
from jax import lax
from jax.experimental import pallas as pl
from jax.experimental.pallas import tpu as pltpu
from jax.sharding import PartitionSpec as P

LMAX = 31
F32, BF16 = jnp.float32, jnp.bfloat16
NX, NY, NZ, NC, HALF = 4, 4, 8, 2, 4
ANG, RAD = 8, 32
PTS, TOTAL = 128, 1024
PIECE = PTS * ANG // RAD


def ring(d, n):
    return min(d, n - d)


PLANE = sorted(
    ((dx, dy, dc) for dx in range(NX) for dy in range(NY) for dc in range(NC) if (dx, dy, dc) != (0, 0, 0)),
    key=lambda o: -(ring(o[0], NX) + ring(o[1], NY)),
)
NEXT = 3
BY_ID = pl.DeviceIdType.LOGICAL


def device(place):
    x, y, z, core = place
    return x * (ANG * RAD // NX) + z * (NY * NC) + y * NC + core


def piece_of(x, half, zl, y, core):
    edge = (zl == 0) | (zl == HALF - 1)
    other = jnp.where(edge, 1 - half, half)
    pair = jnp.where(edge, lax.div(zl, HALF - 1), zl - 1)
    return lax.rem(x - y + 2 + NX, NX) * 2 + other, pair * 2 + core


def coupling_rows(order):
    degree = jnp.zeros(order.shape, jnp.int32)
    for edge in range(1, LMAX + 1):
        degree = degree + (order >= edge * edge).astype(jnp.int32)
    m = order - degree * degree - degree
    lf, mf = degree.astype(F32), m.astype(F32)
    upper = jnp.where(degree + 1 <= LMAX, order + 2 * degree + 2, -1)
    upper_num = (lf + 1.0) * (lf + 1.0) - mf * mf
    upper_coef = jnp.sqrt(jnp.maximum(upper_num, 0.0) / ((2.0 * lf + 1.0) * (2.0 * lf + 3.0)))
    lower = jnp.where(degree - 1 >= jnp.abs(m), order - 2 * degree, -1)
    lower_num = lf * lf - mf * mf
    lower_den = jnp.maximum((2.0 * lf - 1.0) * (2.0 * lf + 1.0), 1.0)
    lower_coef = jnp.sqrt(jnp.maximum(lower_num, 0.0) / lower_den)
    return upper.astype(F32), upper_coef, lower.astype(F32), lower_coef


def turned(block):
    rows, lanes = block.shape
    row = lax.broadcasted_iota(jnp.int32, block.shape, 0)
    group = lax.broadcasted_iota(jnp.int32, block.shape, 1) // 16
    for s in (1, 2, 4):
        below = pltpu.roll(pltpu.roll(block, rows - s, 0), 16 * s, 1)
        above = pltpu.roll(pltpu.roll(block, s, 0), lanes - 16 * s, 1)
        low_row, low_group = (row & s) == 0, (group & s) == 0
        block = jnp.where(
            low_row == low_group, block, jnp.where(low_row, below, above)
        )
    return block


def kernel(
    bound_hbm, cont_hbm, ylm_hbm, weight_hbm, order_hbm, out_ref,
    bound, cont, ylm, order_ref, weight_ref, ys, ncol, z_ref, mine, m_full, cont_t, *rest
):
    sendbufs, (recvbuf, *semaphores) = rest[:HALF], rest[HALF:]
    local_sem, out_sem, a_recv, f_recv, m_recv, relay_recv, end_send, end_recv, *signals = semaphores
    here, both, answer, all_here = signals
    ang, rad = lax.axis_index("ang"), lax.axis_index("rad")
    x, half, core, spot = lax.div(ang, 2), lax.rem(ang, 2), lax.rem(rad, NC), lax.div(rad, NC)
    zl, y = lax.div(spot, NY), lax.rem(spot, NY)
    z = half * HALF + zl
    me = ang * RAD + rad
    x_step = ANG * RAD // NX
    x_peers = [me + (lax.rem(x + d, NX) - x) * x_step for d in (2, 1, 3)]
    opposite = me + RAD - 2 * RAD * half
    twin = me + 1 - 2 * core
    first_spot = me - NC * spot
    edge = (zl == 0) | (zl == HALF - 1)
    z_other = jnp.where(edge, NZ - 1 - z, z)
    to_x, from_x = lax.rem(x + y + 2, NX), lax.rem(x - y + 2 + NX, NX)
    rows_to, rows_from = (device((i, y, z_other, 1 - core)) for i in (to_x, from_x))
    y_peers = [me + (lax.rem(y + d, NY) - y) * NC for d in (2, 1, 3)]
    zl_peers = [me + (lax.rem(zl + d, HALF) - zl) * NY * NC for d in (2, 1, 3)]

    def signal(semaphore, where):
        pl.semaphore_signal(semaphore, inc=1, device_id=where, device_id_type=BY_ID)

    def each(start, end, act):
        def body(i, carry):
            act(i)
            return carry

        lax.fori_loop(start, end, body, 0)

    def send(src, dst, send_sem, recv_sem, where):
        return pltpu.make_async_remote_copy(
            src_ref=src, dst_ref=dst, send_sem=send_sem, recv_sem=recv_sem,
            device_id=where, device_id_type=BY_ID,
        )

    barrier = pltpu.get_barrier_semaphore()
    lines = (rows_from, rows_to, *zl_peers, *x_peers, *y_peers, twin)
    late_edge, near_edge = edge & (half == 1), edge & (half == 0)
    for where in lines:
        signal(barrier, where)

    @pl.when(jnp.logical_not(late_edge))
    def _():
        signal(barrier, opposite)

    loads = [
        pltpu.make_async_copy(ylm_hbm, ylm, local_sem.at[0]),
        pltpu.make_async_copy(order_hbm, order_ref, local_sem.at[3]),
        pltpu.make_async_copy(cont_hbm, cont, local_sem.at[1]),
        pltpu.make_async_copy(bound_hbm, bound.at[ang], local_sem.at[2]),
        pltpu.make_async_copy(weight_hbm, weight_ref, local_sem.at[4]),
    ]
    load_ylm, load_order, load_cont, load_bound, load_weight = loads
    for load in loads:
        load.start()
    pl.semaphore_wait(barrier, jnp.where(near_edge, len(lines), len(lines) + 1))

    quarter_to = piece_of(to_x, lax.div(z_other, HALF), lax.rem(z_other, HALF), y, 1 - core)[1]
    rows = send(
        ylm.at[pl.ds(pl.multiple_of(quarter_to * PIECE, PIECE), PIECE)],
        ys, out_sem.at[0], f_recv, rows_to,
    )
    load_ylm.wait()
    rows.start()

    across = send(bound_hbm, bound.at[ang], out_sem.at[1], a_recv.at[0], opposite)

    @pl.when(late_edge)
    def _():
        signal(answer, opposite)

    @pl.when((half == 0) & jnp.logical_not(edge))
    def _():
        across.start()

    for where in y_peers:
        signal(here, where)

    load_order.wait()
    order = order_ref[...]
    upper, upper_coef, lower, lower_coef = coupling_rows(order)
    orderf = order.astype(F32)
    for s in range(TOTAL // 128):
        ncol[pl.ds(s * 128, 128)] = jnp.broadcast_to(orderf[s : s + 1], (128, 128)).T

    def couple(s, carry):
        here = pl.ds(pl.multiple_of(s * 128, 128), 128)
        column = ncol[here]
        blocks = []
        for t in range(TOTAL // 128):
            cut = slice(t, t + 1)
            blocks.append(
                jnp.where(
                    column == upper[cut],
                    upper_coef[cut],
                    jnp.where(column == lower[cut], lower_coef[cut], 0.0),
                ).astype(BF16)
            )
        g = jnp.concatenate(blocks, axis=1)
        z_ref[here] = lax.dot_general(
            g, ylm[...], (((1,), (1,)), ((), ())), preferred_element_type=F32
        ).astype(BF16)
        return carry

    lax.fori_loop(0, TOTAL // 128, couple, 0)
    for where in x_peers:
        send(bound_hbm, bound.at[ang], out_sem.at[2], a_recv.at[1], where).start()

    @pl.when(near_edge)
    def _():
        pl.semaphore_wait(answer, 1)

    @pl.when((half == 1) | edge)
    def _():
        across.start()

    load_cont.wait()
    shells = weight_ref.shape[0]
    count_c = cont.shape[0] // shells
    for r in range(shells):
        for c in range(count_c // 128):
            part = cont[pl.ds(r * count_c + c * 128, 128)].astype(F32).T
            cont_t[pl.ds(r * 128, 128), pl.ds(c * 128, 128)] = part.astype(BF16)

    pl.semaphore_wait(here, NY - 1)
    signal(both, twin)

    def block_of(i):
        cls, quarter = piece_of(x, half, lax.div(i, NY), lax.rem(i, NY), core)
        return cls * (RAD // ANG) + quarter

    block = block_of(spot)
    rows.wait_recv()
    mine[...] = jnp.dot(ys[...], z_ref[...], preferred_element_type=F32).astype(BF16)
    spots = RAD // NC
    pl.semaphore_wait(both, 1)

    far, step = jnp.where(zl < HALF // 2, HALF - 1, 0), jnp.where(zl < HALF // 2, -1, 1)

    def give_pieces(own_k, steps, both_from):
        for k in steps:
            for d in (2, 1, 3, 0):
                if (k, d) == (own_k, 0):
                    continue
                where = ang * RAD + (far + step * k) * NY * NC + lax.rem(y + d, NY) * NC + core
                send(mine, m_full.at[block], out_sem.at[3], m_recv.at[spot], where).start()
                if both_from and own_k - k >= both_from:
                    where = where + 1 - 2 * core
                    send(mine, m_full.at[block], out_sem.at[6], relay_recv, where).start()

    @pl.when(edge)
    def _():
        give_pieces(HALF - 1, (1, 0, 2, 3), NEXT)

    @pl.when(jnp.logical_not(edge))
    def _():
        give_pieces(HALF // 2, range(HALF), 0)

    send(mine, m_full.at[block], out_sem.at[4], relay_recv, twin).start()
    m_full[block] = mine[...]

    signal(all_here.at[0], opposite)
    across.wait_recv()
    other = bound.at[ang + 1 - 2 * half]
    for where in x_peers:
        send(other, other, out_sem.at[5], a_recv.at[2], where).start()
    pl.semaphore_wait(all_here.at[0], 1)
    for where in x_peers:
        signal(all_here.at[1], where)

    def pass_on(start, end, limit):
        def act(i):
            @pl.when(i != spot)
            def _():
                there = m_full.at[block_of(i)]
                send(there, there, out_sem.at[4], m_recv.at[i], twin).wait_recv()

                @pl.when(jnp.abs(lax.div(i, NY) - zl) < limit)
                def _():
                    send(there, there, out_sem.at[4], relay_recv, twin).start()

        each(start, end, act)

    pass_on(NY, spots - NY, spots)
    pass_on(0, NY, NEXT)
    pass_on(spots - NY, spots, NEXT)
    load_bound.wait()
    load_weight.wait()
    three = bound.at[pl.ds(0, NX - 1)]
    for i in (1, 2):
        send(three, three, out_sem.at[2], a_recv.at[i], twin).wait_recv()
    pl.semaphore_wait(all_here.at[1], NX - 1)
    signal(all_here.at[2], twin)
    bound_all = jnp.concatenate([bound[i] for i in range(ANG)], axis=1)
    half_m = m_full.at[pl.ds(0, spots)]
    send(half_m, half_m, out_sem.at[4], relay_recv, twin).wait_recv()
    pl.semaphore_wait(all_here.at[2], 1)

    operator = m_full[...].reshape(PTS * ANG, PTS)
    d = jnp.dot(bound_all, operator, preferred_element_type=F32)
    nb = d.shape[0] // shells
    weighted = [d[r * nb : (r + 1) * nb] * weight_ref[r] for r in range(shells)]
    wide = jnp.concatenate(weighted, axis=1).astype(BF16)

    def give(q, row, number):
        pltpu.make_async_remote_copy(
            src_ref=sendbufs[q].at[pl.ds(row, 1)], dst_ref=recvbuf.at[pl.ds(me, 1)],
            send_sem=end_send, recv_sem=end_recv, device_id=number, device_id_type=BY_ID,
        ).start()

    columns = []
    for dx, dy, dc in PLANE:
        there_x = lax.rem(x + dx, NX)
        there_yc = lax.rem(y + dy, NY) * NC + lax.rem(core + dc, NC)
        columns.append((there_x * 16 + there_yc, there_x * x_step + there_yc))
    for q in range(HALF):
        terms = jnp.dot(
            wide, cont_t[:, pl.ds(q * 128, 128)], preferred_element_type=F32
        )
        sendbufs[q][...] = turned(terms)
        for row, number in columns:
            give(q, row, number + q * NY * NC)
    for q in range(HALF):
        for row, number in columns:
            give(q, row + 8, number + (q + HALF) * NY * NC)
    own_yc = y * NC + core
    for there in range(NZ):
        q, row = there % HALF, x * 16 + there // HALF * 8 + own_yc

        @pl.when(z != there)
        def _():
            give(q, row, x * x_step + there * NY * NC + own_yc)

        @pl.when(z == there)
        def _():
            pltpu.make_async_copy(
                sendbufs[q].at[pl.ds(row, 1)], recvbuf.at[pl.ds(me, 1)], end_recv
            ).start()

    rows.wait_send()
    across.wait_send()
    for i in (2, 5):
        send(three, three, out_sem.at[i], a_recv.at[1], twin).wait_send()
    own_m = m_full.at[pl.ds(0, spots - 1)]
    send(own_m, own_m, out_sem.at[3], relay_recv, twin).wait_send()

    def sent_pieces(i, n):
        part = m_full.at[pl.ds(0, n)]
        send(part, part, out_sem.at[i], relay_recv, twin).wait_send()

    sent_pieces(4, spots - NY)

    @pl.when(edge)
    def _():
        sent_pieces(6, NY)

    @pl.when(jnp.logical_not(edge))
    def _():
        sent_pieces(4, NY)

    pltpu.make_async_copy(recvbuf, recvbuf, end_recv).wait()
    row = jnp.sum(recvbuf[...], axis=0, keepdims=True)
    wide_row = jnp.broadcast_to(row, (8, 128))
    at = lax.broadcasted_iota(jnp.int32, (8, 128), 0)
    spread = wide_row
    for j in range(1, 8):
        spread = jnp.where(at == j, pltpu.roll(wide_row, 128 - 16 * j, 1), spread)
    out_ref[...] = spread[:, : out_ref.shape[1]]
    sent = recvbuf.at[pl.ds(0, ANG * RAD - 1)]
    pltpu.make_async_copy(sent, sent, end_send).wait()


def shards(psi_bound, psi_cont, ylm, radial_weight, order):
    shells, nb, points = psi_bound.shape
    count = psi_cont.shape[1]
    any_space = pl.BlockSpec(memory_space=pl.ANY)
    dma = pltpu.SemaphoreType.DMA
    return pl.pallas_call(
        kernel,
        out_shape=jax.ShapeDtypeStruct((nb // ANG, count // RAD), F32),
        in_specs=[
            any_space,
            any_space,
            any_space,
            any_space,
            any_space,
        ],
        out_specs=pl.BlockSpec(memory_space=pltpu.VMEM),
        scratch_shapes=[
            pltpu.VMEM((ANG, shells * nb, points), BF16),
            pltpu.VMEM((shells * count, points), BF16),
            pltpu.VMEM((points, TOTAL), BF16),
            pltpu.VMEM((8, TOTAL // 8), jnp.int32),
            pltpu.SMEM((shells,), F32),
            pltpu.VMEM((PIECE, TOTAL), BF16),
            pltpu.VMEM((TOTAL, 128), F32),
            pltpu.VMEM((TOTAL, points), BF16),
            pltpu.VMEM((PIECE, points), BF16),
            pltpu.VMEM((RAD, PIECE, points), BF16),
            pltpu.VMEM((shells * points, count), BF16),
            *[pltpu.VMEM((64, 128), F32)] * HALF,
            pltpu.VMEM((ANG * RAD, 128), F32),
            dma((5,)),
            dma((7,)),
            dma((3,)),
            dma,
            dma((RAD // NC,)),
            dma,
            dma,
            dma,
            *[pltpu.SemaphoreType.REGULAR] * 3,
            pltpu.SemaphoreType.REGULAR((3,)),
        ],
        compiler_params=pltpu.CompilerParams(collective_id=0, has_side_effects=True),
        name="dipole",
    )(
        psi_bound.reshape(shells * nb, points),
        psi_cont.reshape(shells * count, points),
        ylm,
        radial_weight,
        order.reshape(8, TOTAL // 8),
    )


def solution(mesh):
    return jax.shard_map(
        shards,
        mesh=mesh,
        in_specs=(P("rad", None, "ang"), P("rad", None, "ang"), P("ang", None), P("rad"), P()),
        out_specs=P("ang", "rad"),
        check_vma=False,
    )
```

```python
import functools

import jax
import jax.numpy as jnp
from jax import lax
from jax.experimental import pallas as pl
from jax.experimental.pallas import tpu as pltpu
from jax.sharding import PartitionSpec as P

LMAX = 31
F32, BF16 = jnp.float32, jnp.bfloat16
NX, NY, NZ, NC, HALF = 4, 4, 8, 2, 4
ANG, RAD = 8, 32
PTS, TOTAL = 128, 1024
PIECE = PTS * ANG // RAD


def ring(d, n):
    return min(d, n - d)


PLANE = sorted(
    ((dx, dy, dc) for dx in range(NX) for dy in range(NY) for dc in range(NC) if (dx, dy, dc) != (0, 0, 0)),
    key=lambda o: -(ring(o[0], NX) + ring(o[1], NY)),
)
NEXT = 3
BY_ID = pl.DeviceIdType.LOGICAL


def device(place):
    x, y, z, core = place
    return x * (ANG * RAD // NX) + z * (NY * NC) + y * NC + core


def piece_of(x, half, zl, y, core):
    edge = (zl == 0) | (zl == HALF - 1)
    other = jnp.where(edge, 1 - half, half)
    pair = jnp.where(edge, lax.div(zl, HALF - 1), zl - 1)
    return lax.rem(x - y + 2 + NX, NX) * 2 + other, pair * 2 + core


def coupling_rows(order):
    degree = jnp.zeros(order.shape, jnp.int32)
    for edge in range(1, LMAX + 1):
        degree = degree + (order >= edge * edge).astype(jnp.int32)
    m = order - degree * degree - degree
    lf, mf = degree.astype(F32), m.astype(F32)
    upper = jnp.where(degree + 1 <= LMAX, order + 2 * degree + 2, -1)
    upper_num = (lf + 1.0) * (lf + 1.0) - mf * mf
    upper_coef = jnp.sqrt(jnp.maximum(upper_num, 0.0) / ((2.0 * lf + 1.0) * (2.0 * lf + 3.0)))
    lower = jnp.where(degree - 1 >= jnp.abs(m), order - 2 * degree, -1)
    lower_num = lf * lf - mf * mf
    lower_den = jnp.maximum((2.0 * lf - 1.0) * (2.0 * lf + 1.0), 1.0)
    lower_coef = jnp.sqrt(jnp.maximum(lower_num, 0.0) / lower_den)
    return upper.astype(F32), upper_coef, lower.astype(F32), lower_coef


def turned(block):
    rows, lanes = block.shape
    tiles = block.reshape(rows // 8, 8, lanes)
    row = lax.broadcasted_iota(jnp.int32, (1, 8, lanes), 1)
    group = lax.broadcasted_iota(jnp.int32, (1, 8, lanes), 2) // 16
    for s in (1, 2, 4):
        low = jnp.broadcast_to((row & s) == 0, tiles.shape)
        same = jnp.broadcast_to(((row ^ group) & s) == 0, tiles.shape)
        below = pltpu.roll(pltpu.roll(tiles, 8 - s, 1), 16 * s, 2)
        if 2 * s < 8:
            above = pltpu.roll(pltpu.roll(tiles, s, 1), lanes - 16 * s, 2)
            below = jnp.where(low, below, above)
        tiles = jnp.where(same, tiles, below)
    return tiles.reshape(rows, lanes)


def kernel(
    bound_hbm, cont_hbm, ylm_hbm, weight_hbm, order_hbm, out_ref,
    bound, cont, ylm, order_ref, weight_ref, ys, ncol, z_ref, mine, m_full, early_d, cont_t, *rest
):
    sendbufs, (recvbuf, *semaphores) = rest[:HALF], rest[HALF:]
    local_sem, out_sem, a_recv, f_recv, m_recv, relay_recv, end_send, end_recv, *signals = semaphores
    here, both, all_here = signals
    ang, rad = lax.axis_index("ang"), lax.axis_index("rad")
    x, half, core, spot = lax.div(ang, 2), lax.rem(ang, 2), lax.rem(rad, NC), lax.div(rad, NC)
    zl, y = lax.div(spot, NY), lax.rem(spot, NY)
    z = half * HALF + zl
    me = ang * RAD + rad
    x_step = ANG * RAD // NX
    x_peers = [me + (lax.rem(x + d, NX) - x) * x_step for d in (2, 1, 3)]
    opposite = me + RAD - 2 * RAD * half
    twin = me + 1 - 2 * core
    first_spot = me - NC * spot
    edge = (zl == 0) | (zl == HALF - 1)
    z_other = jnp.where(edge, NZ - 1 - z, z)
    to_x, from_x = lax.rem(x + y + 2, NX), lax.rem(x - y + 2 + NX, NX)
    rows_to, rows_from = (device((i, y, z_other, 1 - core)) for i in (to_x, from_x))
    y_peers = [me + (lax.rem(y + d, NY) - y) * NC for d in (2, 1, 3)]
    zl_peers = [me + (lax.rem(zl + d, HALF) - zl) * NY * NC for d in (2, 1, 3)]

    def signal(semaphore, where):
        pl.semaphore_signal(semaphore, inc=1, device_id=where, device_id_type=BY_ID)

    def each(start, end, act):
        def body(i, carry):
            act(i)
            return carry

        lax.fori_loop(start, end, body, 0)

    def send(src, dst, send_sem, recv_sem, where):
        return pltpu.make_async_remote_copy(
            src_ref=src, dst_ref=dst, send_sem=send_sem, recv_sem=recv_sem,
            device_id=where, device_id_type=BY_ID,
        )

    barrier = pltpu.get_barrier_semaphore()
    lines = (rows_from, opposite, rows_to, *zl_peers, *x_peers, *y_peers, twin)
    for where in lines:
        signal(barrier, where)
    loads = [
        pltpu.make_async_copy(ylm_hbm, ylm, local_sem.at[0]),
        pltpu.make_async_copy(order_hbm, order_ref, local_sem.at[3]),
        pltpu.make_async_copy(cont_hbm, cont, local_sem.at[1]),
        pltpu.make_async_copy(bound_hbm, bound.at[ang], local_sem.at[2]),
        pltpu.make_async_copy(weight_hbm, weight_ref, local_sem.at[4]),
    ]
    load_ylm, load_order, load_cont, load_bound, load_weight = loads
    for load in loads:
        load.start()
    pl.semaphore_wait(barrier, len(lines))

    quarter_to = piece_of(to_x, lax.div(z_other, HALF), lax.rem(z_other, HALF), y, 1 - core)[1]
    rows = send(
        ylm.at[pl.ds(pl.multiple_of(quarter_to * PIECE, PIECE), PIECE)],
        ys, out_sem.at[0], f_recv, rows_to,
    )
    load_ylm.wait()
    rows.start()

    across = send(bound_hbm, bound.at[ang], out_sem.at[1], a_recv.at[0], opposite)

    @pl.when(half == 0)
    def _():
        across.start()

    for where in y_peers:
        signal(here, where)

    load_order.wait()
    order = order_ref[...]
    upper, upper_coef, lower, lower_coef = coupling_rows(order)
    orderf = order.astype(F32)
    for s in range(TOTAL // 128):
        ncol[pl.ds(s * 128, 128)] = jnp.broadcast_to(orderf[s : s + 1], (128, 128)).T

    def couple(s, carry):
        here = pl.ds(pl.multiple_of(s * 128, 128), 128)
        column = ncol[here]
        blocks = []
        for t in range(TOTAL // 128):
            cut = slice(t, t + 1)
            blocks.append(
                jnp.where(
                    column == upper[cut],
                    upper_coef[cut],
                    jnp.where(column == lower[cut], lower_coef[cut], 0.0),
                ).astype(BF16)
            )
        g = jnp.concatenate(blocks, axis=1)
        z_ref[here] = lax.dot_general(
            g, ylm[...], (((1,), (1,)), ((), ())), preferred_element_type=F32
        ).astype(BF16)
        return carry

    lax.fori_loop(0, TOTAL // 128, couple, 0)
    for where in x_peers:
        send(bound_hbm, bound.at[ang], out_sem.at[2], a_recv.at[1], where).start()

    @pl.when(half == 1)
    def _():
        across.start()

    load_cont.wait()
    shells = weight_ref.shape[0]
    count_c = cont.shape[0] // shells
    for r in range(shells):
        for c in range(count_c // 128):
            part = cont[pl.ds(r * count_c + c * 128, 128)].astype(F32).T
            cont_t[pl.ds(r * 128, 128), pl.ds(c * 128, 128)] = part.astype(BF16)

    pl.semaphore_wait(here, NY - 1)
    signal(both, twin)

    def block_of(i):
        cls, quarter = piece_of(x, half, lax.div(i, NY), lax.rem(i, NY), core)
        return cls * (RAD // ANG) + quarter

    block = block_of(spot)
    rows.wait_recv()
    mine[...] = jnp.dot(ys[...], z_ref[...], preferred_element_type=F32).astype(BF16)
    spots = RAD // NC
    pl.semaphore_wait(both, 1)

    far, step = jnp.where(zl < HALF // 2, HALF - 1, 0), jnp.where(zl < HALF // 2, -1, 1)

    def give_pieces(own_k, steps, both_from):
        for k in steps:
            for d in (2, 1, 3, 0):
                if (k, d) == (own_k, 0):
                    continue
                where = ang * RAD + (far + step * k) * NY * NC + lax.rem(y + d, NY) * NC + core
                send(mine, m_full.at[block], out_sem.at[3], m_recv.at[spot], where).start()
                if both_from and own_k - k >= both_from:
                    where = where + 1 - 2 * core
                    send(mine, m_full.at[block], out_sem.at[6], relay_recv.at[1], where).start()

    @pl.when(edge)
    def _():
        give_pieces(HALF - 1, (1, 0, 2, 3), NEXT)

    @pl.when(jnp.logical_not(edge))
    def _():
        give_pieces(HALF // 2, range(HALF), 0)

    when = jnp.where(edge, 1, 0)
    send(mine, m_full.at[block], out_sem.at[4], relay_recv.at[when], twin).start()
    m_full[block] = mine[...]

    signal(all_here.at[0], opposite)
    across.wait_recv()
    other = bound.at[ang + 1 - 2 * half]
    for where in x_peers:
        send(other, other, out_sem.at[5], a_recv.at[2], where).start()
    pl.semaphore_wait(all_here.at[0], 1)
    for where in x_peers:
        signal(all_here.at[1], where)

    def pass_on(start, end, limit, when):
        def act(i):
            @pl.when(i != spot)
            def _():
                there = m_full.at[block_of(i)]
                send(there, there, out_sem.at[4], m_recv.at[i], twin).wait_recv()

                @pl.when(jnp.abs(lax.div(i, NY) - zl) < limit)
                def _():
                    send(there, there, out_sem.at[4], relay_recv.at[when], twin).start()

        each(start, end, act)

    def passed(when):
        part = m_full.at[pl.ds(0, spots // 2)]
        send(part, part, out_sem.at[4], relay_recv.at[when], twin).wait_recv()

    def product(side):
        left = jnp.concatenate([bound[2 * i + side] for i in range(NX)], axis=1)
        right = [
            m_full[pl.ds((2 * i + side) * (RAD // ANG), RAD // ANG)].reshape(PTS, PTS)
            for i in range(NX)
        ]
        right = jnp.concatenate(right, axis=0)
        return jnp.dot(left, right, preferred_element_type=F32)

    pass_on(NY, spots - NY, spots, 0)
    load_bound.wait()
    load_weight.wait()
    three = bound.at[pl.ds(0, NX - 1)]
    send(three, three, out_sem.at[2], a_recv.at[1], twin).wait_recv()
    passed(0)
    early_d[...] = product(half)
    pass_on(0, NY, NEXT, 1)
    pass_on(spots - NY, spots, NEXT, 1)
    send(three, three, out_sem.at[2], a_recv.at[2], twin).wait_recv()
    pl.semaphore_wait(all_here.at[1], NX - 1)
    signal(all_here.at[2], twin)
    passed(1)
    pl.semaphore_wait(all_here.at[2], 1)

    d = early_d[...] + product(1 - half)
    nb = d.shape[0] // shells
    weighted = [d[r * nb : (r + 1) * nb] * weight_ref[r] for r in range(shells)]
    wide = jnp.concatenate(weighted, axis=1).astype(BF16)

    def give(q, row, number):
        pltpu.make_async_remote_copy(
            src_ref=sendbufs[q].at[pl.ds(row, 1)], dst_ref=recvbuf.at[pl.ds(me, 1)],
            send_sem=end_send, recv_sem=end_recv, device_id=number, device_id_type=BY_ID,
        ).start()

    columns = []
    for dx, dy, dc in PLANE:
        there_x = lax.rem(x + dx, NX)
        there_yc = lax.rem(y + dy, NY) * NC + lax.rem(core + dc, NC)
        columns.append((there_x * 16 + there_yc, there_x * x_step + there_yc))
    for q in range(HALF):
        terms = jnp.dot(
            wide, cont_t[:, pl.ds(q * 128, 128)], preferred_element_type=F32
        )
        sendbufs[q][...] = turned(terms)
        for row, number in columns:
            give(q, row, number + q * NY * NC)
    for q in range(HALF):
        for row, number in columns:
            give(q, row + 8, number + (q + HALF) * NY * NC)
    own_yc = y * NC + core
    for there in range(NZ):
        q, row = there % HALF, x * 16 + there // HALF * 8 + own_yc

        @pl.when(z != there)
        def _():
            give(q, row, x * x_step + there * NY * NC + own_yc)

        @pl.when(z == there)
        def _():
            pltpu.make_async_copy(
                sendbufs[q].at[pl.ds(row, 1)], recvbuf.at[pl.ds(me, 1)], end_recv
            ).start()

    rows.wait_send()
    across.wait_send()
    for i in (2, 5):
        send(three, three, out_sem.at[i], a_recv.at[1], twin).wait_send()
    own_m = m_full.at[pl.ds(0, spots - 1)]
    send(own_m, own_m, out_sem.at[3], relay_recv.at[0], twin).wait_send()

    def sent_pieces(i, n):
        part = m_full.at[pl.ds(0, n)]
        send(part, part, out_sem.at[i], relay_recv.at[0], twin).wait_send()

    sent_pieces(4, spots - NY)

    @pl.when(edge)
    def _():
        sent_pieces(6, NY)

    @pl.when(jnp.logical_not(edge))
    def _():
        sent_pieces(4, NY)

    pltpu.make_async_copy(recvbuf, recvbuf, end_recv).wait()
    row = jnp.sum(recvbuf[...], axis=0, keepdims=True)
    wide_row = jnp.broadcast_to(row, (8, 128))
    at = lax.broadcasted_iota(jnp.int32, (8, 128), 0)
    spread = wide_row
    for j in range(1, 8):
        spread = jnp.where(at == j, pltpu.roll(wide_row, 128 - 16 * j, 1), spread)
    out_ref[...] = spread[:, : out_ref.shape[1]]
    sent = recvbuf.at[pl.ds(0, ANG * RAD - 1)]
    pltpu.make_async_copy(sent, sent, end_send).wait()


def shards(psi_bound, psi_cont, ylm, radial_weight, order):
    shells, nb, points = psi_bound.shape
    count = psi_cont.shape[1]
    any_space = pl.BlockSpec(memory_space=pl.ANY)
    dma = pltpu.SemaphoreType.DMA
    return pl.pallas_call(
        kernel,
        out_shape=jax.ShapeDtypeStruct((nb // ANG, count // RAD), F32),
        in_specs=[
            any_space,
            any_space,
            any_space,
            any_space,
            any_space,
        ],
        out_specs=pl.BlockSpec(memory_space=pltpu.VMEM),
        scratch_shapes=[
            pltpu.VMEM((ANG, shells * nb, points), BF16),
            pltpu.VMEM((shells * count, points), BF16),
            pltpu.VMEM((points, TOTAL), BF16),
            pltpu.VMEM((8, TOTAL // 8), jnp.int32),
            pltpu.SMEM((shells,), F32),
            pltpu.VMEM((PIECE, TOTAL), BF16),
            pltpu.VMEM((TOTAL, 128), F32),
            pltpu.VMEM((TOTAL, points), BF16),
            pltpu.VMEM((PIECE, points), BF16),
            pltpu.VMEM((RAD, PIECE, points), BF16),
            pltpu.VMEM((shells * nb, points), F32),
            pltpu.VMEM((shells * points, count), BF16),
            *[pltpu.VMEM((64, 128), F32)] * HALF,
            pltpu.VMEM((ANG * RAD, 128), F32),
            dma((5,)),
            dma((7,)),
            dma((3,)),
            dma,
            dma((RAD // NC,)),
            dma((2,)),
            dma,
            dma,
            *[pltpu.SemaphoreType.REGULAR] * 2,
            pltpu.SemaphoreType.REGULAR((3,)),
        ],
        compiler_params=pltpu.CompilerParams(collective_id=0, has_side_effects=True),
        name="dipole",
    )(
        psi_bound.reshape(shells * nb, points),
        psi_cont.reshape(shells * count, points),
        ylm,
        radial_weight,
        order.reshape(8, TOTAL // 8),
    )


def solution(mesh):
    return jax.shard_map(
        shards,
        mesh=mesh,
        in_specs=(P("rad", None, "ang"), P("rad", None, "ang"), P("ang", None), P("rad"), P()),
        out_specs=P("ang", "rad"),
        check_vma=False,
    )
```

```python
import functools

import jax
import jax.numpy as jnp
from jax import lax
from jax.experimental import pallas as pl
from jax.experimental.pallas import tpu as pltpu
from jax.sharding import PartitionSpec as P

LMAX = 31
F32, BF16 = jnp.float32, jnp.bfloat16
NX, NY, NZ, NC, HALF = 4, 4, 8, 2, 4
ANG, RAD = 8, 32
PTS, TOTAL = 128, 1024
PIECE = PTS * ANG // RAD


def ring(d, n):
    return min(d, n - d)


PLANE = sorted(
    ((dx, dy, dc) for dx in range(NX) for dy in range(NY) for dc in range(NC) if (dx, dy, dc) != (0, 0, 0)),
    key=lambda o: -(ring(o[0], NX) + ring(o[1], NY)),
)
NEXT = 3
BY_ID = pl.DeviceIdType.LOGICAL


def device(place):
    x, y, z, core = place
    return x * (ANG * RAD // NX) + z * (NY * NC) + y * NC + core


def piece_of(x, half, zl, y, core):
    edge = (zl == 0) | (zl == HALF - 1)
    other = jnp.where(edge, 1 - half, half)
    pair = jnp.where(edge, lax.div(zl, HALF - 1), zl - 1)
    return lax.rem(x - y + 2 + NX, NX) * 2 + other, pair * 2 + core


def coupling_rows(order):
    degree = jnp.zeros(order.shape, jnp.int32)
    for edge in range(1, LMAX + 1):
        degree = degree + (order >= edge * edge).astype(jnp.int32)
    m = order - degree * degree - degree
    lf, mf = degree.astype(F32), m.astype(F32)
    upper = jnp.where(degree + 1 <= LMAX, order + 2 * degree + 2, -1)
    upper_num = (lf + 1.0) * (lf + 1.0) - mf * mf
    upper_coef = jnp.sqrt(jnp.maximum(upper_num, 0.0) / ((2.0 * lf + 1.0) * (2.0 * lf + 3.0)))
    lower = jnp.where(degree - 1 >= jnp.abs(m), order - 2 * degree, -1)
    lower_num = lf * lf - mf * mf
    lower_den = jnp.maximum((2.0 * lf - 1.0) * (2.0 * lf + 1.0), 1.0)
    lower_coef = jnp.sqrt(jnp.maximum(lower_num, 0.0) / lower_den)
    return upper.astype(F32), upper_coef, lower.astype(F32), lower_coef


def turned(block):
    rows, lanes = block.shape
    tiles = block.reshape(rows // 8, 8, lanes)
    row = lax.broadcasted_iota(jnp.int32, (1, 8, lanes), 1)
    group = lax.broadcasted_iota(jnp.int32, (1, 8, lanes), 2) // 16
    for s in (1, 2, 4):
        low = jnp.broadcast_to((row & s) == 0, tiles.shape)
        same = jnp.broadcast_to(((row ^ group) & s) == 0, tiles.shape)
        below = pltpu.roll(pltpu.roll(tiles, 8 - s, 1), 16 * s, 2)
        if 2 * s < 8:
            above = pltpu.roll(pltpu.roll(tiles, s, 1), lanes - 16 * s, 2)
            below = jnp.where(low, below, above)
        tiles = jnp.where(same, tiles, below)
    return tiles.reshape(rows, lanes)


def kernel(
    bound_hbm, cont_hbm, ylm_hbm, weight_hbm, order_hbm, out_ref,
    bound, cont, ylm, order_ref, weight_ref, ys, ncol, z_ref, mine, m_full, early_d, cont_t, *rest
):
    sendbufs, (recvbuf, *semaphores) = rest[:HALF], rest[HALF:]
    local_sem, out_sem, a_recv, f_recv, m_recv, relay_recv, end_send, end_recv, *signals = semaphores
    here, both, all_here = signals
    ang, rad = lax.axis_index("ang"), lax.axis_index("rad")
    x, half, core, spot = lax.div(ang, 2), lax.rem(ang, 2), lax.rem(rad, NC), lax.div(rad, NC)
    zl, y = lax.div(spot, NY), lax.rem(spot, NY)
    z = half * HALF + zl
    me = ang * RAD + rad
    x_step = ANG * RAD // NX
    x_peers = [me + (lax.rem(x + d, NX) - x) * x_step for d in (2, 1, 3)]
    opposite = me + RAD - 2 * RAD * half
    twin = me + 1 - 2 * core
    first_spot = me - NC * spot
    edge = (zl == 0) | (zl == HALF - 1)
    z_other = jnp.where(edge, NZ - 1 - z, z)
    to_x, from_x = lax.rem(x + y + 2, NX), lax.rem(x - y + 2 + NX, NX)
    rows_to, rows_from = (device((i, y, z_other, 1 - core)) for i in (to_x, from_x))
    y_peers = [me + (lax.rem(y + d, NY) - y) * NC for d in (2, 1, 3)]
    zl_peers = [me + (lax.rem(zl + d, HALF) - zl) * NY * NC for d in (2, 1, 3)]

    def signal(semaphore, where):
        pl.semaphore_signal(semaphore, inc=1, device_id=where, device_id_type=BY_ID)

    def each(start, end, act):
        def body(i, carry):
            act(i)
            return carry

        lax.fori_loop(start, end, body, 0)

    def send(src, dst, send_sem, recv_sem, where):
        return pltpu.make_async_remote_copy(
            src_ref=src, dst_ref=dst, send_sem=send_sem, recv_sem=recv_sem,
            device_id=where, device_id_type=BY_ID,
        )

    barrier = pltpu.get_barrier_semaphore()
    lines = (rows_from, opposite, rows_to, *zl_peers, *x_peers, *y_peers, twin)
    for where in lines:
        signal(barrier, where)
    loads = [
        pltpu.make_async_copy(ylm_hbm, ylm, local_sem.at[0]),
        pltpu.make_async_copy(order_hbm, order_ref, local_sem.at[3]),
        pltpu.make_async_copy(cont_hbm, cont, local_sem.at[1]),
        pltpu.make_async_copy(bound_hbm, bound.at[ang], local_sem.at[2]),
        pltpu.make_async_copy(weight_hbm, weight_ref, local_sem.at[4]),
    ]
    load_ylm, load_order, load_cont, load_bound, load_weight = loads
    for load in loads:
        load.start()
    pl.semaphore_wait(barrier, len(lines))

    quarter_to = piece_of(to_x, lax.div(z_other, HALF), lax.rem(z_other, HALF), y, 1 - core)[1]
    rows = send(
        ylm.at[pl.ds(pl.multiple_of(quarter_to * PIECE, PIECE), PIECE)],
        ys, out_sem.at[0], f_recv, rows_to,
    )
    load_ylm.wait()
    rows.start()

    across = send(bound_hbm, bound.at[ang], out_sem.at[1], a_recv.at[0], opposite)

    @pl.when(half == 0)
    def _():
        across.start()

    for where in y_peers:
        signal(here, where)

    load_order.wait()
    order = order_ref[...]
    upper, upper_coef, lower, lower_coef = coupling_rows(order)
    orderf = order.astype(F32)
    for s in range(TOTAL // 128):
        ncol[pl.ds(s * 128, 128)] = jnp.broadcast_to(orderf[s : s + 1], (128, 128)).T

    def couple(s, carry):
        here = pl.ds(pl.multiple_of(s * 128, 128), 128)
        column = ncol[here]
        blocks = []
        for t in range(TOTAL // 128):
            cut = slice(t, t + 1)
            blocks.append(
                jnp.where(
                    column == upper[cut],
                    upper_coef[cut],
                    jnp.where(column == lower[cut], lower_coef[cut], 0.0),
                ).astype(BF16)
            )
        g = jnp.concatenate(blocks, axis=1)
        z_ref[here] = lax.dot_general(
            g, ylm[...], (((1,), (1,)), ((), ())), preferred_element_type=F32
        ).astype(BF16)
        return carry

    lax.fori_loop(0, TOTAL // 128, couple, 0)
    for where in x_peers:
        send(bound_hbm, bound.at[ang], out_sem.at[2], a_recv.at[1], where).start()

    @pl.when(half == 1)
    def _():
        across.start()

    load_cont.wait()
    shells = weight_ref.shape[0]
    count_c = cont.shape[0] // shells
    for r in range(shells):
        for c in range(count_c // 128):
            part = cont[pl.ds(r * count_c + c * 128, 128)].astype(F32).T
            cont_t[pl.ds(r * 128, 128), pl.ds(c * 128, 128)] = part.astype(BF16)

    pl.semaphore_wait(here, NY - 1)
    signal(both, twin)

    def block_of(i):
        cls, quarter = piece_of(x, half, lax.div(i, NY), lax.rem(i, NY), core)
        return cls * (RAD // ANG) + quarter

    block = block_of(spot)
    rows.wait_recv()
    mine[...] = jnp.dot(ys[...], z_ref[...], preferred_element_type=F32).astype(BF16)
    spots = RAD // NC
    pl.semaphore_wait(both, 1)

    far, step = jnp.where(zl < HALF // 2, HALF - 1, 0), jnp.where(zl < HALF // 2, -1, 1)

    def give_pieces(own_k, steps, both_from):
        for k in steps:
            for d in (2, 1, 3, 0):
                if (k, d) == (own_k, 0):
                    continue
                where = ang * RAD + (far + step * k) * NY * NC + lax.rem(y + d, NY) * NC + core
                send(mine, m_full.at[block], out_sem.at[3], m_recv.at[spot], where).start()
                if both_from and own_k - k >= both_from:
                    where = where + 1 - 2 * core
                    send(mine, m_full.at[block], out_sem.at[6], relay_recv.at[1], where).start()

    @pl.when(edge)
    def _():
        give_pieces(HALF - 1, (1, 0, 2, 3), NEXT)

    @pl.when(jnp.logical_not(edge))
    def _():
        give_pieces(HALF // 2, range(HALF), 0)

    when = jnp.where(edge, 1, 0)
    send(mine, m_full.at[block], out_sem.at[4], relay_recv.at[when], twin).start()
    m_full[block] = mine[...]

    signal(all_here.at[0], opposite)
    across.wait_recv()
    other = bound.at[ang + 1 - 2 * half]
    for where in x_peers:
        send(other, other, out_sem.at[5], a_recv.at[2], where).start()
    pl.semaphore_wait(all_here.at[0], 1)
    for where in x_peers:
        signal(all_here.at[1], where)

    def pass_on(start, end, limit, when):
        def act(i):
            @pl.when(i != spot)
            def _():
                there = m_full.at[block_of(i)]
                send(there, there, out_sem.at[4], m_recv.at[i], twin).wait_recv()

                @pl.when(jnp.abs(lax.div(i, NY) - zl) < limit)
                def _():
                    send(there, there, out_sem.at[4], relay_recv.at[when], twin).start()

        each(start, end, act)

    def passed(when):
        part = m_full.at[pl.ds(0, spots // 2)]
        send(part, part, out_sem.at[4], relay_recv.at[when], twin).wait_recv()

    def product(side):
        left = jnp.concatenate([bound[2 * i + side] for i in range(NX)], axis=1)
        right = [
            m_full[pl.ds((2 * i + side) * (RAD // ANG), RAD // ANG)].reshape(PTS, PTS)
            for i in range(NX)
        ]
        right = jnp.concatenate(right, axis=0)
        return jnp.dot(left, right, preferred_element_type=F32)

    pass_on(NY, spots - NY, spots, 0)
    load_bound.wait()
    load_weight.wait()
    three = bound.at[pl.ds(0, NX - 1)]
    send(three, three, out_sem.at[2], a_recv.at[1], twin).wait_recv()
    passed(0)
    early_d[...] = product(half)
    near = jnp.where(zl < HALF // 2, 0, spots - NY)
    for start in (near, spots - NY - near):
        pass_on(start, start + NY, NEXT, 1)
    send(three, three, out_sem.at[2], a_recv.at[2], twin).wait_recv()
    pl.semaphore_wait(all_here.at[1], NX - 1)
    signal(all_here.at[2], twin)
    passed(1)
    pl.semaphore_wait(all_here.at[2], 1)

    d = early_d[...] + product(1 - half)
    nb = d.shape[0] // shells
    weighted = [d[r * nb : (r + 1) * nb] * weight_ref[r] for r in range(shells)]
    wide = jnp.concatenate(weighted, axis=1).astype(BF16)

    def give(q, row, number):
        pltpu.make_async_remote_copy(
            src_ref=sendbufs[q].at[pl.ds(row, 1)], dst_ref=recvbuf.at[pl.ds(me, 1)],
            send_sem=end_send, recv_sem=end_recv, device_id=number, device_id_type=BY_ID,
        ).start()

    columns = []
    for dx, dy, dc in PLANE:
        there_x = lax.rem(x + dx, NX)
        there_yc = lax.rem(y + dy, NY) * NC + lax.rem(core + dc, NC)
        columns.append((there_x * 16 + there_yc, there_x * x_step + there_yc))
    for q in range(HALF):
        terms = jnp.dot(
            wide, cont_t[:, pl.ds(q * 128, 128)], preferred_element_type=F32
        )
        sendbufs[q][...] = turned(terms)
        for row, number in columns:
            give(q, row, number + q * NY * NC)
    for q in range(HALF):
        for row, number in columns:
            give(q, row + 8, number + (q + HALF) * NY * NC)
    own_yc = y * NC + core
    for there in range(NZ):
        q, row = there % HALF, x * 16 + there // HALF * 8 + own_yc

        @pl.when(z != there)
        def _():
            give(q, row, x * x_step + there * NY * NC + own_yc)

        @pl.when(z == there)
        def _():
            pltpu.make_async_copy(
                sendbufs[q].at[pl.ds(row, 1)], recvbuf.at[pl.ds(me, 1)], end_recv
            ).start()

    rows.wait_send()
    across.wait_send()
    for i in (2, 5):
        send(three, three, out_sem.at[i], a_recv.at[1], twin).wait_send()
    own_m = m_full.at[pl.ds(0, spots - 1)]
    send(own_m, own_m, out_sem.at[3], relay_recv.at[0], twin).wait_send()

    def sent_pieces(i, n):
        part = m_full.at[pl.ds(0, n)]
        send(part, part, out_sem.at[i], relay_recv.at[0], twin).wait_send()

    sent_pieces(4, spots - NY)

    @pl.when(edge)
    def _():
        sent_pieces(6, NY)

    @pl.when(jnp.logical_not(edge))
    def _():
        sent_pieces(4, NY)

    pltpu.make_async_copy(recvbuf, recvbuf, end_recv).wait()
    row = jnp.sum(recvbuf[...], axis=0, keepdims=True)
    wide_row = jnp.broadcast_to(row, (8, 128))
    at = lax.broadcasted_iota(jnp.int32, (8, 128), 0)
    spread = wide_row
    for j in range(1, 8):
        spread = jnp.where(at == j, pltpu.roll(wide_row, 128 - 16 * j, 1), spread)
    out_ref[...] = spread[:, : out_ref.shape[1]]
    sent = recvbuf.at[pl.ds(0, ANG * RAD - 1)]
    pltpu.make_async_copy(sent, sent, end_send).wait()


def shards(psi_bound, psi_cont, ylm, radial_weight, order):
    shells, nb, points = psi_bound.shape
    count = psi_cont.shape[1]
    any_space = pl.BlockSpec(memory_space=pl.ANY)
    dma = pltpu.SemaphoreType.DMA
    return pl.pallas_call(
        kernel,
        out_shape=jax.ShapeDtypeStruct((nb // ANG, count // RAD), F32),
        in_specs=[
            any_space,
            any_space,
            any_space,
            any_space,
            any_space,
        ],
        out_specs=pl.BlockSpec(memory_space=pltpu.VMEM),
        scratch_shapes=[
            pltpu.VMEM((ANG, shells * nb, points), BF16),
            pltpu.VMEM((shells * count, points), BF16),
            pltpu.VMEM((points, TOTAL), BF16),
            pltpu.VMEM((8, TOTAL // 8), jnp.int32),
            pltpu.SMEM((shells,), F32),
            pltpu.VMEM((PIECE, TOTAL), BF16),
            pltpu.VMEM((TOTAL, 128), F32),
            pltpu.VMEM((TOTAL, points), BF16),
            pltpu.VMEM((PIECE, points), BF16),
            pltpu.VMEM((RAD, PIECE, points), BF16),
            pltpu.VMEM((shells * nb, points), F32),
            pltpu.VMEM((shells * points, count), BF16),
            *[pltpu.VMEM((64, 128), F32)] * HALF,
            pltpu.VMEM((ANG * RAD, 128), F32),
            dma((5,)),
            dma((7,)),
            dma((3,)),
            dma,
            dma((RAD // NC,)),
            dma((2,)),
            dma,
            dma,
            *[pltpu.SemaphoreType.REGULAR] * 2,
            pltpu.SemaphoreType.REGULAR((3,)),
        ],
        compiler_params=pltpu.CompilerParams(collective_id=0, has_side_effects=True),
        name="dipole",
    )(
        psi_bound.reshape(shells * nb, points),
        psi_cont.reshape(shells * count, points),
        ylm,
        radial_weight,
        order.reshape(8, TOTAL // 8),
    )


def solution(mesh):
    return jax.shard_map(
        shards,
        mesh=mesh,
        in_specs=(P("rad", None, "ang"), P("rad", None, "ang"), P("ang", None), P("rad"), P()),
        out_specs=P("ang", "rad"),
        check_vma=False,
    )
```

```python
import functools

import jax
import jax.numpy as jnp
from jax import lax
from jax.experimental import pallas as pl
from jax.experimental.pallas import tpu as pltpu
from jax.sharding import PartitionSpec as P

LMAX = 31
F32, BF16 = jnp.float32, jnp.bfloat16
NX, NY, NZ, NC, HALF = 4, 4, 8, 2, 4
ANG, RAD = 8, 32
PTS, TOTAL = 128, 1024
PIECE = PTS * ANG // RAD


def ring(d, n):
    return min(d, n - d)


PLANE = sorted(
    ((dx, dy, dc) for dx in range(NX) for dy in range(NY) for dc in range(NC) if (dx, dy, dc) != (0, 0, 0)),
    key=lambda o: -(ring(o[0], NX) + ring(o[1], NY)),
)
NEXT = 2
BY_ID = pl.DeviceIdType.LOGICAL


def device(place):
    x, y, z, core = place
    return x * (ANG * RAD // NX) + z * (NY * NC) + y * NC + core


def piece_of(x, half, zl, y, core):
    edge = (zl == 0) | (zl == HALF - 1)
    other = jnp.where(edge, 1 - half, half)
    pair = jnp.where(edge, lax.div(zl, HALF - 1), zl - 1)
    return lax.rem(x - y + 2 + NX, NX) * 2 + other, pair * 2 + core


def coupling_rows(order):
    degree = jnp.zeros(order.shape, jnp.int32)
    for edge in range(1, LMAX + 1):
        degree = degree + (order >= edge * edge).astype(jnp.int32)
    m = order - degree * degree - degree
    lf, mf = degree.astype(F32), m.astype(F32)
    upper = jnp.where(degree + 1 <= LMAX, order + 2 * degree + 2, -1)
    upper_num = (lf + 1.0) * (lf + 1.0) - mf * mf
    upper_coef = jnp.sqrt(jnp.maximum(upper_num, 0.0) / ((2.0 * lf + 1.0) * (2.0 * lf + 3.0)))
    lower = jnp.where(degree - 1 >= jnp.abs(m), order - 2 * degree, -1)
    lower_num = lf * lf - mf * mf
    lower_den = jnp.maximum((2.0 * lf - 1.0) * (2.0 * lf + 1.0), 1.0)
    lower_coef = jnp.sqrt(jnp.maximum(lower_num, 0.0) / lower_den)
    return upper.astype(F32), upper_coef, lower.astype(F32), lower_coef


def turned(block):
    rows, lanes = block.shape
    tiles = block.reshape(rows // 8, 8, lanes)
    row = lax.broadcasted_iota(jnp.int32, (1, 8, lanes), 1)
    group = lax.broadcasted_iota(jnp.int32, (1, 8, lanes), 2) // 16
    for s in (1, 2, 4):
        low = jnp.broadcast_to((row & s) == 0, tiles.shape)
        same = jnp.broadcast_to(((row ^ group) & s) == 0, tiles.shape)
        below = pltpu.roll(pltpu.roll(tiles, 8 - s, 1), 16 * s, 2)
        if 2 * s < 8:
            above = pltpu.roll(pltpu.roll(tiles, s, 1), lanes - 16 * s, 2)
            below = jnp.where(low, below, above)
        tiles = jnp.where(same, tiles, below)
    return tiles.reshape(rows, lanes)


def kernel(
    bound_hbm, cont_hbm, ylm_hbm, weight_hbm, order_hbm, out_ref,
    bound, cont, ylm, order_ref, weight_ref, ys, ncol, z_ref, mine, m_full, early_d, cont_t, *rest
):
    sendbufs, (recvbuf, *semaphores) = rest[:HALF], rest[HALF:]
    local_sem, out_sem, a_recv, f_recv, m_recv, relay_recv, end_send, end_recv, *signals = semaphores
    here, both, all_here = signals
    ang, rad = lax.axis_index("ang"), lax.axis_index("rad")
    x, half, core, spot = lax.div(ang, 2), lax.rem(ang, 2), lax.rem(rad, NC), lax.div(rad, NC)
    zl, y = lax.div(spot, NY), lax.rem(spot, NY)
    z = half * HALF + zl
    me = ang * RAD + rad
    x_step = ANG * RAD // NX
    x_peers = [me + (lax.rem(x + d, NX) - x) * x_step for d in (2, 1, 3)]
    opposite = me + RAD - 2 * RAD * half
    twin = me + 1 - 2 * core
    first_spot = me - NC * spot
    edge = (zl == 0) | (zl == HALF - 1)
    z_other = jnp.where(edge, NZ - 1 - z, z)
    to_x, from_x = lax.rem(x + y + 2, NX), lax.rem(x - y + 2 + NX, NX)
    rows_to, rows_from = (device((i, y, z_other, 1 - core)) for i in (to_x, from_x))
    y_peers = [me + (lax.rem(y + d, NY) - y) * NC for d in (2, 1, 3)]
    zl_peers = [me + (lax.rem(zl + d, HALF) - zl) * NY * NC for d in (2, 1, 3)]

    def signal(semaphore, where):
        pl.semaphore_signal(semaphore, inc=1, device_id=where, device_id_type=BY_ID)

    def each(start, end, act):
        def body(i, carry):
            act(i)
            return carry

        lax.fori_loop(start, end, body, 0)

    def send(src, dst, send_sem, recv_sem, where):
        return pltpu.make_async_remote_copy(
            src_ref=src, dst_ref=dst, send_sem=send_sem, recv_sem=recv_sem,
            device_id=where, device_id_type=BY_ID,
        )

    barrier = pltpu.get_barrier_semaphore()
    lines = (rows_from, opposite, rows_to, *zl_peers, *x_peers, *y_peers, twin)
    for where in lines:
        signal(barrier, where)
    loads = [
        pltpu.make_async_copy(ylm_hbm, ylm, local_sem.at[0]),
        pltpu.make_async_copy(order_hbm, order_ref, local_sem.at[3]),
        pltpu.make_async_copy(cont_hbm, cont, local_sem.at[1]),
        pltpu.make_async_copy(bound_hbm, bound.at[ang], local_sem.at[2]),
        pltpu.make_async_copy(weight_hbm, weight_ref, local_sem.at[4]),
    ]
    load_ylm, load_order, load_cont, load_bound, load_weight = loads
    for load in loads:
        load.start()
    pl.semaphore_wait(barrier, len(lines))

    quarter_to = piece_of(to_x, lax.div(z_other, HALF), lax.rem(z_other, HALF), y, 1 - core)[1]
    rows = send(
        ylm.at[pl.ds(pl.multiple_of(quarter_to * PIECE, PIECE), PIECE)],
        ys, out_sem.at[0], f_recv, rows_to,
    )
    load_ylm.wait()
    rows.start()

    across = send(bound_hbm, bound.at[ang], out_sem.at[1], a_recv.at[0], opposite)

    @pl.when(half == 0)
    def _():
        across.start()

    for where in y_peers:
        signal(here, where)

    load_order.wait()
    order = order_ref[...]
    upper, upper_coef, lower, lower_coef = coupling_rows(order)
    orderf = order.astype(F32)
    for s in range(TOTAL // 128):
        ncol[pl.ds(s * 128, 128)] = jnp.broadcast_to(orderf[s : s + 1], (128, 128)).T

    def couple(s, carry):
        here = pl.ds(pl.multiple_of(s * 128, 128), 128)
        column = ncol[here]
        blocks = []
        for t in range(TOTAL // 128):
            cut = slice(t, t + 1)
            blocks.append(
                jnp.where(
                    column == upper[cut],
                    upper_coef[cut],
                    jnp.where(column == lower[cut], lower_coef[cut], 0.0),
                ).astype(BF16)
            )
        g = jnp.concatenate(blocks, axis=1)
        z_ref[here] = lax.dot_general(
            g, ylm[...], (((1,), (1,)), ((), ())), preferred_element_type=F32
        ).astype(BF16)
        return carry

    lax.fori_loop(0, TOTAL // 128, couple, 0)
    for where in x_peers:
        send(bound_hbm, bound.at[ang], out_sem.at[2], a_recv.at[1], where).start()

    @pl.when(half == 1)
    def _():
        across.start()

    load_cont.wait()
    shells = weight_ref.shape[0]
    count_c = cont.shape[0] // shells
    for r in range(shells):
        for c in range(count_c // 128):
            part = cont[pl.ds(r * count_c + c * 128, 128)].astype(F32).T
            cont_t[pl.ds(r * 128, 128), pl.ds(c * 128, 128)] = part.astype(BF16)

    pl.semaphore_wait(here, NY - 1)
    signal(both, twin)

    def block_of(i):
        cls, quarter = piece_of(x, half, lax.div(i, NY), lax.rem(i, NY), core)
        return cls * (RAD // ANG) + quarter

    block = block_of(spot)
    rows.wait_recv()
    mine[...] = jnp.dot(ys[...], z_ref[...], preferred_element_type=F32).astype(BF16)
    spots = RAD // NC
    pl.semaphore_wait(both, 1)

    far, step = jnp.where(zl < HALF // 2, HALF - 1, 0), jnp.where(zl < HALF // 2, -1, 1)

    def give_pieces(own_k, steps, both_from):
        for k in steps:
            for d in (2, 1, 3, 0):
                if (k, d) == (own_k, 0):
                    continue
                where = ang * RAD + (far + step * k) * NY * NC + lax.rem(y + d, NY) * NC + core
                send(mine, m_full.at[block], out_sem.at[3], m_recv.at[spot], where).start()
                if both_from and own_k - k == both_from:
                    where = where + 1 - 2 * core
                    send(mine, m_full.at[block], out_sem.at[6], relay_recv.at[1], where).start()

    @pl.when(edge)
    def _():
        give_pieces(HALF - 1, (1, 0, 2, 3), NEXT)

    @pl.when(jnp.logical_not(edge))
    def _():
        give_pieces(HALF // 2, range(HALF), 0)

    when = jnp.where(edge, 1, 0)
    send(mine, m_full.at[block], out_sem.at[4], relay_recv.at[when], twin).start()
    m_full[block] = mine[...]

    signal(all_here.at[0], opposite)
    across.wait_recv()
    other = bound.at[ang + 1 - 2 * half]
    for where in x_peers:
        send(other, other, out_sem.at[5], a_recv.at[2], where).start()
    pl.semaphore_wait(all_here.at[0], 1)
    for where in x_peers:
        signal(all_here.at[1], where)

    def pass_on(start, end, not_at, when):
        def act(i):
            @pl.when(i != spot)
            def _():
                there = m_full.at[block_of(i)]
                send(there, there, out_sem.at[4], m_recv.at[i], twin).wait_recv()

                @pl.when(jnp.abs(lax.div(i, NY) - zl) != not_at)
                def _():
                    send(there, there, out_sem.at[4], relay_recv.at[when], twin).start()

        each(start, end, act)

    def passed(when):
        part = m_full.at[pl.ds(0, spots // 2)]
        send(part, part, out_sem.at[4], relay_recv.at[when], twin).wait_recv()

    def product(side):
        left = jnp.concatenate([bound[2 * i + side] for i in range(NX)], axis=1)
        right = [
            m_full[pl.ds((2 * i + side) * (RAD // ANG), RAD // ANG)].reshape(PTS, PTS)
            for i in range(NX)
        ]
        right = jnp.concatenate(right, axis=0)
        return jnp.dot(left, right, preferred_element_type=F32)

    pass_on(NY, spots - NY, spots, 0)
    load_bound.wait()
    load_weight.wait()
    three = bound.at[pl.ds(0, NX - 1)]
    send(three, three, out_sem.at[2], a_recv.at[1], twin).wait_recv()
    passed(0)
    early_d[...] = product(half)
    near = jnp.where(zl < HALF // 2, 0, spots - NY)
    for start in (near, spots - NY - near):
        pass_on(start, start + NY, NEXT, 1)
    send(three, three, out_sem.at[2], a_recv.at[2], twin).wait_recv()
    pl.semaphore_wait(all_here.at[1], NX - 1)
    signal(all_here.at[2], twin)
    passed(1)
    pl.semaphore_wait(all_here.at[2], 1)

    d = early_d[...] + product(1 - half)
    nb = d.shape[0] // shells
    weighted = [d[r * nb : (r + 1) * nb] * weight_ref[r] for r in range(shells)]
    wide = jnp.concatenate(weighted, axis=1).astype(BF16)

    def give(q, row, number):
        pltpu.make_async_remote_copy(
            src_ref=sendbufs[q].at[pl.ds(row, 1)], dst_ref=recvbuf.at[pl.ds(me, 1)],
            send_sem=end_send, recv_sem=end_recv, device_id=number, device_id_type=BY_ID,
        ).start()

    columns = []
    for dx, dy, dc in PLANE:
        there_x = lax.rem(x + dx, NX)
        there_yc = lax.rem(y + dy, NY) * NC + lax.rem(core + dc, NC)
        columns.append((there_x * 16 + there_yc, there_x * x_step + there_yc))
    for q in range(HALF):
        terms = jnp.dot(
            wide, cont_t[:, pl.ds(q * 128, 128)], preferred_element_type=F32
        )
        sendbufs[q][...] = turned(terms)
        for row, number in columns:
            give(q, row, number + q * NY * NC)
    for q in range(HALF):
        for row, number in columns:
            give(q, row + 8, number + (q + HALF) * NY * NC)
    own_yc = y * NC + core
    for there in range(NZ):
        q, row = there % HALF, x * 16 + there // HALF * 8 + own_yc

        @pl.when(z != there)
        def _():
            give(q, row, x * x_step + there * NY * NC + own_yc)

        @pl.when(z == there)
        def _():
            pltpu.make_async_copy(
                sendbufs[q].at[pl.ds(row, 1)], recvbuf.at[pl.ds(me, 1)], end_recv
            ).start()

    rows.wait_send()
    across.wait_send()
    for i in (2, 5):
        send(three, three, out_sem.at[i], a_recv.at[1], twin).wait_send()
    own_m = m_full.at[pl.ds(0, spots - 1)]
    send(own_m, own_m, out_sem.at[3], relay_recv.at[0], twin).wait_send()

    def sent_pieces(i, n):
        part = m_full.at[pl.ds(0, n)]
        send(part, part, out_sem.at[i], relay_recv.at[0], twin).wait_send()

    sent_pieces(4, spots - NY)

    @pl.when(edge)
    def _():
        sent_pieces(4, NY)
        sent_pieces(6, NY)

    pltpu.make_async_copy(recvbuf, recvbuf, end_recv).wait()
    row = jnp.sum(recvbuf[...], axis=0, keepdims=True)
    wide_row = jnp.broadcast_to(row, (8, 128))
    at = lax.broadcasted_iota(jnp.int32, (8, 128), 0)
    spread = wide_row
    for j in range(1, 8):
        spread = jnp.where(at == j, pltpu.roll(wide_row, 128 - 16 * j, 1), spread)
    out_ref[...] = spread[:, : out_ref.shape[1]]
    sent = recvbuf.at[pl.ds(0, ANG * RAD - 1)]
    pltpu.make_async_copy(sent, sent, end_send).wait()


def shards(psi_bound, psi_cont, ylm, radial_weight, order):
    shells, nb, points = psi_bound.shape
    count = psi_cont.shape[1]
    any_space = pl.BlockSpec(memory_space=pl.ANY)
    dma = pltpu.SemaphoreType.DMA
    return pl.pallas_call(
        kernel,
        out_shape=jax.ShapeDtypeStruct((nb // ANG, count // RAD), F32),
        in_specs=[
            any_space,
            any_space,
            any_space,
            any_space,
            any_space,
        ],
        out_specs=pl.BlockSpec(memory_space=pltpu.VMEM),
        scratch_shapes=[
            pltpu.VMEM((ANG, shells * nb, points), BF16),
            pltpu.VMEM((shells * count, points), BF16),
            pltpu.VMEM((points, TOTAL), BF16),
            pltpu.VMEM((8, TOTAL // 8), jnp.int32),
            pltpu.SMEM((shells,), F32),
            pltpu.VMEM((PIECE, TOTAL), BF16),
            pltpu.VMEM((TOTAL, 128), F32),
            pltpu.VMEM((TOTAL, points), BF16),
            pltpu.VMEM((PIECE, points), BF16),
            pltpu.VMEM((RAD, PIECE, points), BF16),
            pltpu.VMEM((shells * nb, points), F32),
            pltpu.VMEM((shells * points, count), BF16),
            *[pltpu.VMEM((64, 128), F32)] * HALF,
            pltpu.VMEM((ANG * RAD, 128), F32),
            dma((5,)),
            dma((7,)),
            dma((3,)),
            dma,
            dma((RAD // NC,)),
            dma((2,)),
            dma,
            dma,
            *[pltpu.SemaphoreType.REGULAR] * 2,
            pltpu.SemaphoreType.REGULAR((3,)),
        ],
        compiler_params=pltpu.CompilerParams(collective_id=0, has_side_effects=True),
        name="dipole",
    )(
        psi_bound.reshape(shells * nb, points),
        psi_cont.reshape(shells * count, points),
        ylm,
        radial_weight,
        order.reshape(8, TOTAL // 8),
    )


def solution(mesh):
    return jax.shard_map(
        shards,
        mesh=mesh,
        in_specs=(P("rad", None, "ang"), P("rad", None, "ang"), P("ang", None), P("rad"), P()),
        out_specs=P("ang", "rad"),
        check_vma=False,
    )
```

```python
import functools

import jax
import jax.numpy as jnp
from jax import lax
from jax.experimental import pallas as pl
from jax.experimental.pallas import tpu as pltpu
from jax.sharding import PartitionSpec as P

LMAX = 31
F32, BF16 = jnp.float32, jnp.bfloat16
NX, NY, NZ, NC, HALF = 4, 4, 8, 2, 4
ANG, RAD = 8, 32
PTS, TOTAL = 128, 1024
PIECE = PTS * ANG // RAD


def ring(d, n):
    return min(d, n - d)


PLANE = sorted(
    ((dx, dy, dc) for dx in range(NX) for dy in range(NY) for dc in range(NC) if (dx, dy, dc) != (0, 0, 0)),
    key=lambda o: -(ring(o[0], NX) + ring(o[1], NY)),
)
BY_ID = pl.DeviceIdType.LOGICAL


def device(place):
    x, y, z, core = place
    return x * (ANG * RAD // NX) + z * (NY * NC) + y * NC + core


def piece_of(x, half, zl, y, core):
    edge = (zl == 0) | (zl == HALF - 1)
    other = jnp.where(edge, 1 - half, half)
    pair = jnp.where(edge, lax.div(zl, HALF - 1), zl - 1)
    return lax.rem(x - y + 2 + NX, NX) * 2 + other, pair * 2 + core


def coupling_rows(order):
    degree = jnp.zeros(order.shape, jnp.int32)
    for edge in range(1, LMAX + 1):
        degree = degree + (order >= edge * edge).astype(jnp.int32)
    m = order - degree * degree - degree
    lf, mf = degree.astype(F32), m.astype(F32)
    upper = jnp.where(degree + 1 <= LMAX, order + 2 * degree + 2, -1)
    upper_num = (lf + 1.0) * (lf + 1.0) - mf * mf
    upper_coef = jnp.sqrt(jnp.maximum(upper_num, 0.0) / ((2.0 * lf + 1.0) * (2.0 * lf + 3.0)))
    lower = jnp.where(degree - 1 >= jnp.abs(m), order - 2 * degree, -1)
    lower_num = lf * lf - mf * mf
    lower_den = jnp.maximum((2.0 * lf - 1.0) * (2.0 * lf + 1.0), 1.0)
    lower_coef = jnp.sqrt(jnp.maximum(lower_num, 0.0) / lower_den)
    return upper.astype(F32), upper_coef, lower.astype(F32), lower_coef


def turned(block):
    rows, lanes = block.shape
    tiles = block.reshape(rows // 8, 8, lanes)
    row = lax.broadcasted_iota(jnp.int32, (1, 8, lanes), 1)
    group = lax.broadcasted_iota(jnp.int32, (1, 8, lanes), 2) // 16
    for s in (1, 2, 4):
        low = jnp.broadcast_to((row & s) == 0, tiles.shape)
        same = jnp.broadcast_to(((row ^ group) & s) == 0, tiles.shape)
        below = pltpu.roll(pltpu.roll(tiles, 8 - s, 1), 16 * s, 2)
        if 2 * s < 8:
            above = pltpu.roll(pltpu.roll(tiles, s, 1), lanes - 16 * s, 2)
            below = jnp.where(low, below, above)
        tiles = jnp.where(same, tiles, below)
    return tiles.reshape(rows, lanes)


def kernel(
    bound_hbm, cont_hbm, ylm_hbm, weight_hbm, order_hbm, out_ref,
    bound, cont, ylm, order_ref, weight_ref, ys, ncol, z_ref, mine, m_full, early_d, cont_t, *rest
):
    sendbufs, (recvbuf, *semaphores) = rest[:HALF], rest[HALF:]
    local_sem, out_sem, a_recv, f_recv, m_recv, relay_recv, end_send, end_recv, *signals = semaphores
    here, both, all_here = signals
    ang, rad = lax.axis_index("ang"), lax.axis_index("rad")
    x, half, core, spot = lax.div(ang, 2), lax.rem(ang, 2), lax.rem(rad, NC), lax.div(rad, NC)
    zl, y = lax.div(spot, NY), lax.rem(spot, NY)
    z = half * HALF + zl
    me = ang * RAD + rad
    x_step = ANG * RAD // NX
    x_peers = [me + (lax.rem(x + d, NX) - x) * x_step for d in (2, 1, 3)]
    opposite = me + RAD - 2 * RAD * half
    twin = me + 1 - 2 * core
    first_spot = me - NC * spot
    edge = (zl == 0) | (zl == HALF - 1)
    z_other = jnp.where(edge, NZ - 1 - z, z)
    to_x, from_x = lax.rem(x + y + 2, NX), lax.rem(x - y + 2 + NX, NX)
    rows_to, rows_from = (device((i, y, z_other, 1 - core)) for i in (to_x, from_x))
    y_peers = [me + (lax.rem(y + d, NY) - y) * NC for d in (2, 1, 3)]
    zl_peers = [me + (lax.rem(zl + d, HALF) - zl) * NY * NC for d in (2, 1, 3)]

    def signal(semaphore, where):
        pl.semaphore_signal(semaphore, inc=1, device_id=where, device_id_type=BY_ID)

    def each(start, end, act):
        def body(i, carry):
            act(i)
            return carry

        lax.fori_loop(start, end, body, 0)

    def send(src, dst, send_sem, recv_sem, where):
        return pltpu.make_async_remote_copy(
            src_ref=src, dst_ref=dst, send_sem=send_sem, recv_sem=recv_sem,
            device_id=where, device_id_type=BY_ID,
        )

    barrier = pltpu.get_barrier_semaphore()
    lines = (rows_from, opposite, rows_to, *zl_peers, *x_peers, *y_peers, twin)
    for where in lines:
        signal(barrier, where)
    loads = [
        pltpu.make_async_copy(ylm_hbm, ylm, local_sem.at[0]),
        pltpu.make_async_copy(order_hbm, order_ref, local_sem.at[3]),
        pltpu.make_async_copy(cont_hbm, cont, local_sem.at[1]),
        pltpu.make_async_copy(bound_hbm, bound.at[ang], local_sem.at[2]),
        pltpu.make_async_copy(weight_hbm, weight_ref, local_sem.at[4]),
    ]
    load_ylm, load_order, load_cont, load_bound, load_weight = loads
    for load in loads:
        load.start()
    pl.semaphore_wait(barrier, len(lines))

    quarter_to = piece_of(to_x, lax.div(z_other, HALF), lax.rem(z_other, HALF), y, 1 - core)[1]
    rows = send(
        ylm.at[pl.ds(pl.multiple_of(quarter_to * PIECE, PIECE), PIECE)],
        ys, out_sem.at[0], f_recv, rows_to,
    )
    load_ylm.wait()
    rows.start()

    across = send(bound_hbm, bound.at[ang], out_sem.at[1], a_recv.at[0], opposite)

    @pl.when(half == 0)
    def _():
        across.start()

    for where in y_peers:
        signal(here, where)

    load_order.wait()
    order = order_ref[...]
    upper, upper_coef, lower, lower_coef = coupling_rows(order)
    orderf = order.astype(F32)
    for s in range(TOTAL // 128):
        ncol[pl.ds(s * 128, 128)] = jnp.broadcast_to(orderf[s : s + 1], (128, 128)).T

    def couple(s, carry):
        here = pl.ds(pl.multiple_of(s * 128, 128), 128)
        column = ncol[here]
        blocks = []
        for t in range(TOTAL // 128):
            cut = slice(t, t + 1)
            blocks.append(
                jnp.where(
                    column == upper[cut],
                    upper_coef[cut],
                    jnp.where(column == lower[cut], lower_coef[cut], 0.0),
                ).astype(BF16)
            )
        g = jnp.concatenate(blocks, axis=1)
        z_ref[here] = lax.dot_general(
            g, ylm[...], (((1,), (1,)), ((), ())), preferred_element_type=F32
        ).astype(BF16)
        return carry

    lax.fori_loop(0, TOTAL // 128, couple, 0)
    for where in x_peers:
        send(bound_hbm, bound.at[ang], out_sem.at[2], a_recv.at[1], where).start()

    @pl.when(half == 1)
    def _():
        across.start()

    load_cont.wait()
    shells = weight_ref.shape[0]
    count_c = cont.shape[0] // shells
    for r in range(shells):
        for c in range(count_c // 128):
            part = cont[pl.ds(r * count_c + c * 128, 128)].astype(F32).T
            cont_t[pl.ds(r * 128, 128), pl.ds(c * 128, 128)] = part.astype(BF16)

    pl.semaphore_wait(here, NY - 1)
    signal(both, twin)

    def block_of(i):
        cls, quarter = piece_of(x, half, lax.div(i, NY), lax.rem(i, NY), core)
        return cls * (RAD // ANG) + quarter

    block = block_of(spot)
    rows.wait_recv()
    mine[...] = jnp.dot(ys[...], z_ref[...], preferred_element_type=F32).astype(BF16)
    spots = RAD // NC
    pl.semaphore_wait(both, 1)

    far, step = jnp.where(zl < HALF // 2, HALF - 1, 0), jnp.where(zl < HALF // 2, -1, 1)

    def give_pieces(own_k, steps):
        for k in steps:
            for d in (2, 1, 3, 0):
                if (k, d) != (own_k, 0):
                    where = ang * RAD + (far + step * k) * NY * NC + lax.rem(y + d, NY) * NC + core
                    send(mine, m_full.at[block], out_sem.at[3], m_recv.at[spot], where).start()

    @pl.when(edge)
    def _():
        give_pieces(HALF - 1, (1, 0, 2, 3))

    @pl.when(jnp.logical_not(edge))
    def _():
        give_pieces(HALF // 2, range(HALF))

    when = jnp.where(edge, 1, 0)
    send(mine, m_full.at[block], out_sem.at[4], relay_recv.at[when], twin).start()
    m_full[block] = mine[...]

    signal(all_here.at[0], opposite)
    across.wait_recv()
    other = bound.at[ang + 1 - 2 * half]
    for where in x_peers:
        send(other, other, out_sem.at[5], a_recv.at[2], where).start()
    pl.semaphore_wait(all_here.at[0], 1)
    for where in x_peers:
        signal(all_here.at[1], where)

    def pass_on(start, end, when):
        def act(i):
            @pl.when(i != spot)
            def _():
                there = m_full.at[block_of(i)]
                send(there, there, out_sem.at[4], m_recv.at[i], twin).wait_recv()
                send(there, there, out_sem.at[4], relay_recv.at[when], twin).start()

        each(start, end, act)

    def passed(when):
        part = m_full.at[pl.ds(0, spots // 2)]
        send(part, part, out_sem.at[4], relay_recv.at[when], twin).wait_recv()

    def product(side):
        left = jnp.concatenate([bound[2 * i + side] for i in range(NX)], axis=1)
        right = [
            m_full[pl.ds((2 * i + side) * (RAD // ANG), RAD // ANG)].reshape(PTS, PTS)
            for i in range(NX)
        ]
        right = jnp.concatenate(right, axis=0)
        return jnp.dot(left, right, preferred_element_type=F32)

    pass_on(NY, spots - NY, 0)
    load_bound.wait()
    load_weight.wait()
    three = bound.at[pl.ds(0, NX - 1)]
    send(three, three, out_sem.at[2], a_recv.at[1], twin).wait_recv()
    passed(0)
    early_d[...] = product(half)
    near = jnp.where(zl < HALF // 2, 0, spots - NY)
    for start in (near, spots - NY - near):
        pass_on(start, start + NY, 1)
    send(three, three, out_sem.at[2], a_recv.at[2], twin).wait_recv()
    pl.semaphore_wait(all_here.at[1], NX - 1)
    signal(all_here.at[2], twin)
    passed(1)
    pl.semaphore_wait(all_here.at[2], 1)

    d = early_d[...] + product(1 - half)
    nb = d.shape[0] // shells
    weighted = [d[r * nb : (r + 1) * nb] * weight_ref[r] for r in range(shells)]
    wide = jnp.concatenate(weighted, axis=1).astype(BF16)

    def give(q, row, number):
        pltpu.make_async_remote_copy(
            src_ref=sendbufs[q].at[pl.ds(row, 1)], dst_ref=recvbuf.at[pl.ds(me, 1)],
            send_sem=end_send, recv_sem=end_recv, device_id=number, device_id_type=BY_ID,
        ).start()

    columns = []
    for dx, dy, dc in PLANE:
        there_x = lax.rem(x + dx, NX)
        there_yc = lax.rem(y + dy, NY) * NC + lax.rem(core + dc, NC)
        columns.append((there_x * 16 + there_yc, there_x * x_step + there_yc))
    for q in range(HALF):
        terms = jnp.dot(
            wide, cont_t[:, pl.ds(q * 128, 128)], preferred_element_type=F32
        )
        sendbufs[q][...] = turned(terms)
        for row, number in columns:
            give(q, row, number + q * NY * NC)
    for q in range(HALF):
        for row, number in columns:
            give(q, row + 8, number + (q + HALF) * NY * NC)
    own_yc = y * NC + core
    for there in range(NZ):
        q, row = there % HALF, x * 16 + there // HALF * 8 + own_yc

        @pl.when(z != there)
        def _():
            give(q, row, x * x_step + there * NY * NC + own_yc)

        @pl.when(z == there)
        def _():
            pltpu.make_async_copy(
                sendbufs[q].at[pl.ds(row, 1)], recvbuf.at[pl.ds(me, 1)], end_recv
            ).start()

    rows.wait_send()
    across.wait_send()
    for i in (2, 5):
        send(three, three, out_sem.at[i], a_recv.at[1], twin).wait_send()
    own_m = m_full.at[pl.ds(0, spots - 1)]
    send(own_m, own_m, out_sem.at[3], relay_recv.at[0], twin).wait_send()

    def sent_pieces(i, n):
        part = m_full.at[pl.ds(0, n)]
        send(part, part, out_sem.at[i], relay_recv.at[0], twin).wait_send()

    sent_pieces(4, spots)
    pltpu.make_async_copy(recvbuf, recvbuf, end_recv).wait()
    row = jnp.sum(recvbuf[...], axis=0, keepdims=True)
    wide_row = jnp.broadcast_to(row, (8, 128))
    at = lax.broadcasted_iota(jnp.int32, (8, 128), 0)
    spread = wide_row
    for j in range(1, 8):
        spread = jnp.where(at == j, pltpu.roll(wide_row, 128 - 16 * j, 1), spread)
    out_ref[...] = spread[:, : out_ref.shape[1]]
    sent = recvbuf.at[pl.ds(0, ANG * RAD - 1)]
    pltpu.make_async_copy(sent, sent, end_send).wait()


def shards(psi_bound, psi_cont, ylm, radial_weight, order):
    shells, nb, points = psi_bound.shape
    count = psi_cont.shape[1]
    any_space = pl.BlockSpec(memory_space=pl.ANY)
    dma = pltpu.SemaphoreType.DMA
    return pl.pallas_call(
        kernel,
        out_shape=jax.ShapeDtypeStruct((nb // ANG, count // RAD), F32),
        in_specs=[
            any_space,
            any_space,
            any_space,
            any_space,
            any_space,
        ],
        out_specs=pl.BlockSpec(memory_space=pltpu.VMEM),
        scratch_shapes=[
            pltpu.VMEM((ANG, shells * nb, points), BF16),
            pltpu.VMEM((shells * count, points), BF16),
            pltpu.VMEM((points, TOTAL), BF16),
            pltpu.VMEM((8, TOTAL // 8), jnp.int32),
            pltpu.SMEM((shells,), F32),
            pltpu.VMEM((PIECE, TOTAL), BF16),
            pltpu.VMEM((TOTAL, 128), F32),
            pltpu.VMEM((TOTAL, points), BF16),
            pltpu.VMEM((PIECE, points), BF16),
            pltpu.VMEM((RAD, PIECE, points), BF16),
            pltpu.VMEM((shells * nb, points), F32),
            pltpu.VMEM((shells * points, count), BF16),
            *[pltpu.VMEM((64, 128), F32)] * HALF,
            pltpu.VMEM((ANG * RAD, 128), F32),
            dma((5,)),
            dma((6,)),
            dma((3,)),
            dma,
            dma((RAD // NC,)),
            dma((2,)),
            dma,
            dma,
            *[pltpu.SemaphoreType.REGULAR] * 2,
            pltpu.SemaphoreType.REGULAR((3,)),
        ],
        compiler_params=pltpu.CompilerParams(collective_id=0, has_side_effects=True),
        name="dipole",
    )(
        psi_bound.reshape(shells * nb, points),
        psi_cont.reshape(shells * count, points),
        ylm,
        radial_weight,
        order.reshape(8, TOTAL // 8),
    )


def solution(mesh):
    return jax.shard_map(
        shards,
        mesh=mesh,
        in_specs=(P("rad", None, "ang"), P("rad", None, "ang"), P("ang", None), P("rad"), P()),
        out_specs=P("ang", "rad"),
        check_vma=False,
    )
```

```python
import functools

import jax
import jax.numpy as jnp
from jax import lax
from jax.experimental import pallas as pl
from jax.experimental.pallas import tpu as pltpu
from jax.sharding import PartitionSpec as P

LMAX = 31
F32, BF16 = jnp.float32, jnp.bfloat16
NX, NY, NZ, NC, HALF = 4, 4, 8, 2, 4
ANG, RAD = 8, 32
PTS, TOTAL = 128, 1024
PIECE = PTS * ANG // RAD


def ring(d, n):
    return min(d, n - d)


PLANE = sorted(
    ((dx, dy, dc) for dx in range(NX) for dy in range(NY) for dc in range(NC) if (dx, dy, dc) != (0, 0, 0)),
    key=lambda o: -(ring(o[0], NX) + ring(o[1], NY)),
)
NEXT = 3
BY_ID = pl.DeviceIdType.LOGICAL


def device(place):
    x, y, z, core = place
    return x * (ANG * RAD // NX) + z * (NY * NC) + y * NC + core


def piece_of(x, half, zl, y, core):
    edge = (zl == 0) | (zl == HALF - 1)
    other = jnp.where(edge, 1 - half, half)
    pair = jnp.where(edge, lax.div(zl, HALF - 1), zl - 1)
    return lax.rem(x - y + 2 + NX, NX) * 2 + other, pair * 2 + core


def coupling_rows(order):
    degree = jnp.zeros(order.shape, jnp.int32)
    for edge in range(1, LMAX + 1):
        degree = degree + (order >= edge * edge).astype(jnp.int32)
    m = order - degree * degree - degree
    lf, mf = degree.astype(F32), m.astype(F32)
    upper = jnp.where(degree + 1 <= LMAX, order + 2 * degree + 2, -1)
    upper_num = (lf + 1.0) * (lf + 1.0) - mf * mf
    upper_coef = jnp.sqrt(jnp.maximum(upper_num, 0.0) / ((2.0 * lf + 1.0) * (2.0 * lf + 3.0)))
    lower = jnp.where(degree - 1 >= jnp.abs(m), order - 2 * degree, -1)
    lower_num = lf * lf - mf * mf
    lower_den = jnp.maximum((2.0 * lf - 1.0) * (2.0 * lf + 1.0), 1.0)
    lower_coef = jnp.sqrt(jnp.maximum(lower_num, 0.0) / lower_den)
    return upper.astype(F32), upper_coef, lower.astype(F32), lower_coef


def turned(block):
    rows, lanes = block.shape
    tiles = block.reshape(rows // 8, 8, lanes)
    row = lax.broadcasted_iota(jnp.int32, (1, 8, lanes), 1)
    group = lax.broadcasted_iota(jnp.int32, (1, 8, lanes), 2) // 16
    for s in (1, 2, 4):
        low = jnp.broadcast_to((row & s) == 0, tiles.shape)
        same = jnp.broadcast_to(((row ^ group) & s) == 0, tiles.shape)
        below = pltpu.roll(pltpu.roll(tiles, 8 - s, 1), 16 * s, 2)
        if 2 * s < 8:
            above = pltpu.roll(pltpu.roll(tiles, s, 1), lanes - 16 * s, 2)
            below = jnp.where(low, below, above)
        tiles = jnp.where(same, tiles, below)
    return tiles.reshape(rows, lanes)


def kernel(
    bound_hbm, cont_hbm, ylm_hbm, weight_hbm, order_hbm, out_ref,
    bound, cont, ylm, order_ref, weight_ref, ys, ncol, z_ref, mine, m_full, early_d, cont_t, *rest
):
    sendbufs, (recvbuf, *semaphores) = rest[:HALF], rest[HALF:]
    local_sem, out_sem, a_recv, f_recv, m_recv, relay_recv, end_send, end_recv, *signals = semaphores
    here, both, all_here = signals
    ang, rad = lax.axis_index("ang"), lax.axis_index("rad")
    x, half, core, spot = lax.div(ang, 2), lax.rem(ang, 2), lax.rem(rad, NC), lax.div(rad, NC)
    zl, y = lax.div(spot, NY), lax.rem(spot, NY)
    z = half * HALF + zl
    me = ang * RAD + rad
    x_step = ANG * RAD // NX
    x_peers = [me + (lax.rem(x + d, NX) - x) * x_step for d in (2, 1, 3)]
    opposite = me + RAD - 2 * RAD * half
    twin = me + 1 - 2 * core
    first_spot = me - NC * spot
    edge = (zl == 0) | (zl == HALF - 1)
    z_other = jnp.where(edge, NZ - 1 - z, z)
    to_x, from_x = lax.rem(x + y + 2, NX), lax.rem(x - y + 2 + NX, NX)
    rows_to, rows_from = (device((i, y, z_other, 1 - core)) for i in (to_x, from_x))
    y_peers = [me + (lax.rem(y + d, NY) - y) * NC for d in (2, 1, 3)]
    zl_peers = [me + (lax.rem(zl + d, HALF) - zl) * NY * NC for d in (2, 1, 3)]

    def signal(semaphore, where):
        pl.semaphore_signal(semaphore, inc=1, device_id=where, device_id_type=BY_ID)

    def each(start, end, act):
        def body(i, carry):
            act(i)
            return carry

        lax.fori_loop(start, end, body, 0)

    def send(src, dst, send_sem, recv_sem, where):
        return pltpu.make_async_remote_copy(
            src_ref=src, dst_ref=dst, send_sem=send_sem, recv_sem=recv_sem,
            device_id=where, device_id_type=BY_ID,
        )

    barrier = pltpu.get_barrier_semaphore()
    lines = (rows_from, opposite, rows_to, *zl_peers, *x_peers, *y_peers, twin)
    for where in lines:
        signal(barrier, where)
    loads = [
        pltpu.make_async_copy(ylm_hbm, ylm, local_sem.at[0]),
        pltpu.make_async_copy(order_hbm, order_ref, local_sem.at[3]),
        pltpu.make_async_copy(cont_hbm, cont, local_sem.at[1]),
        pltpu.make_async_copy(bound_hbm, bound.at[ang], local_sem.at[2]),
        pltpu.make_async_copy(weight_hbm, weight_ref, local_sem.at[4]),
    ]
    load_ylm, load_order, load_cont, load_bound, load_weight = loads
    for load in loads:
        load.start()
    pl.semaphore_wait(barrier, len(lines))

    quarter_to = piece_of(to_x, lax.div(z_other, HALF), lax.rem(z_other, HALF), y, 1 - core)[1]
    rows = send(
        ylm.at[pl.ds(pl.multiple_of(quarter_to * PIECE, PIECE), PIECE)],
        ys, out_sem.at[0], f_recv, rows_to,
    )
    load_ylm.wait()
    rows.start()

    across = send(bound_hbm, bound.at[ang], out_sem.at[1], a_recv.at[0], opposite)

    for where in y_peers:
        signal(here, where)

    load_order.wait()
    order = order_ref[...]
    upper, upper_coef, lower, lower_coef = coupling_rows(order)
    orderf = order.astype(F32)
    for s in range(TOTAL // 128):
        ncol[pl.ds(s * 128, 128)] = jnp.broadcast_to(orderf[s : s + 1], (128, 128)).T

    def couple(s, carry):
        here = pl.ds(pl.multiple_of(s * 128, 128), 128)
        column = ncol[here]
        blocks = []
        for t in range(TOTAL // 128):
            cut = slice(t, t + 1)
            blocks.append(
                jnp.where(
                    column == upper[cut],
                    upper_coef[cut],
                    jnp.where(column == lower[cut], lower_coef[cut], 0.0),
                ).astype(BF16)
            )
        g = jnp.concatenate(blocks, axis=1)
        z_ref[here] = lax.dot_general(
            g, ylm[...], (((1,), (1,)), ((), ())), preferred_element_type=F32
        ).astype(BF16)
        return carry

    middle = TOTAL // 256
    lax.fori_loop(0, middle, couple, 0)

    @pl.when(half == 0)
    def _():
        across.start()

    lax.fori_loop(middle, TOTAL // 128, couple, 0)
    for where in x_peers:
        send(bound_hbm, bound.at[ang], out_sem.at[2], a_recv.at[1], where).start()

    @pl.when(half == 1)
    def _():
        across.start()

    load_cont.wait()
    shells = weight_ref.shape[0]
    count_c = cont.shape[0] // shells
    for r in range(shells):
        for c in range(count_c // 128):
            part = cont[pl.ds(r * count_c + c * 128, 128)].astype(F32).T
            cont_t[pl.ds(r * 128, 128), pl.ds(c * 128, 128)] = part.astype(BF16)

    pl.semaphore_wait(here, NY - 1)
    signal(both, twin)

    def block_of(i):
        cls, quarter = piece_of(x, half, lax.div(i, NY), lax.rem(i, NY), core)
        return cls * (RAD // ANG) + quarter

    block = block_of(spot)
    rows.wait_recv()
    mine[...] = jnp.dot(ys[...], z_ref[...], preferred_element_type=F32).astype(BF16)
    spots = RAD // NC
    pl.semaphore_wait(both, 1)

    far, step = jnp.where(zl < HALF // 2, HALF - 1, 0), jnp.where(zl < HALF // 2, -1, 1)

    def give_pieces(own_k, steps, both_from):
        for k in steps:
            for d in (2, 1, 3, 0):
                if (k, d) == (own_k, 0):
                    continue
                where = ang * RAD + (far + step * k) * NY * NC + lax.rem(y + d, NY) * NC + core
                send(mine, m_full.at[block], out_sem.at[3], m_recv.at[spot], where).start()
                if both_from and own_k - k >= both_from:
                    where = where + 1 - 2 * core
                    send(mine, m_full.at[block], out_sem.at[6], relay_recv.at[1], where).start()

    @pl.when(edge)
    def _():
        give_pieces(HALF - 1, (1, 0, 2, 3), NEXT)

    @pl.when(jnp.logical_not(edge))
    def _():
        give_pieces(HALF // 2, range(HALF), 0)

    when = jnp.where(edge, 1, 0)
    send(mine, m_full.at[block], out_sem.at[4], relay_recv.at[when], twin).start()
    m_full[block] = mine[...]

    signal(all_here.at[0], opposite)
    across.wait_recv()
    other = bound.at[ang + 1 - 2 * half]
    for where in x_peers:
        send(other, other, out_sem.at[5], a_recv.at[2], where).start()
    pl.semaphore_wait(all_here.at[0], 1)
    for where in x_peers:
        signal(all_here.at[1], where)

    def pass_on(start, end, limit, when):
        def act(i):
            @pl.when(i != spot)
            def _():
                there = m_full.at[block_of(i)]
                send(there, there, out_sem.at[4], m_recv.at[i], twin).wait_recv()

                @pl.when(jnp.abs(lax.div(i, NY) - zl) < limit)
                def _():
                    send(there, there, out_sem.at[4], relay_recv.at[when], twin).start()

        each(start, end, act)

    def passed(when):
        part = m_full.at[pl.ds(0, spots // 2)]
        send(part, part, out_sem.at[4], relay_recv.at[when], twin).wait_recv()

    def product(side):
        left = jnp.concatenate([bound[2 * i + side] for i in range(NX)], axis=1)
        right = [
            m_full[pl.ds((2 * i + side) * (RAD // ANG), RAD // ANG)].reshape(PTS, PTS)
            for i in range(NX)
        ]
        right = jnp.concatenate(right, axis=0)
        return jnp.dot(left, right, preferred_element_type=F32)

    pass_on(NY, spots - NY, spots, 0)
    load_bound.wait()
    load_weight.wait()
    three = bound.at[pl.ds(0, NX - 1)]
    send(three, three, out_sem.at[2], a_recv.at[1], twin).wait_recv()
    passed(0)
    early_d[...] = product(half)
    pass_on(0, NY, NEXT, 1)
    pass_on(spots - NY, spots, NEXT, 1)
    send(three, three, out_sem.at[2], a_recv.at[2], twin).wait_recv()
    pl.semaphore_wait(all_here.at[1], NX - 1)
    signal(all_here.at[2], twin)
    passed(1)
    pl.semaphore_wait(all_here.at[2], 1)

    d = early_d[...] + product(1 - half)
    nb = d.shape[0] // shells
    weighted = [d[r * nb : (r + 1) * nb] * weight_ref[r] for r in range(shells)]
    wide = jnp.concatenate(weighted, axis=1).astype(BF16)

    def give(q, row, number):
        pltpu.make_async_remote_copy(
            src_ref=sendbufs[q].at[pl.ds(row, 1)], dst_ref=recvbuf.at[pl.ds(me, 1)],
            send_sem=end_send, recv_sem=end_recv, device_id=number, device_id_type=BY_ID,
        ).start()

    columns = []
    for dx, dy, dc in PLANE:
        there_x = lax.rem(x + dx, NX)
        there_yc = lax.rem(y + dy, NY) * NC + lax.rem(core + dc, NC)
        columns.append((there_x * 16 + there_yc, there_x * x_step + there_yc))
    for q in range(HALF):
        terms = jnp.dot(
            wide, cont_t[:, pl.ds(q * 128, 128)], preferred_element_type=F32
        )
        sendbufs[q][...] = turned(terms)
        for row, number in columns:
            give(q, row, number + q * NY * NC)
    for q in range(HALF):
        for row, number in columns:
            give(q, row + 8, number + (q + HALF) * NY * NC)
    own_yc = y * NC + core
    for there in range(NZ):
        q, row = there % HALF, x * 16 + there // HALF * 8 + own_yc

        @pl.when(z != there)
        def _():
            give(q, row, x * x_step + there * NY * NC + own_yc)

        @pl.when(z == there)
        def _():
            pltpu.make_async_copy(
                sendbufs[q].at[pl.ds(row, 1)], recvbuf.at[pl.ds(me, 1)], end_recv
            ).start()

    rows.wait_send()
    across.wait_send()
    for i in (2, 5):
        send(three, three, out_sem.at[i], a_recv.at[1], twin).wait_send()
    own_m = m_full.at[pl.ds(0, spots - 1)]
    send(own_m, own_m, out_sem.at[3], relay_recv.at[0], twin).wait_send()

    def sent_pieces(i, n):
        part = m_full.at[pl.ds(0, n)]
        send(part, part, out_sem.at[i], relay_recv.at[0], twin).wait_send()

    sent_pieces(4, spots - NY)

    @pl.when(edge)
    def _():
        sent_pieces(6, NY)

    @pl.when(jnp.logical_not(edge))
    def _():
        sent_pieces(4, NY)

    pltpu.make_async_copy(recvbuf, recvbuf, end_recv).wait()
    row = jnp.sum(recvbuf[...], axis=0, keepdims=True)
    wide_row = jnp.broadcast_to(row, (8, 128))
    at = lax.broadcasted_iota(jnp.int32, (8, 128), 0)
    spread = wide_row
    for j in range(1, 8):
        spread = jnp.where(at == j, pltpu.roll(wide_row, 128 - 16 * j, 1), spread)
    out_ref[...] = spread[:, : out_ref.shape[1]]
    sent = recvbuf.at[pl.ds(0, ANG * RAD - 1)]
    pltpu.make_async_copy(sent, sent, end_send).wait()


def shards(psi_bound, psi_cont, ylm, radial_weight, order):
    shells, nb, points = psi_bound.shape
    count = psi_cont.shape[1]
    any_space = pl.BlockSpec(memory_space=pl.ANY)
    dma = pltpu.SemaphoreType.DMA
    return pl.pallas_call(
        kernel,
        out_shape=jax.ShapeDtypeStruct((nb // ANG, count // RAD), F32),
        in_specs=[
            any_space,
            any_space,
            any_space,
            any_space,
            any_space,
        ],
        out_specs=pl.BlockSpec(memory_space=pltpu.VMEM),
        scratch_shapes=[
            pltpu.VMEM((ANG, shells * nb, points), BF16),
            pltpu.VMEM((shells * count, points), BF16),
            pltpu.VMEM((points, TOTAL), BF16),
            pltpu.VMEM((8, TOTAL // 8), jnp.int32),
            pltpu.SMEM((shells,), F32),
            pltpu.VMEM((PIECE, TOTAL), BF16),
            pltpu.VMEM((TOTAL, 128), F32),
            pltpu.VMEM((TOTAL, points), BF16),
            pltpu.VMEM((PIECE, points), BF16),
            pltpu.VMEM((RAD, PIECE, points), BF16),
            pltpu.VMEM((shells * nb, points), F32),
            pltpu.VMEM((shells * points, count), BF16),
            *[pltpu.VMEM((64, 128), F32)] * HALF,
            pltpu.VMEM((ANG * RAD, 128), F32),
            dma((5,)),
            dma((7,)),
            dma((3,)),
            dma,
            dma((RAD // NC,)),
            dma((2,)),
            dma,
            dma,
            *[pltpu.SemaphoreType.REGULAR] * 2,
            pltpu.SemaphoreType.REGULAR((3,)),
        ],
        compiler_params=pltpu.CompilerParams(collective_id=0, has_side_effects=True),
        name="dipole",
    )(
        psi_bound.reshape(shells * nb, points),
        psi_cont.reshape(shells * count, points),
        ylm,
        radial_weight,
        order.reshape(8, TOTAL // 8),
    )


def solution(mesh):
    return jax.shard_map(
        shards,
        mesh=mesh,
        in_specs=(P("rad", None, "ang"), P("rad", None, "ang"), P("ang", None), P("rad"), P()),
        out_specs=P("ang", "rad"),
        check_vma=False,
    )
```

```python
import functools

import jax
import jax.numpy as jnp
from jax import lax
from jax.experimental import pallas as pl
from jax.experimental.pallas import tpu as pltpu
from jax.sharding import PartitionSpec as P

LMAX = 31
F32, BF16 = jnp.float32, jnp.bfloat16
NX, NY, NZ, NC, HALF = 4, 4, 8, 2, 4
ANG, RAD = 8, 32
PTS, TOTAL = 128, 1024
PIECE = PTS * ANG // RAD


def ring(d, n):
    return min(d, n - d)


PLANE = sorted(
    ((dx, dy, dc) for dx in range(NX) for dy in range(NY) for dc in range(NC) if (dx, dy, dc) != (0, 0, 0)),
    key=lambda o: -(ring(o[0], NX) + ring(o[1], NY)),
)
NEXT = 3
BY_ID = pl.DeviceIdType.LOGICAL


def device(place):
    x, y, z, core = place
    return x * (ANG * RAD // NX) + z * (NY * NC) + y * NC + core


def piece_of(x, half, zl, y, core):
    edge = (zl == 0) | (zl == HALF - 1)
    other = jnp.where(edge, 1 - half, half)
    pair = jnp.where(edge, lax.div(zl, HALF - 1), zl - 1)
    return lax.rem(x - y + 2 + NX, NX) * 2 + other, pair * 2 + core


def coupling_rows(order):
    degree = jnp.zeros(order.shape, jnp.int32)
    for edge in range(1, LMAX + 1):
        degree = degree + (order >= edge * edge).astype(jnp.int32)
    m = order - degree * degree - degree
    lf, mf = degree.astype(F32), m.astype(F32)
    upper = jnp.where(degree + 1 <= LMAX, order + 2 * degree + 2, -1)
    upper_num = (lf + 1.0) * (lf + 1.0) - mf * mf
    upper_coef = jnp.sqrt(jnp.maximum(upper_num, 0.0) / ((2.0 * lf + 1.0) * (2.0 * lf + 3.0)))
    lower = jnp.where(degree - 1 >= jnp.abs(m), order - 2 * degree, -1)
    lower_num = lf * lf - mf * mf
    lower_den = jnp.maximum((2.0 * lf - 1.0) * (2.0 * lf + 1.0), 1.0)
    lower_coef = jnp.sqrt(jnp.maximum(lower_num, 0.0) / lower_den)
    return upper.astype(F32), upper_coef, lower.astype(F32), lower_coef


def turned(block):
    rows, lanes = block.shape
    tiles = block.reshape(rows // 8, 8, lanes)
    row = lax.broadcasted_iota(jnp.int32, (1, 8, lanes), 1)
    group = lax.broadcasted_iota(jnp.int32, (1, 8, lanes), 2) // 16
    for s in (1, 2, 4):
        low = jnp.broadcast_to((row & s) == 0, tiles.shape)
        same = jnp.broadcast_to(((row ^ group) & s) == 0, tiles.shape)
        below = pltpu.roll(pltpu.roll(tiles, 8 - s, 1), 16 * s, 2)
        if 2 * s < 8:
            above = pltpu.roll(pltpu.roll(tiles, s, 1), lanes - 16 * s, 2)
            below = jnp.where(low, below, above)
        tiles = jnp.where(same, tiles, below)
    return tiles.reshape(rows, lanes)


def kernel(
    bound_hbm, cont_hbm, ylm_hbm, weight_hbm, order_hbm, out_ref,
    bound, cont, ylm, order_ref, weight_ref, ys, ncol, z_ref, mine, m_full, early_d, cont_t, *rest
):
    sendbufs, (recvbuf, *semaphores) = rest[:HALF], rest[HALF:]
    local_sem, out_sem, a_recv, f_recv, m_recv, relay_recv, end_send, end_recv, *signals = semaphores
    here, both, all_here = signals
    ang, rad = lax.axis_index("ang"), lax.axis_index("rad")
    x, half, core, spot = lax.div(ang, 2), lax.rem(ang, 2), lax.rem(rad, NC), lax.div(rad, NC)
    zl, y = lax.div(spot, NY), lax.rem(spot, NY)
    z = half * HALF + zl
    me = ang * RAD + rad
    x_step = ANG * RAD // NX
    x_peers = [me + (lax.rem(x + d, NX) - x) * x_step for d in (2, 1, 3)]
    opposite = me + RAD - 2 * RAD * half
    twin = me + 1 - 2 * core
    first_spot = me - NC * spot
    edge = (zl == 0) | (zl == HALF - 1)
    z_other = jnp.where(edge, NZ - 1 - z, z)
    to_x, from_x = lax.rem(x + y + 2, NX), lax.rem(x - y + 2 + NX, NX)
    rows_to, rows_from = (device((i, y, z_other, 1 - core)) for i in (to_x, from_x))
    y_peers = [me + (lax.rem(y + d, NY) - y) * NC for d in (2, 1, 3)]
    zl_peers = [me + (lax.rem(zl + d, HALF) - zl) * NY * NC for d in (2, 1, 3)]

    def signal(semaphore, where):
        pl.semaphore_signal(semaphore, inc=1, device_id=where, device_id_type=BY_ID)

    def each(start, end, act):
        def body(i, carry):
            act(i)
            return carry

        lax.fori_loop(start, end, body, 0)

    def send(src, dst, send_sem, recv_sem, where):
        return pltpu.make_async_remote_copy(
            src_ref=src, dst_ref=dst, send_sem=send_sem, recv_sem=recv_sem,
            device_id=where, device_id_type=BY_ID,
        )

    barrier = pltpu.get_barrier_semaphore()
    lines = (rows_from, opposite, rows_to, *zl_peers, *x_peers, *y_peers, twin)
    for where in lines:
        signal(barrier, where)
    loads = [
        pltpu.make_async_copy(ylm_hbm, ylm, local_sem.at[0]),
        pltpu.make_async_copy(order_hbm, order_ref, local_sem.at[3]),
        pltpu.make_async_copy(cont_hbm, cont, local_sem.at[1]),
        pltpu.make_async_copy(bound_hbm, bound.at[ang], local_sem.at[2]),
        pltpu.make_async_copy(weight_hbm, weight_ref, local_sem.at[4]),
    ]
    load_ylm, load_order, load_cont, load_bound, load_weight = loads
    for load in loads:
        load.start()
    pl.semaphore_wait(barrier, len(lines))

    quarter_to = piece_of(to_x, lax.div(z_other, HALF), lax.rem(z_other, HALF), y, 1 - core)[1]
    rows = send(
        ylm.at[pl.ds(pl.multiple_of(quarter_to * PIECE, PIECE), PIECE)],
        ys, out_sem.at[0], f_recv, rows_to,
    )
    load_ylm.wait()
    rows.start()

    across = send(bound_hbm, bound.at[ang], out_sem.at[1], a_recv.at[0], opposite)

    for where in y_peers:
        signal(here, where)

    load_order.wait()
    order = order_ref[...]
    upper, upper_coef, lower, lower_coef = coupling_rows(order)
    orderf = order.astype(F32)
    for s in range(TOTAL // 128):
        ncol[pl.ds(s * 128, 128)] = jnp.broadcast_to(orderf[s : s + 1], (128, 128)).T

    def couple(s, carry):
        here = pl.ds(pl.multiple_of(s * 128, 128), 128)
        column = ncol[here]
        blocks = []
        for t in range(TOTAL // 128):
            cut = slice(t, t + 1)
            blocks.append(
                jnp.where(
                    column == upper[cut],
                    upper_coef[cut],
                    jnp.where(column == lower[cut], lower_coef[cut], 0.0),
                ).astype(BF16)
            )
        g = jnp.concatenate(blocks, axis=1)
        z_ref[here] = lax.dot_general(
            g, ylm[...], (((1,), (1,)), ((), ())), preferred_element_type=F32
        ).astype(BF16)
        return carry

    middle = TOTAL // 256
    lax.fori_loop(0, middle, couple, 0)

    @pl.when(half == 0)
    def _():
        across.start()

    lax.fori_loop(middle, TOTAL // 128, couple, 0)
    for where in x_peers:
        send(bound_hbm, bound.at[ang], out_sem.at[2], a_recv.at[1], where).start()

    @pl.when(half == 1)
    def _():
        across.start()

    load_cont.wait()
    shells = weight_ref.shape[0]
    count_c = cont.shape[0] // shells
    for r in range(shells):
        for c in range(count_c // 128):
            part = cont[pl.ds(r * count_c + c * 128, 128)].astype(F32).T
            cont_t[pl.ds(r * 128, 128), pl.ds(c * 128, 128)] = part.astype(BF16)

    pl.semaphore_wait(here, NY - 1)
    signal(both, twin)

    def block_of(i):
        cls, quarter = piece_of(x, half, lax.div(i, NY), lax.rem(i, NY), core)
        return cls * (RAD // ANG) + quarter

    block = block_of(spot)
    rows.wait_recv()
    mine[...] = jnp.dot(ys[...], z_ref[...], preferred_element_type=F32).astype(BF16)
    spots = RAD // NC
    pl.semaphore_wait(both, 1)

    far, step = jnp.where(zl < HALF // 2, HALF - 1, 0), jnp.where(zl < HALF // 2, -1, 1)

    def give_pieces(own_k, steps, both_from):
        for k in steps:
            for d in (2, 1, 3, 0):
                if (k, d) == (own_k, 0):
                    continue
                where = ang * RAD + (far + step * k) * NY * NC + lax.rem(y + d, NY) * NC + core
                send(mine, m_full.at[block], out_sem.at[3], m_recv.at[spot], where).start()
                if both_from and own_k - k >= both_from:
                    where = where + 1 - 2 * core
                    send(mine, m_full.at[block], out_sem.at[6], relay_recv.at[1], where).start()

    @pl.when(edge)
    def _():
        give_pieces(HALF - 1, (1, 0, 2, 3), NEXT)

    @pl.when(jnp.logical_not(edge))
    def _():
        give_pieces(HALF // 2, range(HALF), 0)

    when = jnp.where(edge, 1, 0)
    send(mine, m_full.at[block], out_sem.at[4], relay_recv.at[when], twin).start()
    m_full[block] = mine[...]

    signal(all_here.at[0], opposite)
    across.wait_recv()
    other = bound.at[ang + 1 - 2 * half]
    for where in x_peers:
        send(other, other, out_sem.at[5], a_recv.at[2], where).start()
    pl.semaphore_wait(all_here.at[0], 1)
    for where in x_peers:
        signal(all_here.at[1], where)

    def pass_on(start, end, limit, when):
        def act(i):
            @pl.when(i != spot)
            def _():
                there = m_full.at[block_of(i)]
                send(there, there, out_sem.at[4], m_recv.at[i], twin).wait_recv()

                @pl.when(jnp.abs(lax.div(i, NY) - zl) < limit)
                def _():
                    send(there, there, out_sem.at[4], relay_recv.at[when], twin).start()

        each(start, end, act)

    def passed(when):
        part = m_full.at[pl.ds(0, spots // 2)]
        send(part, part, out_sem.at[4], relay_recv.at[when], twin).wait_recv()

    def product(side):
        left = jnp.concatenate([bound[2 * i + side] for i in range(NX)], axis=1)
        right = [
            m_full[pl.ds((2 * i + side) * (RAD // ANG), RAD // ANG)].reshape(PTS, PTS)
            for i in range(NX)
        ]
        right = jnp.concatenate(right, axis=0)
        return jnp.dot(left, right, preferred_element_type=F32)

    pass_on(NY, spots - NY, spots, 0)
    load_bound.wait()
    load_weight.wait()
    three = bound.at[pl.ds(0, NX - 1)]
    send(three, three, out_sem.at[2], a_recv.at[1], twin).wait_recv()
    passed(0)
    early_d[...] = product(half)
    near = jnp.where(zl < HALF // 2, 0, spots - NY)
    for start in (near, spots - NY - near):
        pass_on(start, start + NY, NEXT, 1)
    send(three, three, out_sem.at[2], a_recv.at[2], twin).wait_recv()
    pl.semaphore_wait(all_here.at[1], NX - 1)
    signal(all_here.at[2], twin)
    passed(1)
    pl.semaphore_wait(all_here.at[2], 1)

    d = early_d[...] + product(1 - half)
    nb = d.shape[0] // shells
    weighted = [d[r * nb : (r + 1) * nb] * weight_ref[r] for r in range(shells)]
    wide = jnp.concatenate(weighted, axis=1).astype(BF16)

    def give(q, row, number):
        pltpu.make_async_remote_copy(
            src_ref=sendbufs[q].at[pl.ds(row, 1)], dst_ref=recvbuf.at[pl.ds(me, 1)],
            send_sem=end_send, recv_sem=end_recv, device_id=number, device_id_type=BY_ID,
        ).start()

    columns = []
    for dx, dy, dc in PLANE:
        there_x = lax.rem(x + dx, NX)
        there_yc = lax.rem(y + dy, NY) * NC + lax.rem(core + dc, NC)
        columns.append((there_x * 16 + there_yc, there_x * x_step + there_yc))
    for q in range(HALF):
        terms = jnp.dot(
            wide, cont_t[:, pl.ds(q * 128, 128)], preferred_element_type=F32
        )
        sendbufs[q][...] = turned(terms)
        for row, number in columns:
            give(q, row, number + q * NY * NC)
    for q in range(HALF):
        for row, number in columns:
            give(q, row + 8, number + (q + HALF) * NY * NC)
    own_yc = y * NC + core
    for there in range(NZ):
        q, row = there % HALF, x * 16 + there // HALF * 8 + own_yc

        @pl.when(z != there)
        def _():
            give(q, row, x * x_step + there * NY * NC + own_yc)

        @pl.when(z == there)
        def _():
            pltpu.make_async_copy(
                sendbufs[q].at[pl.ds(row, 1)], recvbuf.at[pl.ds(me, 1)], end_recv
            ).start()

    rows.wait_send()
    across.wait_send()
    for i in (2, 5):
        send(three, three, out_sem.at[i], a_recv.at[1], twin).wait_send()
    own_m = m_full.at[pl.ds(0, spots - 1)]
    send(own_m, own_m, out_sem.at[3], relay_recv.at[0], twin).wait_send()

    def sent_pieces(i, n):
        part = m_full.at[pl.ds(0, n)]
        send(part, part, out_sem.at[i], relay_recv.at[0], twin).wait_send()

    sent_pieces(4, spots - NY)

    @pl.when(edge)
    def _():
        sent_pieces(6, NY)

    @pl.when(jnp.logical_not(edge))
    def _():
        sent_pieces(4, NY)

    pltpu.make_async_copy(recvbuf, recvbuf, end_recv).wait()
    row = jnp.sum(recvbuf[...], axis=0, keepdims=True)
    wide_row = jnp.broadcast_to(row, (8, 128))
    at = lax.broadcasted_iota(jnp.int32, (8, 128), 0)
    spread = wide_row
    for j in range(1, 8):
        spread = jnp.where(at == j, pltpu.roll(wide_row, 128 - 16 * j, 1), spread)
    out_ref[...] = spread[:, : out_ref.shape[1]]
    sent = recvbuf.at[pl.ds(0, ANG * RAD - 1)]
    pltpu.make_async_copy(sent, sent, end_send).wait()


def shards(psi_bound, psi_cont, ylm, radial_weight, order):
    shells, nb, points = psi_bound.shape
    count = psi_cont.shape[1]
    any_space = pl.BlockSpec(memory_space=pl.ANY)
    dma = pltpu.SemaphoreType.DMA
    return pl.pallas_call(
        kernel,
        out_shape=jax.ShapeDtypeStruct((nb // ANG, count // RAD), F32),
        in_specs=[
            any_space,
            any_space,
            any_space,
            any_space,
            any_space,
        ],
        out_specs=pl.BlockSpec(memory_space=pltpu.VMEM),
        scratch_shapes=[
            pltpu.VMEM((ANG, shells * nb, points), BF16),
            pltpu.VMEM((shells * count, points), BF16),
            pltpu.VMEM((points, TOTAL), BF16),
            pltpu.VMEM((8, TOTAL // 8), jnp.int32),
            pltpu.SMEM((shells,), F32),
            pltpu.VMEM((PIECE, TOTAL), BF16),
            pltpu.VMEM((TOTAL, 128), F32),
            pltpu.VMEM((TOTAL, points), BF16),
            pltpu.VMEM((PIECE, points), BF16),
            pltpu.VMEM((RAD, PIECE, points), BF16),
            pltpu.VMEM((shells * nb, points), F32),
            pltpu.VMEM((shells * points, count), BF16),
            *[pltpu.VMEM((64, 128), F32)] * HALF,
            pltpu.VMEM((ANG * RAD, 128), F32),
            dma((5,)),
            dma((7,)),
            dma((3,)),
            dma,
            dma((RAD // NC,)),
            dma((2,)),
            dma,
            dma,
            *[pltpu.SemaphoreType.REGULAR] * 2,
            pltpu.SemaphoreType.REGULAR((3,)),
        ],
        compiler_params=pltpu.CompilerParams(collective_id=0, has_side_effects=True),
        name="dipole",
    )(
        psi_bound.reshape(shells * nb, points),
        psi_cont.reshape(shells * count, points),
        ylm,
        radial_weight,
        order.reshape(8, TOTAL // 8),
    )


def solution(mesh):
    return jax.shard_map(
        shards,
        mesh=mesh,
        in_specs=(P("rad", None, "ang"), P("rad", None, "ang"), P("ang", None), P("rad"), P()),
        out_specs=P("ang", "rad"),
        check_vma=False,
    )
```
